256 devices in a mesh: ctx: 64 (over x_hi, z, y), head: 4 (over x_lo, core).
Axes of the slice: x: 4 (x_hi: 2, x_lo: 2; x = x_hi * 2 + x_lo), y: 4, z: 8, core: 2. Of those that a mesh axis runs over, the one named last changes fastest.
Arguments:
- queries: bfloat16 [8192, 4096], P('ctx', 'head'), may hold values from -81 to 81
- key_states: bfloat16 [8192, 1024], P('ctx', 'head'), may hold values from -7 to 7
- value_states: bfloat16 [8192, 1024], P('ctx', 'head'), may hold values from -6 to 6
- out_weight: bfloat16 [4096, 4096], P('head'), may hold values from -0.09375 to 0.09375
- head_role: int32 [8], replicated, may hold values from 0 to 1, as said below
- sink_len: int32 [8], replicated, may hold values from 32 to 128, as said below
- window_len: int32 [8], replicated, may hold values from 256 to 1024, as said below
Outputs:
- mixed: bfloat16 [8192, 4096], P(('ctx', 'head'))
The draws below stay inside these ranges and needn't reach their ends.
Inputs may be any that keep to these rules, and one draw needn't show every extreme that they name: `head_role`: exactly 4 heads are retrieval heads. `sink_len`: some head has exactly 128. `window_len`: some head has exactly 1024.
All inputs are finite; a program needn't handle non-finite values.
Results may differ from the reference program's by a relative error of at most 0.012.
Values may be sent and summed in bfloat16 or wider, within the bound.
A program may use at most 128 MiB of HBM per device.

```python
import math
import jax
import jax.numpy as jnp
from jax import lax

D = 4096
HQ = 32
KV = 8
HD = 128
SINK = 128
WIN = 1024
TOKENS = 8192
GROUP = 4


def draw_queries(key, part):
    normal_part = jnp.clip(jax.random.normal(jax.random.fold_in(key, 33), (TOKENS, KV, GROUP, HD)), -6.0, 6.0)
    return normal_part.reshape(TOKENS, HQ * HD).astype(jnp.bfloat16)


def draw_key_states(key, part):
    normal_part = jnp.clip(jax.random.normal(jax.random.fold_in(key, 23), (TOKENS, KV, HD)), -6.0, 6.0)
    return normal_part.reshape(TOKENS, KV * HD).astype(jnp.bfloat16)


def draw_head_role(key, part):
    order = jax.random.permutation(jax.random.fold_in(key, 3), KV)
    return (order < KV // 2).astype(jnp.int32)


def draw_sink_len(key, part):
    counts = jax.random.randint(jax.random.fold_in(key, 1), (KV,), max(1, SINK // 4), SINK + 1)
    chosen_head = jax.random.randint(jax.random.fold_in(key, 2), (), 0, KV)
    return jnp.where(jnp.arange(KV) == chosen_head, SINK, counts).astype(jnp.int32)


def draw_window_len(key, part):
    counts = jax.random.randint(jax.random.fold_in(key, 4), (KV,), max(2, WIN // 4), WIN + 1)
    chosen_head = jax.random.randint(jax.random.fold_in(key, 5), (), 0, KV)
    return jnp.where(jnp.arange(KV) == chosen_head, WIN, counts).astype(jnp.int32)


def levels(own_key, shape, pieces, smallest, top_value):
    gain, own = 1.0, jax.random.fold_in(own_key, 6)
    for position, blocks in pieces:
        draws = jnp.exp(jax.random.uniform(jax.random.fold_in(own, position), (blocks,), jnp.float32, smallest / len(pieces), top_value / len(pieces)))
        gain = gain * jnp.repeat(draws, shape[position] // blocks).reshape([-1 if axis == position else 1 for axis in range(len(shape))])
    return gain


def normal_values(stream_key, extent, width, limit, pieces=(), kind=jnp.bfloat16):
    factor_of = levels(stream_key, extent, pieces, -0.22, 0.18) if pieces else 1.0
    result = jax.random.normal(stream_key, extent, jnp.float32) * width * factor_of
    return jnp.minimum(jnp.maximum(result, -limit), limit).astype(kind)


def setup_inputs(seed: int = 0) -> dict:
    streams_of = jax.random.split(jax.random.key(seed), 8)
    return {
        "queries": draw_queries(jax.random.fold_in(streams_of[7], 71), 0),
        "key_states": draw_key_states(jax.random.fold_in(streams_of[7], 71), 0),
        "value_states": normal_values(streams_of[2], (TOKENS, KV * HD), 1.0, 6.0, ((0, 64), (1, 4))),
        "out_weight": normal_values(streams_of[3], (HQ * HD, D), (HQ * HD) ** -0.5, 0.09375, ((0, 4),)),
        "head_role": draw_head_role(jax.random.fold_in(streams_of[7], 71), 0),
        "sink_len": draw_sink_len(jax.random.fold_in(streams_of[7], 71), 0),
        "window_len": draw_window_len(jax.random.fold_in(streams_of[7], 71), 0),
    }


NEGATIVE = -1.0e30


def reference(queries, key_states, value_states, out_weight, head_role, sink_len, window_len):
    tokens = queries.shape[0]
    block_rows = math.gcd(tokens, 512)
    query_blocks = queries.reshape(tokens // block_rows, block_rows, KV, GROUP, HD)
    key_heads = key_states.reshape(tokens, KV, HD).transpose(1, 0, 2)
    value_heads = value_states.reshape(tokens, KV, HD).transpose(1, 0, 2)
    key_pos = jnp.arange(tokens, dtype=jnp.int32)
    scale = HD ** -0.5

    def one_block(block_args):
        query_block, offset = block_args
        query_pos = offset + jnp.arange(block_rows, dtype=jnp.int32)

        def one_head(head_args):
            query_head, key_head, value_head, is_retrieval, sink_count, window_count = head_args
            scores = jnp.einsum("tgd,jd->tgj", query_head.astype(jnp.float32), key_head.astype(jnp.float32)) * scale
            later = query_pos[:, None]
            earlier = key_pos[None, :]
            allowed = (earlier <= later) & ((is_retrieval == 1) | (earlier < sink_count) | (later - earlier < window_count))
            visible = allowed[:, None, :]
            row_peak = jnp.max(jnp.where(visible, scores, NEGATIVE), axis=-1, keepdims=True)
            weights = jnp.where(visible, jnp.exp(scores - row_peak), 0.0)
            row_total = jnp.sum(weights, axis=-1)
            rounded = lax.optimization_barrier(weights.astype(jnp.bfloat16)).astype(jnp.float32)
            weighted = jnp.einsum("tgj,jd->tgd", rounded, value_head.astype(jnp.float32))
            return weighted / row_total[..., None]

        per_head = lax.map(one_head, (query_block.transpose(1, 0, 2, 3), key_heads, value_heads, head_role, sink_len, window_len))
        return per_head.transpose(1, 0, 2, 3)

    offsets = jnp.arange(tokens // block_rows, dtype=jnp.int32) * block_rows
    attended = lax.map(one_block, (query_blocks, offsets))
    attended = attended.reshape(tokens, HQ * HD).astype(jnp.bfloat16)
    return jnp.dot(attended, out_weight, preferred_element_type=jnp.float32).astype(jnp.bfloat16)
```

```python
import jax
import jax.numpy as jnp
from jax import lax
from jax.sharding import PartitionSpec as P

HD = 128
GROUP = 4


NEGATIVE = -1e30


def online_update(running, query_heads, key_part, value_part, allowed):
    row_peak, row_total, weighted = running
    scores = jnp.einsum(
        "thgd,jhd->thgj", query_heads, key_part, preferred_element_type=jnp.float32
    ) * HD ** (-0.5)
    visible = allowed[:, :, None, :]
    block_peak = jnp.max(jnp.where(visible, scores, NEGATIVE), axis=-1)
    new_peak = jnp.maximum(row_peak, block_peak)
    weights = jnp.where(visible, jnp.exp(scores - new_peak[..., None]), 0.0)
    row_total = jnp.sum(weights, axis=-1)
    weighted = jnp.einsum(
        "thgj,jhd->thgd",
        weights.astype(jnp.bfloat16),
        value_part,
        preferred_element_type=jnp.float32,
    )
    return (new_peak, row_total, weighted)


def empty_state(row_count, head_count):
    return (
        jnp.full((row_count, head_count, GROUP), NEGATIVE, jnp.float32),
        jnp.zeros((row_count, head_count, GROUP), jnp.float32),
        jnp.zeros((row_count, head_count, GROUP, HD), jnp.float32),
    )


def finish(running, row_count):
    row_peak, row_total, weighted = running
    return (weighted / row_total[..., None]).astype(jnp.bfloat16).reshape(row_count, -1)


def per_device(queries, key_states, value_states, out_weight, head_role, sink_len, window_len):
    row_count = queries.shape[0]
    local_heads = key_states.shape[1] // HD
    row_base = lax.axis_index("ctx") * row_count
    query_pos = row_base + jnp.arange(row_count, dtype=jnp.int32)
    my_group = lax.axis_index("head")
    first_head = my_group * local_heads
    last_row = row_base + row_count - 1
    roles_here = lax.dynamic_slice_in_dim(head_role, first_head, local_heads)
    sinks_here = lax.dynamic_slice_in_dim(sink_len, first_head, local_heads)
    windows_here = lax.dynamic_slice_in_dim(window_len, first_head, local_heads)
    query_heads = queries.reshape(row_count, local_heads, GROUP, HD)
    width = key_states.shape[1]
    both = lax.all_gather(
        jnp.concatenate([key_states, value_states], axis=1), "ctx", axis=0, tiled=True
    )
    key_part = both[:, :width].reshape(-1, local_heads, HD)
    value_part = both[:, width:].reshape(-1, local_heads, HD)
    key_pos = jnp.arange(key_part.shape[0], dtype=jnp.int32)

    def update(state):
        later = query_pos[:, None, None]
        earlier = key_pos[None, None, :]
        allowed = (earlier <= later) & (
            (roles_here[None, :, None] == 1)
            | (earlier < sinks_here[None, :, None])
            | (later - earlier < windows_here[None, :, None])
        )
        return online_update(state, query_heads, key_part, value_part, allowed)

    def unchanged(state):
        return state

    running = lax.cond(
        jnp.int32(0) <= last_row, update, unchanged, empty_state(row_count, local_heads)
    )
    attended = finish(running, row_count)
    mixed = lax.psum_scatter(
        jnp.dot(attended, out_weight, preferred_element_type=jnp.float32).astype(jnp.bfloat16),
        "head",
        scatter_dimension=0,
        tiled=True,
    )
    return mixed


def solution(mesh):
    in_specs = (
        P("ctx", "head"),
        P("ctx", "head"),
        P("ctx", "head"),
        P("head", None),
        P(),
        P(),
        P(),
    )
    out_specs = P(("ctx", "head"), None)
    return jax.shard_map(
        per_device, mesh=mesh, in_specs=in_specs, out_specs=out_specs, check_vma=False
    )
```

```python
import functools

import jax
import jax.numpy as jnp
from jax import lax
from jax.experimental import pallas as pl
from jax.experimental.pallas import tpu as pltpu
from jax.sharding import PartitionSpec as P

HD = 128
GROUP = 4
KEY_BLOCK = 512

NEGATIVE = -1e30


def attention_kernel(table_ref, meta_ref, q_ref, k_ref, v_ref, o_ref, peak_sc, total_sc, acc_sc):
    g = pl.program_id(0)
    step = pl.program_id(1)
    count = meta_ref[g, 0]
    is_retrieval = meta_ref[g, 1]
    sink = meta_ref[g, 2]
    window = meta_ref[g, 3]
    row_base = meta_ref[g, 4]
    rows = q_ref.shape[0]
    width = k_ref.shape[0]

    @pl.when(step == 0)
    def _():
        peak_sc[...] = jnp.full_like(peak_sc, NEGATIVE)
        total_sc[...] = jnp.zeros_like(total_sc)
        acc_sc[...] = jnp.zeros_like(acc_sc)

    @pl.when(step < count)
    def _():
        block = table_ref[g, step]
        key_base = block * width
        row = lax.broadcasted_iota(jnp.int32, (rows, width), 0)
        col = lax.broadcasted_iota(jnp.int32, (rows, width), 1)
        later_minus_earlier = (row - col) + (row_base - key_base)
        reach = jnp.where(is_retrieval == 1, jnp.int32(2**30), window)
        allowed = (later_minus_earlier >= 0) & (
            (later_minus_earlier < reach) | (col + key_base < sink)
        )
        keys = k_ref[...]
        values = v_ref[...]
        for i in range(GROUP):
            query = q_ref[:, i * HD:(i + 1) * HD]
            scores = lax.dot_general(
                query, keys, (((1,), (1,)), ((), ())), preferred_element_type=jnp.float32
            ) * HD ** (-0.5)
            old_peak = peak_sc[i]
            block_peak = jnp.max(jnp.where(allowed, scores, NEGATIVE), axis=-1, keepdims=True)
            new_peak = jnp.maximum(old_peak, block_peak)
            rescale = jnp.exp(old_peak - new_peak)
            weights = jnp.where(allowed, jnp.exp(scores - new_peak), 0.0)
            total_sc[i] = rescale * total_sc[i] + jnp.sum(weights, axis=-1, keepdims=True)
            acc_sc[i] = rescale * acc_sc[i] + jnp.dot(
                weights.astype(jnp.bfloat16), values, preferred_element_type=jnp.float32
            )
            peak_sc[i] = new_peak

    @pl.when(step == pl.num_programs(1) - 1)
    def _():
        for i in range(GROUP):
            o_ref[:, i * HD:(i + 1) * HD] = (acc_sc[i] / total_sc[i]).astype(o_ref.dtype)


def block_table(row_base, row_count, token_count, roles, sinks, windows):
    blocks = token_count // KEY_BLOCK
    first = jnp.arange(blocks, dtype=jnp.int32) * KEY_BLOCK
    last_key = first + KEY_BLOCK - 1
    causal = first <= row_base + row_count - 1
    reach = last_key[None, :] >= row_base - windows[:, None] + 1
    sunk = first[None, :] < sinks[:, None]
    needed = causal[None, :] & ((roles[:, None] == 1) | reach | sunk)
    order = jnp.argsort(jnp.logical_not(needed), axis=1, stable=True).astype(jnp.int32)
    count = jnp.sum(needed, axis=1).astype(jnp.int32)
    last = jnp.take_along_axis(order, (count - 1)[:, None], axis=1)
    steps = jnp.arange(blocks, dtype=jnp.int32)[None, :]
    table = jnp.where(steps < count[:, None], order, last)
    meta = jnp.stack(
        [count, roles, sinks, windows, jnp.broadcast_to(row_base, count.shape)], axis=1
    ).astype(jnp.int32)
    meta = jnp.pad(meta, ((0, 0), (0, 3)))
    return table, meta


def attend(queries, both, table, meta, local_heads):
    rows = queries.shape[0]
    blocks = table.shape[1]
    return pl.pallas_call(
        attention_kernel,
        out_shape=jax.ShapeDtypeStruct(queries.shape, jnp.bfloat16),
        grid_spec=pltpu.PrefetchScalarGridSpec(
            num_scalar_prefetch=2,
            grid=(local_heads, blocks),
            in_specs=[
                pl.BlockSpec((rows, GROUP * HD), lambda g, s, t, m: (0, g)),
                pl.BlockSpec((KEY_BLOCK, HD), lambda g, s, t, m: (t[g, s], g)),
                pl.BlockSpec((KEY_BLOCK, HD), lambda g, s, t, m: (t[g, s], local_heads + g)),
            ],
            out_specs=pl.BlockSpec((rows, GROUP * HD), lambda g, s, t, m: (0, g)),
            scratch_shapes=[
                pltpu.VMEM((GROUP, rows, 1), jnp.float32),
                pltpu.VMEM((GROUP, rows, 1), jnp.float32),
                pltpu.VMEM((GROUP, rows, HD), jnp.float32),
            ],
        ),
        compiler_params=pltpu.CompilerParams(
            dimension_semantics=("arbitrary", "arbitrary")
        ),
    )(table, meta, queries, both, both)


def per_device(queries, key_states, value_states, out_weight, head_role, sink_len, window_len):
    row_count = queries.shape[0]
    local_heads = key_states.shape[1] // HD
    row_base = lax.axis_index("ctx") * row_count
    first_head = lax.axis_index("head") * local_heads
    roles_here = lax.dynamic_slice_in_dim(head_role, first_head, local_heads)
    sinks_here = lax.dynamic_slice_in_dim(sink_len, first_head, local_heads)
    windows_here = lax.dynamic_slice_in_dim(window_len, first_head, local_heads)
    both = lax.all_gather(
        jnp.concatenate([key_states, value_states], axis=1), "ctx", axis=0, tiled=True
    )
    table, meta = block_table(
        row_base, row_count, both.shape[0], roles_here, sinks_here, windows_here
    )
    attended = attend(queries, both, table, meta, local_heads)
    mixed = lax.psum_scatter(
        jnp.dot(attended, out_weight, preferred_element_type=jnp.float32).astype(jnp.bfloat16),
        "head",
        scatter_dimension=0,
        tiled=True,
    )
    return mixed


def solution(mesh):
    in_specs = (
        P("ctx", "head"),
        P("ctx", "head"),
        P("ctx", "head"),
        P("head", None),
        P(),
        P(),
        P(),
    )
    out_specs = P(("ctx", "head"), None)
    return jax.shard_map(
        per_device, mesh=mesh, in_specs=in_specs, out_specs=out_specs, check_vma=False
    )
```

```python
import functools

import jax
import jax.numpy as jnp
from jax import lax
from jax.experimental import pallas as pl
from jax.experimental.pallas import tpu as pltpu
from jax.sharding import PartitionSpec as P

HD = 128
GROUP = 4
KEY_BLOCK = 512

NEGATIVE = -1e30


def attention_kernel(table_ref, meta_ref, q_ref, k_ref, v_ref, acc_ref, peak_ref, total_ref):
    g = pl.program_id(0)
    step = pl.program_id(1)
    count = meta_ref[g, 0]
    is_retrieval = meta_ref[g, 1]
    sink = meta_ref[g, 2]
    window = meta_ref[g, 3]
    row_base = meta_ref[g, 4]
    key_offset = meta_ref[g, 5]
    rows = q_ref.shape[0]
    width = k_ref.shape[0]

    @pl.when(step == 0)
    def _():
        peak_ref[...] = jnp.full_like(peak_ref, NEGATIVE)
        total_ref[...] = jnp.zeros_like(total_ref)
        acc_ref[...] = jnp.zeros_like(acc_ref)

    @pl.when(step < count)
    def _():
        block = table_ref[g, step]
        key_base = key_offset + block * width
        row = lax.broadcasted_iota(jnp.int32, (rows, width), 0)
        col = lax.broadcasted_iota(jnp.int32, (rows, width), 1)
        later_minus_earlier = (row - col) + (row_base - key_base)
        reach = jnp.where(is_retrieval == 1, jnp.int32(2**30), window)
        allowed = (later_minus_earlier >= 0) & (
            (later_minus_earlier < reach) | (col + key_base < sink)
        )
        keys = k_ref[...]
        values = v_ref[...]
        for i in range(GROUP):
            query = q_ref[:, i * HD:(i + 1) * HD]
            scores = lax.dot_general(
                query, keys, (((1,), (1,)), ((), ())), preferred_element_type=jnp.float32
            ) * HD ** (-0.5)
            old_peak = peak_ref[i]
            block_peak = jnp.max(jnp.where(allowed, scores, NEGATIVE), axis=-1, keepdims=True)
            new_peak = jnp.maximum(old_peak, block_peak)
            rescale = jnp.exp(old_peak - new_peak)
            weights = jnp.where(allowed, jnp.exp(scores - new_peak), 0.0)
            total_ref[i] = rescale * total_ref[i] + jnp.sum(weights, axis=-1, keepdims=True)
            acc_ref[:, i * HD:(i + 1) * HD] = rescale * acc_ref[:, i * HD:(i + 1) * HD] + jnp.dot(
                weights.astype(jnp.bfloat16), values, preferred_element_type=jnp.float32
            )
            peak_ref[i] = new_peak


def block_table(row_base, row_count, key_offset, key_count, roles, sinks, windows):
    blocks = key_count // KEY_BLOCK
    first = key_offset + jnp.arange(blocks, dtype=jnp.int32) * KEY_BLOCK
    last_key = first + KEY_BLOCK - 1
    causal = first <= row_base + row_count - 1
    reach = last_key[None, :] >= row_base - windows[:, None] + 1
    sunk = first[None, :] < sinks[:, None]
    needed = causal[None, :] & ((roles[:, None] == 1) | reach | sunk)
    order = jnp.argsort(jnp.logical_not(needed), axis=1, stable=True).astype(jnp.int32)
    count = jnp.sum(needed, axis=1).astype(jnp.int32)
    last = jnp.take_along_axis(order, jnp.maximum(count - 1, 0)[:, None], axis=1)
    steps = jnp.arange(blocks, dtype=jnp.int32)[None, :]
    table = jnp.where(steps < count[:, None], order, last)
    meta = jnp.stack(
        [
            count,
            roles,
            sinks,
            windows,
            jnp.broadcast_to(row_base, count.shape),
            jnp.broadcast_to(key_offset, count.shape),
        ],
        axis=1,
    ).astype(jnp.int32)
    meta = jnp.pad(meta, ((0, 0), (0, 2)))
    return table, meta


def attend(queries, both, table, meta, local_heads):
    rows = queries.shape[0]
    blocks = table.shape[1]
    heads = local_heads * GROUP
    return pl.pallas_call(
        attention_kernel,
        out_shape=(
            jax.ShapeDtypeStruct(queries.shape, jnp.float32),
            jax.ShapeDtypeStruct((heads, rows, 1), jnp.float32),
            jax.ShapeDtypeStruct((heads, rows, 1), jnp.float32),
        ),
        grid_spec=pltpu.PrefetchScalarGridSpec(
            num_scalar_prefetch=2,
            grid=(local_heads, blocks),
            in_specs=[
                pl.BlockSpec((rows, GROUP * HD), lambda g, s, t, m: (0, g)),
                pl.BlockSpec((KEY_BLOCK, HD), lambda g, s, t, m: (t[g, s], g)),
                pl.BlockSpec((KEY_BLOCK, HD), lambda g, s, t, m: (t[g, s], local_heads + g)),
            ],
            out_specs=(
                pl.BlockSpec((rows, GROUP * HD), lambda g, s, t, m: (0, g)),
                pl.BlockSpec((GROUP, rows, 1), lambda g, s, t, m: (g, 0, 0)),
                pl.BlockSpec((GROUP, rows, 1), lambda g, s, t, m: (g, 0, 0)),
            ),
        ),
        compiler_params=pltpu.CompilerParams(
            dimension_semantics=("arbitrary", "arbitrary")
        ),
    )(table, meta, queries, both, both)


def merge(own, other, row_count):
    acc_a, peak_a, total_a = own
    acc_b, peak_b, total_b = other
    heads = peak_a.shape[0]
    peak_a = peak_a.reshape(heads, row_count).T[:, :, None]
    peak_b = peak_b.reshape(heads, row_count).T[:, :, None]
    total_a = total_a.reshape(heads, row_count).T[:, :, None]
    total_b = total_b.reshape(heads, row_count).T[:, :, None]
    peak = jnp.maximum(peak_a, peak_b)
    scale_a = jnp.exp(peak_a - peak)
    scale_b = jnp.exp(peak_b - peak)
    acc = acc_a.reshape(row_count, heads, HD) * scale_a + acc_b.reshape(row_count, heads, HD) * scale_b
    total = total_a * scale_a + total_b * scale_b
    return (acc / total).astype(jnp.bfloat16).reshape(row_count, heads * HD)


def per_device(queries, key_states, value_states, out_weight, head_role, sink_len, window_len):
    row_count = queries.shape[0]
    local_heads = key_states.shape[1] // HD
    half = lax.axis_index("xh")
    ctx = half * lax.axis_size("zy") + lax.axis_index("zy")
    partner = (1 - half) * lax.axis_size("zy") + lax.axis_index("zy")
    first_head = lax.axis_index("head") * local_heads
    roles_here = lax.dynamic_slice_in_dim(head_role, first_head, local_heads)
    sinks_here = lax.dynamic_slice_in_dim(sink_len, first_head, local_heads)
    windows_here = lax.dynamic_slice_in_dim(window_len, first_head, local_heads)
    swap = [(0, 1), (1, 0)]
    partner_queries = lax.ppermute(queries, "xh", swap)
    both = lax.all_gather(
        jnp.concatenate([key_states, value_states], axis=1), "zy", axis=0, tiled=True
    )
    key_offset = half * both.shape[0]
    table, meta = block_table(
        partner * row_count, row_count, key_offset, both.shape[0],
        roles_here, sinks_here, windows_here,
    )
    for_partner = attend(partner_queries, both, table, meta, local_heads)
    from_partner = lax.ppermute(for_partner, "xh", swap)
    table, meta = block_table(
        ctx * row_count, row_count, key_offset, both.shape[0],
        roles_here, sinks_here, windows_here,
    )
    own = attend(queries, both, table, meta, local_heads)
    attended = merge(own, from_partner, row_count)
    mixed = lax.psum_scatter(
        jnp.dot(attended, out_weight, preferred_element_type=jnp.float32).astype(jnp.bfloat16),
        "head",
        scatter_dimension=0,
        tiled=True,
    )
    return mixed


def solution(mesh):
    ctx_size = mesh.shape["ctx"]
    devices = mesh.devices.reshape(2, ctx_size // 2, mesh.shape["head"])
    split = jax.sharding.Mesh(devices, ("xh", "zy", "head"))
    tokens = ("xh", "zy")
    in_specs = (
        P(tokens, "head"),
        P(tokens, "head"),
        P(tokens, "head"),
        P("head", None),
        P(),
        P(),
        P(),
    )
    out_specs = P(("xh", "zy", "head"), None)
    return jax.shard_map(
        per_device, mesh=split, in_specs=in_specs, out_specs=out_specs, check_vma=False
    )
```

```python
import functools

import jax
import jax.numpy as jnp
from jax import lax
from jax.experimental import pallas as pl
from jax.experimental.pallas import tpu as pltpu
from jax.sharding import PartitionSpec as P

HD = 128
GROUP = 4
KEY_BLOCK = 512

NEGATIVE = -1e30


def attention_kernel(table_ref, meta_ref, q_ref, k_ref, v_ref, acc_ref, peak_ref, total_ref):
    g = pl.program_id(0)
    step = pl.program_id(1)
    blocks = pl.num_programs(1)
    count = meta_ref[g, 0]
    is_retrieval = meta_ref[g, 1]
    sink = meta_ref[g, 2]
    window = meta_ref[g, 3]
    row_base = meta_ref[g, 4]
    key_offset = meta_ref[g, 5]
    rows = q_ref.shape[1] // GROUP
    width = k_ref.shape[0]

    @pl.when(step == 0)
    def _():
        peak_ref[...] = jnp.full_like(peak_ref, NEGATIVE)
        total_ref[...] = jnp.zeros_like(total_ref)
        acc_ref[...] = jnp.zeros_like(acc_ref)

    def update(allowed):
        scores = lax.dot_general(
            q_ref[0], k_ref[...], (((1,), (1,)), ((), ())), preferred_element_type=jnp.float32
        ) * HD ** (-0.5)
        old_peak = peak_ref[0]
        if allowed is None:
            block_peak = jnp.max(scores, axis=-1, keepdims=True)
            new_peak = jnp.maximum(old_peak, block_peak)
            weights = jnp.exp(scores - new_peak)
        else:
            scores = scores.reshape(GROUP, rows, width)
            block_peak = jnp.max(
                jnp.where(allowed, scores, NEGATIVE), axis=-1, keepdims=True
            ).reshape(GROUP * rows, 1)
            new_peak = jnp.maximum(old_peak, block_peak)
            weights = jnp.where(
                allowed, jnp.exp(scores - new_peak.reshape(GROUP, rows, 1)), 0.0
            ).reshape(GROUP * rows, width)
        rescale = jnp.exp(old_peak - new_peak)
        total_ref[0] = rescale * total_ref[0] + jnp.sum(weights, axis=-1, keepdims=True)
        acc_ref[0] = rescale * acc_ref[0] + jnp.dot(
            weights.astype(jnp.bfloat16), v_ref[...], preferred_element_type=jnp.float32
        )
        peak_ref[0] = new_peak

    full = table_ref[g, blocks + step]

    @pl.when((step < count) & (full == 1))
    def _():
        update(None)

    @pl.when((step < count) & (full == 0))
    def _():
        block = table_ref[g, step]
        key_base = key_offset + block * width
        row = lax.broadcasted_iota(jnp.int32, (rows, width), 0)
        col = lax.broadcasted_iota(jnp.int32, (rows, width), 1)
        later_minus_earlier = (row - col) + (row_base - key_base)
        reach = jnp.where(is_retrieval == 1, jnp.int32(2**30), window)
        allowed = (later_minus_earlier >= 0) & (
            (later_minus_earlier < reach) | (col + key_base < sink)
        )
        update(allowed[None])


def block_table(row_base, row_count, key_offset, key_count, roles, sinks, windows):
    blocks = key_count // KEY_BLOCK
    first = key_offset + jnp.arange(blocks, dtype=jnp.int32) * KEY_BLOCK
    last_key = first + KEY_BLOCK - 1
    last_row = row_base + row_count - 1
    causal = first <= last_row
    reach = last_key[None, :] >= row_base - windows[:, None] + 1
    sunk = first[None, :] < sinks[:, None]
    retrieval = roles[:, None] == 1
    needed = causal[None, :] & (retrieval | reach | sunk)
    whole = (last_key <= row_base)[None, :] & (
        retrieval
        | (last_key[None, :] < sinks[:, None])
        | (last_row - first[None, :] < windows[:, None])
    )
    order = jnp.argsort(jnp.logical_not(needed), axis=1, stable=True).astype(jnp.int32)
    count = jnp.sum(needed, axis=1).astype(jnp.int32)
    last = jnp.take_along_axis(order, jnp.maximum(count - 1, 0)[:, None], axis=1)
    steps = jnp.arange(blocks, dtype=jnp.int32)[None, :]
    table = jnp.where(steps < count[:, None], order, last)
    full = jnp.take_along_axis(whole, table, axis=1).astype(jnp.int32)
    meta = jnp.stack(
        [
            count,
            roles,
            sinks,
            windows,
            jnp.broadcast_to(row_base, count.shape),
            jnp.broadcast_to(key_offset, count.shape),
        ],
        axis=1,
    ).astype(jnp.int32)
    meta = jnp.pad(meta, ((0, 0), (0, 2)))
    return jnp.concatenate([table, full], axis=1), meta


def attend(stacked, both, table, meta):
    local_heads, stack_rows, _ = stacked.shape
    blocks = table.shape[1] // 2
    return pl.pallas_call(
        attention_kernel,
        out_shape=(
            jax.ShapeDtypeStruct(stacked.shape, jnp.float32),
            jax.ShapeDtypeStruct((local_heads, stack_rows, 1), jnp.float32),
            jax.ShapeDtypeStruct((local_heads, stack_rows, 1), jnp.float32),
        ),
        grid_spec=pltpu.PrefetchScalarGridSpec(
            num_scalar_prefetch=2,
            grid=(local_heads, blocks),
            in_specs=[
                pl.BlockSpec((1, stack_rows, HD), lambda g, s, t, m: (g, 0, 0)),
                pl.BlockSpec((KEY_BLOCK, HD), lambda g, s, t, m: (t[g, s], g)),
                pl.BlockSpec((KEY_BLOCK, HD), lambda g, s, t, m: (t[g, s], local_heads + g)),
            ],
            out_specs=(
                pl.BlockSpec((1, stack_rows, HD), lambda g, s, t, m: (g, 0, 0)),
                pl.BlockSpec((1, stack_rows, 1), lambda g, s, t, m: (g, 0, 0)),
                pl.BlockSpec((1, stack_rows, 1), lambda g, s, t, m: (g, 0, 0)),
            ),
        ),
        compiler_params=pltpu.CompilerParams(
            dimension_semantics=("arbitrary", "arbitrary")
        ),
    )(table, meta, stacked, both, both)


def stack_heads(queries, local_heads):
    rows = queries.shape[0]
    return (
        queries.reshape(rows, local_heads, GROUP, HD)
        .transpose(1, 2, 0, 3)
        .reshape(local_heads, GROUP * rows, HD)
    )


def merge(own, other, row_count):
    acc_a, peak_a, total_a = own
    acc_b, peak_b, total_b = other
    peak = jnp.maximum(peak_a, peak_b)
    scale_a = jnp.exp(peak_a - peak)
    scale_b = jnp.exp(peak_b - peak)
    acc = acc_a * scale_a + acc_b * scale_b
    total = total_a * scale_a + total_b * scale_b
    local_heads = acc.shape[0]
    attended = (acc / total).astype(jnp.bfloat16)
    return (
        attended.reshape(local_heads, GROUP, row_count, HD)
        .transpose(2, 0, 1, 3)
        .reshape(row_count, local_heads * GROUP * HD)
    )


def per_device(queries, key_states, value_states, out_weight, head_role, sink_len, window_len):
    row_count = queries.shape[0]
    local_heads = key_states.shape[1] // HD
    half = lax.axis_index("xh")
    ctx = half * lax.axis_size("zy") + lax.axis_index("zy")
    partner = (1 - half) * lax.axis_size("zy") + lax.axis_index("zy")
    first_head = lax.axis_index("head") * local_heads
    roles_here = lax.dynamic_slice_in_dim(head_role, first_head, local_heads)
    sinks_here = lax.dynamic_slice_in_dim(sink_len, first_head, local_heads)
    windows_here = lax.dynamic_slice_in_dim(window_len, first_head, local_heads)
    swap = [(0, 1), (1, 0)]
    partner_queries = lax.ppermute(stack_heads(queries, local_heads), "xh", swap)
    both = lax.all_gather(
        jnp.concatenate([key_states, value_states], axis=1), "zy", axis=0, tiled=True
    )
    key_offset = half * both.shape[0]
    table, meta = block_table(
        partner * row_count, row_count, key_offset, both.shape[0],
        roles_here, sinks_here, windows_here,
    )
    for_partner = attend(partner_queries, both, table, meta)
    from_partner = lax.ppermute(for_partner, "xh", swap)
    table, meta = block_table(
        ctx * row_count, row_count, key_offset, both.shape[0],
        roles_here, sinks_here, windows_here,
    )
    own = attend(stack_heads(queries, local_heads), both, table, meta)
    attended = merge(own, from_partner, row_count)
    mixed = lax.psum_scatter(
        jnp.dot(attended, out_weight, preferred_element_type=jnp.float32).astype(jnp.bfloat16),
        "head",
        scatter_dimension=0,
        tiled=True,
    )
    return mixed


def solution(mesh):
    ctx_size = mesh.shape["ctx"]
    devices = mesh.devices.reshape(2, ctx_size // 2, mesh.shape["head"])
    split = jax.sharding.Mesh(devices, ("xh", "zy", "head"))
    tokens = ("xh", "zy")
    in_specs = (
        P(tokens, "head"),
        P(tokens, "head"),
        P(tokens, "head"),
        P("head", None),
        P(),
        P(),
        P(),
    )
    out_specs = P(("xh", "zy", "head"), None)
    return jax.shard_map(
        per_device, mesh=split, in_specs=in_specs, out_specs=out_specs, check_vma=False
    )
```

```python
import functools

import jax
import jax.numpy as jnp
from jax import lax
from jax.experimental import pallas as pl
from jax.experimental.pallas import tpu as pltpu
from jax.sharding import PartitionSpec as P

HD = 128
GROUP = 4
KEY_BLOCK = 512

NEGATIVE = -1e30


def attention_kernel(table_ref, meta_ref, q_ref, k_ref, v_ref, acc_ref, peak_ref, total_ref):
    g = pl.program_id(0)
    step = pl.program_id(1)
    blocks = pl.num_programs(1)
    count = meta_ref[g, 0]
    is_retrieval = meta_ref[g, 1]
    sink = meta_ref[g, 2]
    window = meta_ref[g, 3]
    row_base = meta_ref[g, 4]
    key_offset = meta_ref[g, 5]
    rows = q_ref.shape[1] // GROUP
    width = k_ref.shape[0]

    @pl.when(step == 0)
    def _():
        peak_ref[...] = jnp.full_like(peak_ref, NEGATIVE)
        total_ref[...] = jnp.zeros_like(total_ref)
        acc_ref[...] = jnp.zeros_like(acc_ref)

    def update(allowed):
        scores = lax.dot_general(
            q_ref[0], k_ref[...], (((1,), (1,)), ((), ())), preferred_element_type=jnp.float32
        ) * HD ** (-0.5)
        old_peak = peak_ref[0]
        if allowed is None:
            block_peak = jnp.max(scores, axis=-1, keepdims=True)
            new_peak = jnp.maximum(old_peak, block_peak)
            weights = jnp.exp(scores - new_peak)
        else:
            scores = scores.reshape(GROUP, rows, width)
            block_peak = jnp.max(
                jnp.where(allowed, scores, NEGATIVE), axis=-1, keepdims=True
            ).reshape(GROUP * rows, 1)
            new_peak = jnp.maximum(old_peak, block_peak)
            weights = jnp.where(
                allowed, jnp.exp(scores - new_peak.reshape(GROUP, rows, 1)), 0.0
            ).reshape(GROUP * rows, width)
        rescale = jnp.exp(old_peak - new_peak)
        total_ref[0] = rescale * total_ref[0] + jnp.sum(weights, axis=-1, keepdims=True)
        acc_ref[0] = rescale * acc_ref[0] + jnp.dot(
            weights.astype(jnp.bfloat16), v_ref[...], preferred_element_type=jnp.float32
        )
        peak_ref[0] = new_peak

    full = table_ref[g, blocks + step]

    @pl.when((step < count) & (full == 1))
    def _():
        update(None)

    @pl.when((step < count) & (full == 0))
    def _():
        block = table_ref[g, step]
        key_base = key_offset + block * width
        row = lax.broadcasted_iota(jnp.int32, (rows, width), 0)
        col = lax.broadcasted_iota(jnp.int32, (rows, width), 1)
        later_minus_earlier = (row - col) + (row_base - key_base)
        reach = jnp.where(is_retrieval == 1, jnp.int32(2**30), window)
        allowed = (later_minus_earlier >= 0) & (
            (later_minus_earlier < reach) | (col + key_base < sink)
        )
        update(allowed[None])


def block_table(row_base, row_count, key_offset, key_count, roles, sinks, windows):
    blocks = key_count // KEY_BLOCK
    first = key_offset + jnp.arange(blocks, dtype=jnp.int32) * KEY_BLOCK
    last_key = first + KEY_BLOCK - 1
    last_row = row_base + row_count - 1
    causal = first <= last_row
    reach = last_key[None, :] >= row_base - windows[:, None] + 1
    sunk = first[None, :] < sinks[:, None]
    retrieval = roles[:, None] == 1
    needed = causal[None, :] & (retrieval | reach | sunk)
    whole = (last_key <= row_base)[None, :] & (
        retrieval
        | (last_key[None, :] < sinks[:, None])
        | (last_row - first[None, :] < windows[:, None])
    )
    order = jnp.argsort(jnp.logical_not(needed), axis=1, stable=True).astype(jnp.int32)
    count = jnp.sum(needed, axis=1).astype(jnp.int32)
    last = jnp.take_along_axis(order, jnp.maximum(count - 1, 0)[:, None], axis=1)
    steps = jnp.arange(blocks, dtype=jnp.int32)[None, :]
    table = jnp.where(steps < count[:, None], order, last)
    full = jnp.take_along_axis(whole, table, axis=1).astype(jnp.int32)
    meta = jnp.stack(
        [
            count,
            roles,
            sinks,
            windows,
            jnp.broadcast_to(row_base, count.shape),
            jnp.broadcast_to(key_offset, count.shape),
        ],
        axis=1,
    ).astype(jnp.int32)
    meta = jnp.pad(meta, ((0, 0), (0, 2)))
    return jnp.concatenate([table, full], axis=1), meta


def attend(stacked, both, table, meta):
    local_heads, stack_rows, _ = stacked.shape
    blocks = table.shape[1] // 2
    return pl.pallas_call(
        attention_kernel,
        out_shape=(
            jax.ShapeDtypeStruct(stacked.shape, jnp.float32),
            jax.ShapeDtypeStruct((local_heads, stack_rows, 1), jnp.float32),
            jax.ShapeDtypeStruct((local_heads, stack_rows, 1), jnp.float32),
        ),
        grid_spec=pltpu.PrefetchScalarGridSpec(
            num_scalar_prefetch=2,
            grid=(local_heads, blocks),
            in_specs=[
                pl.BlockSpec((1, stack_rows, HD), lambda g, s, t, m: (g, 0, 0)),
                pl.BlockSpec((KEY_BLOCK, HD), lambda g, s, t, m: (t[g, s], g)),
                pl.BlockSpec((KEY_BLOCK, HD), lambda g, s, t, m: (t[g, s], local_heads + g)),
            ],
            out_specs=(
                pl.BlockSpec((1, stack_rows, HD), lambda g, s, t, m: (g, 0, 0)),
                pl.BlockSpec((1, stack_rows, 1), lambda g, s, t, m: (g, 0, 0)),
                pl.BlockSpec((1, stack_rows, 1), lambda g, s, t, m: (g, 0, 0)),
            ),
        ),
        compiler_params=pltpu.CompilerParams(
            dimension_semantics=("arbitrary", "arbitrary")
        ),
    )(table, meta, stacked, both, both)


def stack_heads(queries, local_heads):
    rows = queries.shape[0]
    return (
        queries.reshape(rows, local_heads, GROUP, HD)
        .transpose(1, 2, 0, 3)
        .reshape(local_heads, GROUP * rows, HD)
    )


def merge(own, other, row_count):
    acc_a, peak_a, total_a = own
    acc_b, peak_b, total_b = other
    peak = jnp.maximum(peak_a, peak_b)
    scale_a = jnp.exp(peak_a - peak)
    scale_b = jnp.exp(peak_b - peak)
    acc = acc_a * scale_a + acc_b * scale_b
    total = total_a * scale_a + total_b * scale_b
    local_heads = acc.shape[0]
    attended = (acc / total).astype(jnp.bfloat16)
    return (
        attended.reshape(local_heads, GROUP, row_count, HD)
        .transpose(2, 0, 1, 3)
        .reshape(row_count, local_heads * GROUP * HD)
    )


def per_device(queries, key_states, value_states, out_weight, head_role, sink_len, window_len):
    row_count = queries.shape[0]
    local_heads = key_states.shape[1] // HD
    half_size = lax.axis_size("z") * lax.axis_size("y")
    half = lax.axis_index("xh")
    place = lax.axis_index("z") * lax.axis_size("y") + lax.axis_index("y")
    ctx = half * half_size + place
    partner = (1 - half) * half_size + place
    first_head = lax.axis_index("head") * local_heads
    roles_here = lax.dynamic_slice_in_dim(head_role, first_head, local_heads)
    sinks_here = lax.dynamic_slice_in_dim(sink_len, first_head, local_heads)
    windows_here = lax.dynamic_slice_in_dim(window_len, first_head, local_heads)
    partner_queries = lax.ppermute(stack_heads(queries, local_heads), "xh", [(1, 0)])
    both = jnp.concatenate([key_states, value_states], axis=1)
    both = lax.all_gather(both, "y", axis=0, tiled=True)
    both = lax.all_gather(both, "z", axis=0, tiled=True)
    key_offset = half * both.shape[0]
    table, meta = block_table(
        partner * row_count, row_count, key_offset, both.shape[0],
        roles_here, sinks_here, windows_here,
    )
    acc_p, peak_p, total_p = attend(partner_queries, both, table, meta)
    stats_p = jnp.concatenate(
        [peak_p.reshape(local_heads, -1), total_p.reshape(local_heads, -1)], axis=0
    )
    acc_p = lax.ppermute(acc_p.astype(jnp.bfloat16), "xh", [(0, 1)])
    stats_p = lax.ppermute(stats_p, "xh", [(0, 1)])
    table, meta = block_table(
        ctx * row_count, row_count, key_offset, both.shape[0],
        roles_here, sinks_here, windows_here,
    )
    own = attend(stack_heads(queries, local_heads), both, table, meta)
    received = half == 1
    peak_b = jnp.where(received, stats_p[:local_heads], NEGATIVE)[:, :, None]
    total_b = jnp.where(received, stats_p[local_heads:], 0.0)[:, :, None]
    acc_b = jnp.where(received, acc_p.astype(jnp.float32), 0.0)
    attended = merge(own, (acc_b, peak_b, total_b), row_count)
    mixed = lax.psum_scatter(
        jnp.dot(attended, out_weight, preferred_element_type=jnp.float32).astype(jnp.bfloat16),
        "head",
        scatter_dimension=0,
        tiled=True,
    )
    return mixed


def solution(mesh):
    ctx_size = mesh.shape["ctx"]
    y_size = 4
    devices = mesh.devices.reshape(
        2, ctx_size // (2 * y_size), y_size, mesh.shape["head"]
    )
    split = jax.sharding.Mesh(devices, ("xh", "z", "y", "head"))
    tokens = ("xh", "z", "y")
    in_specs = (
        P(tokens, "head"),
        P(tokens, "head"),
        P(tokens, "head"),
        P("head", None),
        P(),
        P(),
        P(),
    )
    out_specs = P(("xh", "z", "y", "head"), None)
    return jax.shard_map(
        per_device, mesh=split, in_specs=in_specs, out_specs=out_specs, check_vma=False
    )
```

```python
import functools

import jax
import jax.numpy as jnp
from jax import lax
from jax.experimental import pallas as pl
from jax.experimental.pallas import tpu as pltpu
from jax.sharding import PartitionSpec as P

HD = 128
GROUP = 4
KEY_BLOCK = 1024

NEGATIVE = -1e30


def attention_kernel(table_ref, meta_ref, q_ref, k_ref, v_ref, acc_ref, peak_ref, total_ref):
    g = pl.program_id(0)
    step = pl.program_id(1)
    blocks = pl.num_programs(1)
    count = meta_ref[g, 0]
    is_retrieval = meta_ref[g, 1]
    sink = meta_ref[g, 2]
    window = meta_ref[g, 3]
    row_base = meta_ref[g, 4]
    key_offset = meta_ref[g, 5]
    rows = q_ref.shape[1] // GROUP
    width = k_ref.shape[0]

    @pl.when(step == 0)
    def _():
        peak_ref[...] = jnp.full_like(peak_ref, NEGATIVE)
        total_ref[...] = jnp.zeros_like(total_ref)
        acc_ref[...] = jnp.zeros_like(acc_ref)

    def update(allowed):
        scores = lax.dot_general(
            q_ref[0], k_ref[...], (((1,), (1,)), ((), ())), preferred_element_type=jnp.float32
        ) * HD ** (-0.5)
        old_peak = peak_ref[0]
        if allowed is None:
            block_peak = jnp.max(scores, axis=-1, keepdims=True)
            new_peak = jnp.maximum(old_peak, block_peak)
            weights = jnp.exp(scores - new_peak)
        else:
            scores = scores.reshape(GROUP, rows, width)
            block_peak = jnp.max(
                jnp.where(allowed, scores, NEGATIVE), axis=-1, keepdims=True
            ).reshape(GROUP * rows, 1)
            new_peak = jnp.maximum(old_peak, block_peak)
            weights = jnp.where(
                allowed, jnp.exp(scores - new_peak.reshape(GROUP, rows, 1)), 0.0
            ).reshape(GROUP * rows, width)
        rescale = jnp.exp(old_peak - new_peak)
        total_ref[0] = rescale * total_ref[0] + jnp.sum(weights, axis=-1, keepdims=True)
        acc_ref[0] = rescale * acc_ref[0] + jnp.dot(
            weights.astype(jnp.bfloat16), v_ref[...], preferred_element_type=jnp.float32
        )
        peak_ref[0] = new_peak

    full = table_ref[g, blocks + step]

    @pl.when((step < count) & (full == 1))
    def _():
        update(None)

    @pl.when((step < count) & (full == 0))
    def _():
        block = table_ref[g, step]
        key_base = key_offset + block * width
        row = lax.broadcasted_iota(jnp.int32, (rows, width), 0)
        col = lax.broadcasted_iota(jnp.int32, (rows, width), 1)
        later_minus_earlier = (row - col) + (row_base - key_base)
        reach = jnp.where(is_retrieval == 1, jnp.int32(2**30), window)
        allowed = (later_minus_earlier >= 0) & (
            (later_minus_earlier < reach) | (col + key_base < sink)
        )
        update(allowed[None])


def block_table(row_base, row_count, key_offset, key_count, roles, sinks, windows):
    blocks = key_count // KEY_BLOCK
    first = key_offset + jnp.arange(blocks, dtype=jnp.int32) * KEY_BLOCK
    last_key = first + KEY_BLOCK - 1
    last_row = row_base + row_count - 1
    causal = first <= last_row
    reach = last_key[None, :] >= row_base - windows[:, None] + 1
    sunk = first[None, :] < sinks[:, None]
    retrieval = roles[:, None] == 1
    needed = causal[None, :] & (retrieval | reach | sunk)
    whole = (last_key <= row_base)[None, :] & (
        retrieval
        | (last_key[None, :] < sinks[:, None])
        | (last_row - first[None, :] < windows[:, None])
    )
    order = jnp.argsort(jnp.logical_not(needed), axis=1, stable=True).astype(jnp.int32)
    count = jnp.sum(needed, axis=1).astype(jnp.int32)
    last = jnp.take_along_axis(order, jnp.maximum(count - 1, 0)[:, None], axis=1)
    steps = jnp.arange(blocks, dtype=jnp.int32)[None, :]
    table = jnp.where(steps < count[:, None], order, last)
    full = jnp.take_along_axis(whole, table, axis=1).astype(jnp.int32)
    meta = jnp.stack(
        [
            count,
            roles,
            sinks,
            windows,
            jnp.broadcast_to(row_base, count.shape),
            jnp.broadcast_to(key_offset, count.shape),
        ],
        axis=1,
    ).astype(jnp.int32)
    meta = jnp.pad(meta, ((0, 0), (0, 2)))
    return jnp.concatenate([table, full], axis=1), meta


def attend(stacked, both, table, meta):
    local_heads, stack_rows, _ = stacked.shape
    blocks = table.shape[1] // 2
    return pl.pallas_call(
        attention_kernel,
        out_shape=(
            jax.ShapeDtypeStruct(stacked.shape, jnp.float32),
            jax.ShapeDtypeStruct((local_heads, stack_rows, 1), jnp.float32),
            jax.ShapeDtypeStruct((local_heads, stack_rows, 1), jnp.float32),
        ),
        grid_spec=pltpu.PrefetchScalarGridSpec(
            num_scalar_prefetch=2,
            grid=(local_heads, blocks),
            in_specs=[
                pl.BlockSpec((1, stack_rows, HD), lambda g, s, t, m: (g, 0, 0)),
                pl.BlockSpec((KEY_BLOCK, HD), lambda g, s, t, m: (t[g, s], g)),
                pl.BlockSpec((KEY_BLOCK, HD), lambda g, s, t, m: (t[g, s], local_heads + g)),
            ],
            out_specs=(
                pl.BlockSpec((1, stack_rows, HD), lambda g, s, t, m: (g, 0, 0)),
                pl.BlockSpec((1, stack_rows, 1), lambda g, s, t, m: (g, 0, 0)),
                pl.BlockSpec((1, stack_rows, 1), lambda g, s, t, m: (g, 0, 0)),
            ),
        ),
        compiler_params=pltpu.CompilerParams(
            dimension_semantics=("arbitrary", "arbitrary")
        ),
    )(table, meta, stacked, both, both)


def stack_heads(queries, local_heads):
    rows = queries.shape[0]
    return (
        queries.reshape(rows, local_heads, GROUP, HD)
        .transpose(1, 2, 0, 3)
        .reshape(local_heads, GROUP * rows, HD)
    )


def merge(own, other, row_count):
    acc_a, peak_a, total_a = own
    acc_b, peak_b, total_b = other
    peak = jnp.maximum(peak_a, peak_b)
    scale_a = jnp.exp(peak_a - peak)
    scale_b = jnp.exp(peak_b - peak)
    acc = acc_a * scale_a + acc_b * scale_b
    total = total_a * scale_a + total_b * scale_b
    local_heads = acc.shape[0]
    attended = (acc / total).astype(jnp.bfloat16)
    return (
        attended.reshape(local_heads, GROUP, row_count, HD)
        .transpose(2, 0, 1, 3)
        .reshape(row_count, local_heads * GROUP * HD)
    )


def per_device(queries, key_states, value_states, out_weight, head_role, sink_len, window_len):
    row_count = queries.shape[0]
    local_heads = key_states.shape[1] // HD
    half_size = lax.axis_size("z") * lax.axis_size("y")
    half = lax.axis_index("xh")
    place = lax.axis_index("z") * lax.axis_size("y") + lax.axis_index("y")
    ctx = half * half_size + place
    partner = (1 - half) * half_size + place
    first_head = lax.axis_index("head") * local_heads
    roles_here = lax.dynamic_slice_in_dim(head_role, first_head, local_heads)
    sinks_here = lax.dynamic_slice_in_dim(sink_len, first_head, local_heads)
    windows_here = lax.dynamic_slice_in_dim(window_len, first_head, local_heads)
    partner_queries = lax.ppermute(stack_heads(queries, local_heads), "xh", [(1, 0)])
    both = jnp.concatenate([key_states, value_states], axis=1)
    both = lax.all_gather(both, "y", axis=0, tiled=True)
    both = lax.all_gather(both, "z", axis=0, tiled=True)
    key_offset = half * both.shape[0]
    table, meta = block_table(
        partner * row_count, row_count, key_offset, both.shape[0],
        roles_here, sinks_here, windows_here,
    )
    acc_p, peak_p, total_p = attend(partner_queries, both, table, meta)
    stats_p = jnp.concatenate(
        [peak_p.reshape(local_heads, -1), total_p.reshape(local_heads, -1)], axis=0
    )
    acc_p = lax.ppermute(acc_p.astype(jnp.bfloat16), "xh", [(0, 1)])
    stats_p = lax.ppermute(stats_p, "xh", [(0, 1)])
    table, meta = block_table(
        ctx * row_count, row_count, key_offset, both.shape[0],
        roles_here, sinks_here, windows_here,
    )
    own = attend(stack_heads(queries, local_heads), both, table, meta)
    received = half == 1
    peak_b = jnp.where(received, stats_p[:local_heads], NEGATIVE)[:, :, None]
    total_b = jnp.where(received, stats_p[local_heads:], 0.0)[:, :, None]
    acc_b = jnp.where(received, acc_p.astype(jnp.float32), 0.0)
    attended = merge(own, (acc_b, peak_b, total_b), row_count)
    mixed = lax.psum_scatter(
        jnp.dot(attended, out_weight, preferred_element_type=jnp.float32).astype(jnp.bfloat16),
        "head",
        scatter_dimension=0,
        tiled=True,
    )
    return mixed


def solution(mesh):
    ctx_size = mesh.shape["ctx"]
    y_size = 4
    devices = mesh.devices.reshape(
        2, ctx_size // (2 * y_size), y_size, mesh.shape["head"]
    )
    split = jax.sharding.Mesh(devices, ("xh", "z", "y", "head"))
    tokens = ("xh", "z", "y")
    in_specs = (
        P(tokens, "head"),
        P(tokens, "head"),
        P(tokens, "head"),
        P("head", None),
        P(),
        P(),
        P(),
    )
    out_specs = P(("xh", "z", "y", "head"), None)
    return jax.shard_map(
        per_device, mesh=split, in_specs=in_specs, out_specs=out_specs, check_vma=False
    )
```

```python
import functools

import jax
import jax.numpy as jnp
from jax import lax
from jax.experimental import pallas as pl
from jax.experimental.pallas import tpu as pltpu
from jax.sharding import PartitionSpec as P

HD = 128
GROUP = 4
KEY_BLOCK = 1024

NEGATIVE = -1e30


def attention_kernel(table_ref, meta_ref, q_ref, k_ref, v_ref, acc_ref, peak_ref, total_ref):
    g = pl.program_id(0)
    step = pl.program_id(1)
    blocks = pl.num_programs(1)
    count = meta_ref[g, 0]
    is_retrieval = meta_ref[g, 1]
    sink = meta_ref[g, 2]
    window = meta_ref[g, 3]
    row_base = meta_ref[g, 4]
    key_offset = meta_ref[g, 5]
    rows = q_ref.shape[1] // GROUP
    width = k_ref.shape[0]

    @pl.when(step == 0)
    def _():
        peak_ref[...] = jnp.full_like(peak_ref, NEGATIVE)
        total_ref[...] = jnp.zeros_like(total_ref)
        acc_ref[...] = jnp.zeros_like(acc_ref)

    def update(allowed):
        scores = lax.dot_general(
            q_ref[0], k_ref[...], (((1,), (1,)), ((), ())), preferred_element_type=jnp.float32
        ) * HD ** (-0.5)
        old_peak = peak_ref[0]
        if allowed is None:
            block_peak = jnp.max(scores, axis=-1, keepdims=True)
            new_peak = jnp.maximum(old_peak, block_peak)
            weights = jnp.exp(scores - new_peak)
        else:
            scores = scores.reshape(GROUP, rows, width)
            block_peak = jnp.max(
                jnp.where(allowed, scores, NEGATIVE), axis=-1, keepdims=True
            ).reshape(GROUP * rows, 1)
            new_peak = jnp.maximum(old_peak, block_peak)
            weights = jnp.where(
                allowed, jnp.exp(scores - new_peak.reshape(GROUP, rows, 1)), 0.0
            ).reshape(GROUP * rows, width)
        rescale = jnp.exp(old_peak - new_peak)
        total_ref[0] = rescale * total_ref[0] + jnp.sum(weights, axis=-1, keepdims=True)
        acc_ref[0] = rescale * acc_ref[0] + jnp.dot(
            weights.astype(jnp.bfloat16), v_ref[...], preferred_element_type=jnp.float32
        )
        peak_ref[0] = new_peak

    full = table_ref[g, blocks + step]

    @pl.when((step < count) & (full == 1))
    def _():
        update(None)

    @pl.when((step < count) & (full == 0))
    def _():
        block = table_ref[g, step]
        key_base = key_offset + block * width
        row = lax.broadcasted_iota(jnp.int32, (rows, width), 0)
        col = lax.broadcasted_iota(jnp.int32, (rows, width), 1)
        later_minus_earlier = (row - col) + (row_base - key_base)
        reach = jnp.where(is_retrieval == 1, jnp.int32(2**30), window)
        allowed = (later_minus_earlier >= 0) & (
            (later_minus_earlier < reach) | (col + key_base < sink)
        )
        update(allowed[None])


def block_table(row_base, row_count, key_offset, key_count, roles, sinks, windows):
    blocks = key_count // KEY_BLOCK
    first = key_offset + jnp.arange(blocks, dtype=jnp.int32) * KEY_BLOCK
    last_key = first + KEY_BLOCK - 1
    last_row = row_base + row_count - 1
    causal = first <= last_row
    reach = last_key[None, :] >= row_base - windows[:, None] + 1
    sunk = first[None, :] < sinks[:, None]
    retrieval = roles[:, None] == 1
    needed = causal[None, :] & (retrieval | reach | sunk)
    whole = (last_key <= row_base)[None, :] & (
        retrieval
        | (last_key[None, :] < sinks[:, None])
        | (last_row - first[None, :] < windows[:, None])
    )
    order = jnp.argsort(jnp.logical_not(needed), axis=1, stable=True).astype(jnp.int32)
    count = jnp.sum(needed, axis=1).astype(jnp.int32)
    last = jnp.take_along_axis(order, jnp.maximum(count - 1, 0)[:, None], axis=1)
    steps = jnp.arange(blocks, dtype=jnp.int32)[None, :]
    table = jnp.where(steps < count[:, None], order, last)
    full = jnp.take_along_axis(whole, table, axis=1).astype(jnp.int32)
    meta = jnp.stack(
        [
            count,
            roles,
            sinks,
            windows,
            jnp.broadcast_to(row_base, count.shape),
            jnp.broadcast_to(key_offset, count.shape),
        ],
        axis=1,
    ).astype(jnp.int32)
    meta = jnp.pad(meta, ((0, 0), (0, 2)))
    return jnp.concatenate([table, full], axis=1), meta


def attend(stacked, both, table, meta):
    local_heads, stack_rows, _ = stacked.shape
    blocks = table.shape[1] // 2
    return pl.pallas_call(
        attention_kernel,
        out_shape=(
            jax.ShapeDtypeStruct(stacked.shape, jnp.float32),
            jax.ShapeDtypeStruct((local_heads, stack_rows, 1), jnp.float32),
            jax.ShapeDtypeStruct((local_heads, stack_rows, 1), jnp.float32),
        ),
        grid_spec=pltpu.PrefetchScalarGridSpec(
            num_scalar_prefetch=2,
            grid=(local_heads, blocks),
            in_specs=[
                pl.BlockSpec((1, stack_rows, HD), lambda g, s, t, m: (g, 0, 0)),
                pl.BlockSpec((KEY_BLOCK, HD), lambda g, s, t, m: (t[g, s], g)),
                pl.BlockSpec((KEY_BLOCK, HD), lambda g, s, t, m: (t[g, s], local_heads + g)),
            ],
            out_specs=(
                pl.BlockSpec((1, stack_rows, HD), lambda g, s, t, m: (g, 0, 0)),
                pl.BlockSpec((1, stack_rows, 1), lambda g, s, t, m: (g, 0, 0)),
                pl.BlockSpec((1, stack_rows, 1), lambda g, s, t, m: (g, 0, 0)),
            ),
        ),
        compiler_params=pltpu.CompilerParams(
            dimension_semantics=("arbitrary", "arbitrary")
        ),
    )(table, meta, stacked, both, both)


def stack_heads(queries, local_heads):
    rows = queries.shape[0]
    return (
        queries.reshape(rows, local_heads, GROUP, HD)
        .transpose(1, 2, 0, 3)
        .reshape(local_heads, GROUP * rows, HD)
    )


def merge(own, other, row_count):
    acc_a, peak_a, total_a = own
    acc_b, peak_b, total_b = other
    peak = jnp.maximum(peak_a, peak_b)
    scale_a = jnp.exp(peak_a - peak)
    scale_b = jnp.exp(peak_b - peak)
    acc = acc_a * scale_a + acc_b * scale_b
    total = total_a * scale_a + total_b * scale_b
    local_heads = acc.shape[0]
    attended = (acc / total).astype(jnp.bfloat16)
    return (
        attended.reshape(local_heads, GROUP, row_count, HD)
        .transpose(2, 0, 1, 3)
        .reshape(row_count, local_heads * GROUP * HD)
    )


def gather_ring(block, axis):
    size = lax.axis_size(axis)
    here = lax.axis_index(axis)
    pieces = [block]
    for shift in range(1, size):
        pieces.append(
            lax.ppermute(block, axis, [(i, (i + shift) % size) for i in range(size)])
        )
    stacked = jnp.stack(pieces)
    order = (here - jnp.arange(size, dtype=jnp.int32)) % size
    return jnp.take(stacked, order, axis=0).reshape(size * block.shape[0], block.shape[1])


def scatter_sum(partial):
    rows, width = partial.shape
    quarter = rows // 4
    parts = partial.reshape(2, 2, quarter, width)
    core = lax.axis_index("core")
    keep = jnp.take(parts, core, axis=1)
    give = jnp.take(parts, 1 - core, axis=1)
    got = lax.ppermute(give.astype(jnp.bfloat16), "core", [(0, 1), (1, 0)])
    summed = keep + got.astype(jnp.float32)
    xl = lax.axis_index("xl")
    keep = jnp.take(summed, xl, axis=0)
    give = jnp.take(summed, 1 - xl, axis=0)
    got = lax.ppermute(give.astype(jnp.bfloat16), "xl", [(0, 1), (1, 0)])
    return (keep + got.astype(jnp.float32)).astype(jnp.bfloat16)


def per_device(queries, key_states, value_states, out_weight, head_role, sink_len, window_len):
    row_count = queries.shape[0]
    local_heads = key_states.shape[1] // HD
    half_size = lax.axis_size("z") * lax.axis_size("y")
    half = lax.axis_index("xh")
    place = lax.axis_index("z") * lax.axis_size("y") + lax.axis_index("y")
    ctx = half * half_size + place
    partner = (1 - half) * half_size + place
    head_index = lax.axis_index("xl") * lax.axis_size("core") + lax.axis_index("core")
    first_head = head_index * local_heads
    roles_here = lax.dynamic_slice_in_dim(head_role, first_head, local_heads)
    sinks_here = lax.dynamic_slice_in_dim(sink_len, first_head, local_heads)
    windows_here = lax.dynamic_slice_in_dim(window_len, first_head, local_heads)
    partner_queries = lax.ppermute(stack_heads(queries, local_heads), "xh", [(1, 0)])
    both = jnp.concatenate([key_states, value_states], axis=1)
    both = gather_ring(both, "y")
    both = lax.all_gather(both, "z", axis=0, tiled=True)
    key_offset = half * both.shape[0]
    table, meta = block_table(
        partner * row_count, row_count, key_offset, both.shape[0],
        roles_here, sinks_here, windows_here,
    )
    acc_p, peak_p, total_p = attend(partner_queries, both, table, meta)
    stats_p = jnp.concatenate(
        [peak_p.reshape(local_heads, -1), total_p.reshape(local_heads, -1)], axis=0
    )
    acc_p = lax.ppermute(acc_p.astype(jnp.bfloat16), "xh", [(0, 1)])
    stats_p = lax.ppermute(stats_p, "xh", [(0, 1)])
    table, meta = block_table(
        ctx * row_count, row_count, key_offset, both.shape[0],
        roles_here, sinks_here, windows_here,
    )
    own = attend(stack_heads(queries, local_heads), both, table, meta)
    received = half == 1
    peak_b = jnp.where(received, stats_p[:local_heads], NEGATIVE)[:, :, None]
    total_b = jnp.where(received, stats_p[local_heads:], 0.0)[:, :, None]
    acc_b = jnp.where(received, acc_p.astype(jnp.float32), 0.0)
    attended = merge(own, (acc_b, peak_b, total_b), row_count)
    partial = jnp.dot(attended, out_weight, preferred_element_type=jnp.float32)
    return scatter_sum(partial)


def solution(mesh):
    ctx_size = mesh.shape["ctx"]
    y_size = 4
    devices = mesh.devices.reshape(2, ctx_size // (2 * y_size), y_size, 2, mesh.shape["head"] // 2)
    split = jax.sharding.Mesh(devices, ("xh", "z", "y", "xl", "core"))
    tokens = ("xh", "z", "y")
    heads = ("xl", "core")
    in_specs = (
        P(tokens, heads),
        P(tokens, heads),
        P(tokens, heads),
        P(heads, None),
        P(),
        P(),
        P(),
    )
    out_specs = P(("xh", "z", "y", "xl", "core"), None)
    return jax.shard_map(
        per_device, mesh=split, in_specs=in_specs, out_specs=out_specs, check_vma=False
    )
```

```python
import functools

import jax
import jax.numpy as jnp
from jax import lax
from jax.experimental import pallas as pl
from jax.experimental.pallas import tpu as pltpu
from jax.sharding import PartitionSpec as P

HD = 128
GROUP = 4
KEY_BLOCK = 1024

NEGATIVE = -1e30


def attention_kernel(table_ref, meta_ref, q_ref, k_ref, v_ref, acc_ref, peak_ref, total_ref):
    g = pl.program_id(0)
    step = pl.program_id(1)
    blocks = pl.num_programs(1)
    count = meta_ref[g, 0]
    is_retrieval = meta_ref[g, 1]
    sink = meta_ref[g, 2]
    window = meta_ref[g, 3]
    row_base = meta_ref[g, 4]
    key_offset = meta_ref[g, 5]
    rows = q_ref.shape[1] // GROUP
    width = k_ref.shape[0]

    @pl.when(step == 0)
    def _():
        peak_ref[...] = jnp.full_like(peak_ref, NEGATIVE)
        total_ref[...] = jnp.zeros_like(total_ref)
        acc_ref[...] = jnp.zeros_like(acc_ref)

    def update(allowed):
        scores = lax.dot_general(
            q_ref[0], k_ref[...], (((1,), (1,)), ((), ())), preferred_element_type=jnp.float32
        ) * HD ** (-0.5)
        old_peak = peak_ref[0]
        if allowed is None:
            block_peak = jnp.max(scores, axis=-1, keepdims=True)
            new_peak = jnp.maximum(old_peak, block_peak)
            weights = jnp.exp(scores - new_peak)
        else:
            scores = scores.reshape(GROUP, rows, width)
            block_peak = jnp.max(
                jnp.where(allowed, scores, NEGATIVE), axis=-1, keepdims=True
            ).reshape(GROUP * rows, 1)
            new_peak = jnp.maximum(old_peak, block_peak)
            weights = jnp.where(
                allowed, jnp.exp(scores - new_peak.reshape(GROUP, rows, 1)), 0.0
            ).reshape(GROUP * rows, width)
        rescale = jnp.exp(old_peak - new_peak)
        total_ref[0] = rescale * total_ref[0] + jnp.sum(weights, axis=-1, keepdims=True)
        acc_ref[0] = rescale * acc_ref[0] + jnp.dot(
            weights.astype(jnp.bfloat16), v_ref[...], preferred_element_type=jnp.float32
        )
        peak_ref[0] = new_peak

    full = table_ref[g, blocks + step]

    @pl.when((step < count) & (full == 1))
    def _():
        update(None)

    @pl.when((step < count) & (full == 0))
    def _():
        block = table_ref[g, step]
        key_base = key_offset + block * width
        row = lax.broadcasted_iota(jnp.int32, (rows, width), 0)
        col = lax.broadcasted_iota(jnp.int32, (rows, width), 1)
        later_minus_earlier = (row - col) + (row_base - key_base)
        reach = jnp.where(is_retrieval == 1, jnp.int32(2**30), window)
        allowed = (later_minus_earlier >= 0) & (
            (later_minus_earlier < reach) | (col + key_base < sink)
        )
        update(allowed[None])


def block_table(row_base, row_count, key_offset, key_count, roles, sinks, windows):
    blocks = key_count // KEY_BLOCK
    first = key_offset + jnp.arange(blocks, dtype=jnp.int32) * KEY_BLOCK
    last_key = first + KEY_BLOCK - 1
    last_row = row_base + row_count - 1
    causal = first <= last_row
    reach = last_key[None, :] >= row_base - windows[:, None] + 1
    sunk = first[None, :] < sinks[:, None]
    retrieval = roles[:, None] == 1
    needed = causal[None, :] & (retrieval | reach | sunk)
    whole = (last_key <= row_base)[None, :] & (
        retrieval
        | (last_key[None, :] < sinks[:, None])
        | (last_row - first[None, :] < windows[:, None])
    )
    order = jnp.argsort(jnp.logical_not(needed), axis=1, stable=True).astype(jnp.int32)
    count = jnp.sum(needed, axis=1).astype(jnp.int32)
    last = jnp.take_along_axis(order, jnp.maximum(count - 1, 0)[:, None], axis=1)
    steps = jnp.arange(blocks, dtype=jnp.int32)[None, :]
    table = jnp.where(steps < count[:, None], order, last)
    full = jnp.take_along_axis(whole, table, axis=1).astype(jnp.int32)
    meta = jnp.stack(
        [
            count,
            roles,
            sinks,
            windows,
            jnp.broadcast_to(row_base, count.shape),
            jnp.broadcast_to(key_offset, count.shape),
        ],
        axis=1,
    ).astype(jnp.int32)
    meta = jnp.pad(meta, ((0, 0), (0, 2)))
    return jnp.concatenate([table, full], axis=1), meta


def attend(stacked, both, table, meta):
    local_heads, stack_rows, _ = stacked.shape
    blocks = table.shape[1] // 2
    return pl.pallas_call(
        attention_kernel,
        out_shape=(
            jax.ShapeDtypeStruct(stacked.shape, jnp.float32),
            jax.ShapeDtypeStruct((local_heads, stack_rows, 1), jnp.float32),
            jax.ShapeDtypeStruct((local_heads, stack_rows, 1), jnp.float32),
        ),
        grid_spec=pltpu.PrefetchScalarGridSpec(
            num_scalar_prefetch=2,
            grid=(local_heads, blocks),
            in_specs=[
                pl.BlockSpec((1, stack_rows, HD), lambda g, s, t, m: (g, 0, 0)),
                pl.BlockSpec((KEY_BLOCK, HD), lambda g, s, t, m: (t[g, s], g)),
                pl.BlockSpec((KEY_BLOCK, HD), lambda g, s, t, m: (t[g, s], local_heads + g)),
            ],
            out_specs=(
                pl.BlockSpec((1, stack_rows, HD), lambda g, s, t, m: (g, 0, 0)),
                pl.BlockSpec((1, stack_rows, 1), lambda g, s, t, m: (g, 0, 0)),
                pl.BlockSpec((1, stack_rows, 1), lambda g, s, t, m: (g, 0, 0)),
            ),
        ),
        compiler_params=pltpu.CompilerParams(
            dimension_semantics=("arbitrary", "arbitrary")
        ),
    )(table, meta, stacked, both, both)


def stack_heads(queries, local_heads):
    rows = queries.shape[0]
    return (
        queries.reshape(rows, local_heads, GROUP, HD)
        .transpose(1, 2, 0, 3)
        .reshape(local_heads, GROUP * rows, HD)
    )


def merge(own, other, row_count):
    acc_a, peak_a, total_a = own
    acc_b, peak_b, total_b = other
    peak = jnp.maximum(peak_a, peak_b)
    scale_a = jnp.exp(peak_a - peak)
    scale_b = jnp.exp(peak_b - peak)
    acc = acc_a * scale_a + acc_b * scale_b
    total = total_a * scale_a + total_b * scale_b
    local_heads = acc.shape[0]
    attended = (acc / total).astype(jnp.bfloat16)
    return (
        attended.reshape(local_heads, GROUP, row_count, HD)
        .transpose(2, 0, 1, 3)
        .reshape(row_count, local_heads * GROUP * HD)
    )


def gather_ring(block, axis):
    size = lax.axis_size(axis)
    here = lax.axis_index(axis)
    pieces = [block]
    for shift in range(1, size):
        pieces.append(
            lax.ppermute(block, axis, [(i, (i + shift) % size) for i in range(size)])
        )
    stacked = jnp.stack(pieces)
    order = (here - jnp.arange(size, dtype=jnp.int32)) % size
    return jnp.take(stacked, order, axis=0).reshape(size * block.shape[0], block.shape[1])


def scatter_sum(partial):
    rows, width = partial.shape
    quarter = rows // 4
    parts = partial.reshape(2, 2, quarter, width)
    core = lax.axis_index("core")
    keep = jnp.take(parts, core, axis=1)
    give = jnp.take(parts, 1 - core, axis=1)
    got = lax.ppermute(give.astype(jnp.bfloat16), "core", [(0, 1), (1, 0)])
    summed = keep + got.astype(jnp.float32)
    xl = lax.axis_index("xl")
    keep = jnp.take(summed, xl, axis=0)
    give = jnp.take(summed, 1 - xl, axis=0)
    got = lax.ppermute(give.astype(jnp.bfloat16), "xl", [(0, 1), (1, 0)])
    return (keep + got.astype(jnp.float32)).astype(jnp.bfloat16)


def per_device(queries, key_states, value_states, out_weight, head_role, sink_len, window_len):
    row_count = queries.shape[0]
    local_heads = key_states.shape[1] // HD
    half_size = lax.axis_size("z") * lax.axis_size("y")
    half = lax.axis_index("xh")
    place = lax.axis_index("z") * lax.axis_size("y") + lax.axis_index("y")
    ctx = half * half_size + place
    partner = (1 - half) * half_size + place
    head_index = lax.axis_index("xl") * lax.axis_size("core") + lax.axis_index("core")
    first_head = head_index * local_heads
    roles_here = lax.dynamic_slice_in_dim(head_role, first_head, local_heads)
    sinks_here = lax.dynamic_slice_in_dim(sink_len, first_head, local_heads)
    windows_here = lax.dynamic_slice_in_dim(window_len, first_head, local_heads)
    partner_queries = lax.ppermute(stack_heads(queries, local_heads), "xh", [(1, 0)])
    both = jnp.concatenate([key_states, value_states], axis=1)
    both = gather_ring(both, "y")
    per_head = [
        lax.all_gather(
            jnp.concatenate(
                [both[:, g * HD:(g + 1) * HD], both[:, (local_heads + g) * HD:(local_heads + g + 1) * HD]],
                axis=1,
            ),
            "z",
            axis=0,
            tiled=True,
        )
        for g in range(local_heads)
    ]
    key_count = per_head[0].shape[0]
    key_offset = half * key_count
    table_p, meta_p = block_table(
        partner * row_count, row_count, key_offset, key_count,
        roles_here, sinks_here, windows_here,
    )
    table_o, meta_o = block_table(
        ctx * row_count, row_count, key_offset, key_count,
        roles_here, sinks_here, windows_here,
    )
    own_queries = stack_heads(queries, local_heads)
    for_partner = []
    own_parts = []
    for g in range(local_heads):
        one = slice(g, g + 1)
        for_partner.append(attend(partner_queries[one], per_head[g], table_p[one], meta_p[one]))
        own_parts.append(attend(own_queries[one], per_head[g], table_o[one], meta_o[one]))
    acc_p, peak_p, total_p = (jnp.concatenate(x, axis=0) for x in zip(*for_partner))
    own = tuple(jnp.concatenate(x, axis=0) for x in zip(*own_parts))
    stats_p = jnp.concatenate(
        [peak_p.reshape(local_heads, -1), total_p.reshape(local_heads, -1)], axis=0
    )
    acc_p = lax.ppermute(acc_p.astype(jnp.bfloat16), "xh", [(0, 1)])
    stats_p = lax.ppermute(stats_p, "xh", [(0, 1)])
    received = half == 1
    peak_b = jnp.where(received, stats_p[:local_heads], NEGATIVE)[:, :, None]
    total_b = jnp.where(received, stats_p[local_heads:], 0.0)[:, :, None]
    acc_b = jnp.where(received, acc_p.astype(jnp.float32), 0.0)
    attended = merge(own, (acc_b, peak_b, total_b), row_count)
    partial = jnp.dot(attended, out_weight, preferred_element_type=jnp.float32)
    return scatter_sum(partial)


def solution(mesh):
    ctx_size = mesh.shape["ctx"]
    y_size = 4
    devices = mesh.devices.reshape(2, ctx_size // (2 * y_size), y_size, 2, mesh.shape["head"] // 2)
    split = jax.sharding.Mesh(devices, ("xh", "z", "y", "xl", "core"))
    tokens = ("xh", "z", "y")
    heads = ("xl", "core")
    in_specs = (
        P(tokens, heads),
        P(tokens, heads),
        P(tokens, heads),
        P(heads, None),
        P(),
        P(),
        P(),
    )
    out_specs = P(("xh", "z", "y", "xl", "core"), None)
    return jax.shard_map(
        per_device, mesh=split, in_specs=in_specs, out_specs=out_specs, check_vma=False
    )
```

```python
import functools

import jax
import jax.numpy as jnp
from jax import lax
from jax.experimental import pallas as pl
from jax.experimental.pallas import tpu as pltpu
from jax.sharding import PartitionSpec as P

HD = 128
GROUP = 4
KEY_BLOCK = 2048

NEGATIVE = -1e30


def attention_kernel(table_ref, meta_ref, q_ref, k_ref, v_ref, acc_ref, peak_ref, total_ref):
    g = pl.program_id(0)
    step = pl.program_id(1)
    blocks = pl.num_programs(1)
    count = meta_ref[g, 0]
    is_retrieval = meta_ref[g, 1]
    sink = meta_ref[g, 2]
    window = meta_ref[g, 3]
    row_base = meta_ref[g, 4]
    key_offset = meta_ref[g, 5]
    rows = q_ref.shape[1] // GROUP
    width = k_ref.shape[0]

    @pl.when(step == 0)
    def _():
        peak_ref[...] = jnp.full_like(peak_ref, NEGATIVE)
        total_ref[...] = jnp.zeros_like(total_ref)
        acc_ref[...] = jnp.zeros_like(acc_ref)

    def update(allowed):
        scores = lax.dot_general(
            q_ref[0], k_ref[...], (((1,), (1,)), ((), ())), preferred_element_type=jnp.float32
        ) * HD ** (-0.5)
        old_peak = peak_ref[0]
        if allowed is None:
            block_peak = jnp.max(scores, axis=-1, keepdims=True)
            new_peak = jnp.maximum(old_peak, block_peak)
            weights = jnp.exp(scores - new_peak)
        else:
            scores = scores.reshape(GROUP, rows, width)
            block_peak = jnp.max(
                jnp.where(allowed, scores, NEGATIVE), axis=-1, keepdims=True
            ).reshape(GROUP * rows, 1)
            new_peak = jnp.maximum(old_peak, block_peak)
            weights = jnp.where(
                allowed, jnp.exp(scores - new_peak.reshape(GROUP, rows, 1)), 0.0
            ).reshape(GROUP * rows, width)
        rescale = jnp.exp(old_peak - new_peak)
        total_ref[0] = rescale * total_ref[0] + jnp.sum(weights, axis=-1, keepdims=True)
        acc_ref[0] = rescale * acc_ref[0] + jnp.dot(
            weights.astype(jnp.bfloat16), v_ref[...], preferred_element_type=jnp.float32
        )
        peak_ref[0] = new_peak

    full = table_ref[g, blocks + step]

    @pl.when((step < count) & (full == 1))
    def _():
        update(None)

    @pl.when((step < count) & (full == 0))
    def _():
        block = table_ref[g, step]
        key_base = key_offset + block * width
        row = lax.broadcasted_iota(jnp.int32, (rows, width), 0)
        col = lax.broadcasted_iota(jnp.int32, (rows, width), 1)
        later_minus_earlier = (row - col) + (row_base - key_base)
        reach = jnp.where(is_retrieval == 1, jnp.int32(2**30), window)
        allowed = (later_minus_earlier >= 0) & (
            (later_minus_earlier < reach) | (col + key_base < sink)
        )
        update(allowed[None])


def block_table(row_base, row_count, key_offset, key_count, roles, sinks, windows):
    blocks = key_count // KEY_BLOCK
    first = key_offset + jnp.arange(blocks, dtype=jnp.int32) * KEY_BLOCK
    last_key = first + KEY_BLOCK - 1
    last_row = row_base + row_count - 1
    causal = first <= last_row
    reach = last_key[None, :] >= row_base - windows[:, None] + 1
    sunk = first[None, :] < sinks[:, None]
    retrieval = roles[:, None] == 1
    needed = causal[None, :] & (retrieval | reach | sunk)
    whole = (last_key <= row_base)[None, :] & (
        retrieval
        | (last_key[None, :] < sinks[:, None])
        | (last_row - first[None, :] < windows[:, None])
    )
    order = jnp.argsort(jnp.logical_not(needed), axis=1, stable=True).astype(jnp.int32)
    count = jnp.sum(needed, axis=1).astype(jnp.int32)
    last = jnp.take_along_axis(order, jnp.maximum(count - 1, 0)[:, None], axis=1)
    steps = jnp.arange(blocks, dtype=jnp.int32)[None, :]
    table = jnp.where(steps < count[:, None], order, last)
    full = jnp.take_along_axis(whole, table, axis=1).astype(jnp.int32)
    meta = jnp.stack(
        [
            count,
            roles,
            sinks,
            windows,
            jnp.broadcast_to(row_base, count.shape),
            jnp.broadcast_to(key_offset, count.shape),
        ],
        axis=1,
    ).astype(jnp.int32)
    meta = jnp.pad(meta, ((0, 0), (0, 2)))
    return jnp.concatenate([table, full], axis=1), meta


def attend(stacked, both, table, meta):
    local_heads, stack_rows, _ = stacked.shape
    blocks = table.shape[1] // 2
    return pl.pallas_call(
        attention_kernel,
        out_shape=(
            jax.ShapeDtypeStruct(stacked.shape, jnp.float32),
            jax.ShapeDtypeStruct((local_heads, stack_rows, 1), jnp.float32),
            jax.ShapeDtypeStruct((local_heads, stack_rows, 1), jnp.float32),
        ),
        grid_spec=pltpu.PrefetchScalarGridSpec(
            num_scalar_prefetch=2,
            grid=(local_heads, blocks),
            in_specs=[
                pl.BlockSpec((1, stack_rows, HD), lambda g, s, t, m: (g, 0, 0)),
                pl.BlockSpec((KEY_BLOCK, HD), lambda g, s, t, m: (t[g, s], g)),
                pl.BlockSpec((KEY_BLOCK, HD), lambda g, s, t, m: (t[g, s], local_heads + g)),
            ],
            out_specs=(
                pl.BlockSpec((1, stack_rows, HD), lambda g, s, t, m: (g, 0, 0)),
                pl.BlockSpec((1, stack_rows, 1), lambda g, s, t, m: (g, 0, 0)),
                pl.BlockSpec((1, stack_rows, 1), lambda g, s, t, m: (g, 0, 0)),
            ),
        ),
        compiler_params=pltpu.CompilerParams(
            dimension_semantics=("arbitrary", "arbitrary")
        ),
    )(table, meta, stacked, both, both)


def stack_heads(queries, local_heads):
    rows = queries.shape[0]
    return (
        queries.reshape(rows, local_heads, GROUP, HD)
        .transpose(1, 2, 0, 3)
        .reshape(local_heads, GROUP * rows, HD)
    )


def merge(own, other, row_count):
    acc_a, peak_a, total_a = own
    acc_b, peak_b, total_b = other
    peak = jnp.maximum(peak_a, peak_b)
    scale_a = jnp.exp(peak_a - peak)
    scale_b = jnp.exp(peak_b - peak)
    acc = acc_a * scale_a + acc_b * scale_b
    total = total_a * scale_a + total_b * scale_b
    local_heads = acc.shape[0]
    attended = (acc / total).astype(jnp.bfloat16)
    return (
        attended.reshape(local_heads, GROUP, row_count, HD)
        .transpose(2, 0, 1, 3)
        .reshape(row_count, local_heads * GROUP * HD)
    )


def gather_ring(block, axis):
    size = lax.axis_size(axis)
    here = lax.axis_index(axis)
    pieces = [block]
    for shift in range(1, size):
        pieces.append(
            lax.ppermute(block, axis, [(i, (i + shift) % size) for i in range(size)])
        )
    stacked = jnp.stack(pieces)
    order = (here - jnp.arange(size, dtype=jnp.int32)) % size
    return jnp.take(stacked, order, axis=0).reshape(size * block.shape[0], block.shape[1])


def scatter_sum(partial):
    rows, width = partial.shape
    quarter = rows // 4
    parts = partial.reshape(2, 2, quarter, width)
    core = lax.axis_index("core")
    keep = jnp.take(parts, core, axis=1)
    give = jnp.take(parts, 1 - core, axis=1)
    got = lax.ppermute(give.astype(jnp.bfloat16), "core", [(0, 1), (1, 0)])
    summed = keep + got.astype(jnp.float32)
    xl = lax.axis_index("xl")
    keep = jnp.take(summed, xl, axis=0)
    give = jnp.take(summed, 1 - xl, axis=0)
    got = lax.ppermute(give.astype(jnp.bfloat16), "xl", [(0, 1), (1, 0)])
    return (keep + got.astype(jnp.float32)).astype(jnp.bfloat16)


def per_device(queries, key_states, value_states, out_weight, head_role, sink_len, window_len):
    row_count = queries.shape[0]
    local_heads = key_states.shape[1] // HD
    half_size = lax.axis_size("z") * lax.axis_size("y")
    half = lax.axis_index("xh")
    place = lax.axis_index("z") * lax.axis_size("y") + lax.axis_index("y")
    ctx = half * half_size + place
    partner = (1 - half) * half_size + place
    head_index = lax.axis_index("xl") * lax.axis_size("core") + lax.axis_index("core")
    first_head = head_index * local_heads
    roles_here = lax.dynamic_slice_in_dim(head_role, first_head, local_heads)
    sinks_here = lax.dynamic_slice_in_dim(sink_len, first_head, local_heads)
    windows_here = lax.dynamic_slice_in_dim(window_len, first_head, local_heads)
    partner_queries = lax.ppermute(stack_heads(queries, local_heads), "xh", [(1, 0)])
    both = jnp.concatenate([key_states, value_states], axis=1)
    both = gather_ring(both, "y")
    both = lax.all_gather(both, "z", axis=0, tiled=True)
    key_offset = half * both.shape[0]
    table, meta = block_table(
        partner * row_count, row_count, key_offset, both.shape[0],
        roles_here, sinks_here, windows_here,
    )
    acc_p, peak_p, total_p = attend(partner_queries, both, table, meta)
    stats_p = jnp.concatenate(
        [peak_p.reshape(local_heads, -1), total_p.reshape(local_heads, -1)], axis=0
    )
    acc_p = lax.ppermute(acc_p.astype(jnp.bfloat16), "xh", [(0, 1)])
    stats_p = lax.ppermute(stats_p, "xh", [(0, 1)])
    table, meta = block_table(
        ctx * row_count, row_count, key_offset, both.shape[0],
        roles_here, sinks_here, windows_here,
    )
    own = attend(stack_heads(queries, local_heads), both, table, meta)
    received = half == 1
    peak_b = jnp.where(received, stats_p[:local_heads], NEGATIVE)[:, :, None]
    total_b = jnp.where(received, stats_p[local_heads:], 0.0)[:, :, None]
    acc_b = jnp.where(received, acc_p.astype(jnp.float32), 0.0)
    attended = merge(own, (acc_b, peak_b, total_b), row_count)
    partial = jnp.dot(attended, out_weight, preferred_element_type=jnp.float32)
    return scatter_sum(partial)


def solution(mesh):
    ctx_size = mesh.shape["ctx"]
    y_size = 4
    devices = mesh.devices.reshape(2, ctx_size // (2 * y_size), y_size, 2, mesh.shape["head"] // 2)
    split = jax.sharding.Mesh(devices, ("xh", "z", "y", "xl", "core"))
    tokens = ("xh", "z", "y")
    heads = ("xl", "core")
    in_specs = (
        P(tokens, heads),
        P(tokens, heads),
        P(tokens, heads),
        P(heads, None),
        P(),
        P(),
        P(),
    )
    out_specs = P(("xh", "z", "y", "xl", "core"), None)
    return jax.shard_map(
        per_device, mesh=split, in_specs=in_specs, out_specs=out_specs, check_vma=False
    )
```

```python
import functools

import jax
import jax.numpy as jnp
from jax import lax
from jax.experimental import pallas as pl
from jax.experimental.pallas import tpu as pltpu
from jax.sharding import PartitionSpec as P

HD = 128
GROUP = 4
KEY_BLOCK = 2048

NEGATIVE = -1e30


def attention_kernel(table_ref, meta_ref, q_ref, k_ref, v_ref, acc_ref, peak_ref, total_ref):
    g = pl.program_id(0)
    step = pl.program_id(1)
    blocks = pl.num_programs(1)
    count = meta_ref[g, 0]
    is_retrieval = meta_ref[g, 1]
    sink = meta_ref[g, 2]
    window = meta_ref[g, 3]
    row_base = meta_ref[g, 4]
    key_offset = meta_ref[g, 5]
    rows = q_ref.shape[1] // GROUP
    width = k_ref.shape[0]

    @pl.when(step == 0)
    def _():
        peak_ref[...] = jnp.full_like(peak_ref, NEGATIVE)
        total_ref[...] = jnp.zeros_like(total_ref)
        acc_ref[...] = jnp.zeros_like(acc_ref)

    def update(allowed):
        scores = lax.dot_general(
            q_ref[0], k_ref[...], (((1,), (1,)), ((), ())), preferred_element_type=jnp.float32
        ) * HD ** (-0.5)
        old_peak = peak_ref[0]
        if allowed is None:
            block_peak = jnp.max(scores, axis=-1, keepdims=True)
            new_peak = jnp.maximum(old_peak, block_peak)
            weights = jnp.exp(scores - new_peak)
        else:
            scores = scores.reshape(GROUP, rows, width)
            block_peak = jnp.max(
                jnp.where(allowed, scores, NEGATIVE), axis=-1, keepdims=True
            ).reshape(GROUP * rows, 1)
            new_peak = jnp.maximum(old_peak, block_peak)
            weights = jnp.where(
                allowed, jnp.exp(scores - new_peak.reshape(GROUP, rows, 1)), 0.0
            ).reshape(GROUP * rows, width)
        rescale = jnp.exp(old_peak - new_peak)
        total_ref[0] = rescale * total_ref[0] + jnp.sum(weights, axis=-1, keepdims=True)
        acc_ref[0] = rescale * acc_ref[0] + jnp.dot(
            weights.astype(jnp.bfloat16), v_ref[...], preferred_element_type=jnp.float32
        )
        peak_ref[0] = new_peak

    full = table_ref[g, blocks + step]

    @pl.when((step < count) & (full == 1))
    def _():
        update(None)

    @pl.when((step < count) & (full == 0))
    def _():
        block = table_ref[g, step]
        key_base = key_offset + block * width
        row = lax.broadcasted_iota(jnp.int32, (rows, width), 0)
        col = lax.broadcasted_iota(jnp.int32, (rows, width), 1)
        later_minus_earlier = (row - col) + (row_base - key_base)
        reach = jnp.where(is_retrieval == 1, jnp.int32(2**30), window)
        allowed = (later_minus_earlier >= 0) & (
            (later_minus_earlier < reach) | (col + key_base < sink)
        )
        update(allowed[None])


def block_table(row_base, row_count, key_offset, key_count, roles, sinks, windows):
    blocks = key_count // KEY_BLOCK
    first = key_offset + jnp.arange(blocks, dtype=jnp.int32) * KEY_BLOCK
    last_key = first + KEY_BLOCK - 1
    last_row = row_base + row_count - 1
    causal = first <= last_row
    reach = last_key[None, :] >= row_base - windows[:, None] + 1
    sunk = first[None, :] < sinks[:, None]
    retrieval = roles[:, None] == 1
    needed = causal[None, :] & (retrieval | reach | sunk)
    whole = (last_key <= row_base)[None, :] & (
        retrieval
        | (last_key[None, :] < sinks[:, None])
        | (last_row - first[None, :] < windows[:, None])
    )
    order = jnp.argsort(jnp.logical_not(needed), axis=1, stable=True).astype(jnp.int32)
    count = jnp.sum(needed, axis=1).astype(jnp.int32)
    last = jnp.take_along_axis(order, jnp.maximum(count - 1, 0)[:, None], axis=1)
    steps = jnp.arange(blocks, dtype=jnp.int32)[None, :]
    table = jnp.where(steps < count[:, None], order, last)
    full = jnp.take_along_axis(whole, table, axis=1).astype(jnp.int32)
    meta = jnp.stack(
        [
            count,
            roles,
            sinks,
            windows,
            jnp.broadcast_to(row_base, count.shape),
            jnp.broadcast_to(key_offset, count.shape),
        ],
        axis=1,
    ).astype(jnp.int32)
    meta = jnp.pad(meta, ((0, 0), (0, 2)))
    return jnp.concatenate([table, full], axis=1), meta


def attend(stacked, both, table, meta):
    local_heads, stack_rows, _ = stacked.shape
    blocks = table.shape[1] // 2
    return pl.pallas_call(
        attention_kernel,
        out_shape=(
            jax.ShapeDtypeStruct(stacked.shape, jnp.float32),
            jax.ShapeDtypeStruct((local_heads, stack_rows, 1), jnp.float32),
            jax.ShapeDtypeStruct((local_heads, stack_rows, 1), jnp.float32),
        ),
        grid_spec=pltpu.PrefetchScalarGridSpec(
            num_scalar_prefetch=2,
            grid=(local_heads, blocks),
            in_specs=[
                pl.BlockSpec((1, stack_rows, HD), lambda g, s, t, m: (g, 0, 0)),
                pl.BlockSpec((KEY_BLOCK, HD), lambda g, s, t, m: (t[g, s], g)),
                pl.BlockSpec((KEY_BLOCK, HD), lambda g, s, t, m: (t[g, s], local_heads + g)),
            ],
            out_specs=(
                pl.BlockSpec((1, stack_rows, HD), lambda g, s, t, m: (g, 0, 0)),
                pl.BlockSpec((1, stack_rows, 1), lambda g, s, t, m: (g, 0, 0)),
                pl.BlockSpec((1, stack_rows, 1), lambda g, s, t, m: (g, 0, 0)),
            ),
        ),
        compiler_params=pltpu.CompilerParams(
            dimension_semantics=("arbitrary", "arbitrary")
        ),
    )(table, meta, stacked, both, both)


def stack_heads(queries, local_heads):
    rows = queries.shape[0]
    return (
        queries.reshape(rows, local_heads, GROUP, HD)
        .transpose(1, 2, 0, 3)
        .reshape(local_heads, GROUP * rows, HD)
    )


def merge(own, other, row_count):
    acc_a, peak_a, total_a = own
    acc_b, peak_b, total_b = other
    peak = jnp.maximum(peak_a, peak_b)
    scale_a = jnp.exp(peak_a - peak)
    scale_b = jnp.exp(peak_b - peak)
    acc = acc_a * scale_a + acc_b * scale_b
    total = total_a * scale_a + total_b * scale_b
    local_heads = acc.shape[0]
    attended = (acc / total).astype(jnp.bfloat16)
    return (
        attended.reshape(local_heads, GROUP, row_count, HD)
        .transpose(2, 0, 1, 3)
        .reshape(row_count, local_heads * GROUP * HD)
    )


def gather_ring(block, axis):
    size = lax.axis_size(axis)
    here = lax.axis_index(axis)
    pieces = [block]
    for shift in range(1, size):
        pieces.append(
            lax.ppermute(block, axis, [(i, (i + shift) % size) for i in range(size)])
        )
    stacked = jnp.stack(pieces)
    order = (here - jnp.arange(size, dtype=jnp.int32)) % size
    return jnp.take(stacked, order, axis=0).reshape(size * block.shape[0], block.shape[1])


def gather_both_ways(block, axis):
    size = lax.axis_size(axis)
    here = lax.axis_index(axis)
    right = [(i, (i + 1) % size) for i in range(size)]
    left = [(i, (i - 1) % size) for i in range(size)]
    pieces = [None] * size
    pieces[0] = block
    forward = block
    backward = block
    for step in range(1, size // 2 + 1):
        forward = lax.ppermute(forward, axis, right)
        pieces[size - step] = forward
        if step < size - size // 2:
            backward = lax.ppermute(backward, axis, left)
            pieces[step] = backward
    stacked = jnp.stack(pieces)
    order = (jnp.arange(size, dtype=jnp.int32) - here) % size
    return jnp.take(stacked, order, axis=0).reshape(size * block.shape[0], block.shape[1])


def scatter_sum(partial):
    rows, width = partial.shape
    quarter = rows // 4
    parts = partial.reshape(2, 2, quarter, width)
    core = lax.axis_index("core")
    keep = jnp.take(parts, core, axis=1)
    give = jnp.take(parts, 1 - core, axis=1)
    got = lax.ppermute(give.astype(jnp.bfloat16), "core", [(0, 1), (1, 0)])
    summed = keep + got.astype(jnp.float32)
    xl = lax.axis_index("xl")
    keep = jnp.take(summed, xl, axis=0)
    give = jnp.take(summed, 1 - xl, axis=0)
    got = lax.ppermute(give.astype(jnp.bfloat16), "xl", [(0, 1), (1, 0)])
    return (keep + got.astype(jnp.float32)).astype(jnp.bfloat16)


def per_device(queries, key_states, value_states, out_weight, head_role, sink_len, window_len):
    row_count = queries.shape[0]
    local_heads = key_states.shape[1] // HD
    half_size = lax.axis_size("z") * lax.axis_size("y")
    half = lax.axis_index("xh")
    place = lax.axis_index("z") * lax.axis_size("y") + lax.axis_index("y")
    ctx = half * half_size + place
    partner = (1 - half) * half_size + place
    head_index = lax.axis_index("xl") * lax.axis_size("core") + lax.axis_index("core")
    first_head = head_index * local_heads
    roles_here = lax.dynamic_slice_in_dim(head_role, first_head, local_heads)
    sinks_here = lax.dynamic_slice_in_dim(sink_len, first_head, local_heads)
    windows_here = lax.dynamic_slice_in_dim(window_len, first_head, local_heads)
    partner_queries = lax.ppermute(stack_heads(queries, local_heads), "xh", [(1, 0)])
    both = jnp.concatenate([key_states, value_states], axis=1)
    both = gather_ring(both, "y")
    both = gather_both_ways(both, "z")
    key_offset = half * both.shape[0]
    table, meta = block_table(
        partner * row_count, row_count, key_offset, both.shape[0],
        roles_here, sinks_here, windows_here,
    )
    acc_p, peak_p, total_p = attend(partner_queries, both, table, meta)
    stats_p = jnp.concatenate(
        [peak_p.reshape(local_heads, -1), total_p.reshape(local_heads, -1)], axis=0
    )
    acc_p = lax.ppermute(acc_p.astype(jnp.bfloat16), "xh", [(0, 1)])
    stats_p = lax.ppermute(stats_p, "xh", [(0, 1)])
    table, meta = block_table(
        ctx * row_count, row_count, key_offset, both.shape[0],
        roles_here, sinks_here, windows_here,
    )
    own = attend(stack_heads(queries, local_heads), both, table, meta)
    received = half == 1
    peak_b = jnp.where(received, stats_p[:local_heads], NEGATIVE)[:, :, None]
    total_b = jnp.where(received, stats_p[local_heads:], 0.0)[:, :, None]
    acc_b = jnp.where(received, acc_p.astype(jnp.float32), 0.0)
    attended = merge(own, (acc_b, peak_b, total_b), row_count)
    partial = jnp.dot(attended, out_weight, preferred_element_type=jnp.float32)
    return scatter_sum(partial)


def solution(mesh):
    ctx_size = mesh.shape["ctx"]
    y_size = 4
    devices = mesh.devices.reshape(2, ctx_size // (2 * y_size), y_size, 2, mesh.shape["head"] // 2)
    split = jax.sharding.Mesh(devices, ("xh", "z", "y", "xl", "core"))
    tokens = ("xh", "z", "y")
    heads = ("xl", "core")
    in_specs = (
        P(tokens, heads),
        P(tokens, heads),
        P(tokens, heads),
        P(heads, None),
        P(),
        P(),
        P(),
    )
    out_specs = P(("xh", "z", "y", "xl", "core"), None)
    return jax.shard_map(
        per_device, mesh=split, in_specs=in_specs, out_specs=out_specs, check_vma=False
    )
```

```python
import functools

import jax
import jax.numpy as jnp
from jax import lax
from jax.experimental import pallas as pl
from jax.experimental.pallas import tpu as pltpu
from jax.sharding import PartitionSpec as P

HD = 128
GROUP = 4
KEY_BLOCK = 2048

NEGATIVE = -1e30


def attention_kernel(table_ref, meta_ref, q_ref, k_ref, v_ref, acc_ref, peak_ref, total_ref):
    g = pl.program_id(0)
    step = pl.program_id(1)
    blocks = pl.num_programs(1)
    count = meta_ref[g, 0]
    is_retrieval = meta_ref[g, 1]
    sink = meta_ref[g, 2]
    window = meta_ref[g, 3]
    row_base = meta_ref[g, 4]
    key_offset = meta_ref[g, 5]
    rows = q_ref.shape[1] // GROUP
    width = k_ref.shape[0]

    @pl.when(step == 0)
    def _():
        peak_ref[...] = jnp.full_like(peak_ref, NEGATIVE)
        total_ref[...] = jnp.zeros_like(total_ref)
        acc_ref[...] = jnp.zeros_like(acc_ref)

    def update(allowed):
        scores = lax.dot_general(
            q_ref[0], k_ref[...], (((1,), (1,)), ((), ())), preferred_element_type=jnp.float32
        ) * HD ** (-0.5)
        old_peak = peak_ref[0]
        if allowed is None:
            block_peak = jnp.max(scores, axis=-1, keepdims=True)
            new_peak = jnp.maximum(old_peak, block_peak)
            weights = jnp.exp(scores - new_peak)
        else:
            scores = scores.reshape(GROUP, rows, width)
            block_peak = jnp.max(
                jnp.where(allowed, scores, NEGATIVE), axis=-1, keepdims=True
            ).reshape(GROUP * rows, 1)
            new_peak = jnp.maximum(old_peak, block_peak)
            weights = jnp.where(
                allowed, jnp.exp(scores - new_peak.reshape(GROUP, rows, 1)), 0.0
            ).reshape(GROUP * rows, width)
        rescale = jnp.exp(old_peak - new_peak)
        total_ref[0] = rescale * total_ref[0] + jnp.sum(weights, axis=-1, keepdims=True)
        acc_ref[0] = rescale * acc_ref[0] + jnp.dot(
            weights.astype(jnp.bfloat16), v_ref[...], preferred_element_type=jnp.float32
        )
        peak_ref[0] = new_peak

    full = table_ref[g, blocks + step]

    @pl.when((step < count) & (full == 1))
    def _():
        update(None)

    @pl.when((step < count) & (full == 0))
    def _():
        block = table_ref[g, step]
        key_base = key_offset + block * width
        row = lax.broadcasted_iota(jnp.int32, (rows, width), 0)
        col = lax.broadcasted_iota(jnp.int32, (rows, width), 1)
        later_minus_earlier = (row - col) + (row_base - key_base)
        reach = jnp.where(is_retrieval == 1, jnp.int32(2**30), window)
        allowed = (later_minus_earlier >= 0) & (
            (later_minus_earlier < reach) | (col + key_base < sink)
        )
        update(allowed[None])


def block_table(row_base, row_count, key_offset, key_count, roles, sinks, windows):
    blocks = key_count // KEY_BLOCK
    first = key_offset + jnp.arange(blocks, dtype=jnp.int32) * KEY_BLOCK
    last_key = first + KEY_BLOCK - 1
    last_row = row_base + row_count - 1
    causal = first <= last_row
    reach = last_key[None, :] >= row_base - windows[:, None] + 1
    sunk = first[None, :] < sinks[:, None]
    retrieval = roles[:, None] == 1
    needed = causal[None, :] & (retrieval | reach | sunk)
    whole = (last_key <= row_base)[None, :] & (
        retrieval
        | (last_key[None, :] < sinks[:, None])
        | (last_row - first[None, :] < windows[:, None])
    )
    order = jnp.argsort(jnp.logical_not(needed), axis=1, stable=True).astype(jnp.int32)
    count = jnp.sum(needed, axis=1).astype(jnp.int32)
    last = jnp.take_along_axis(order, jnp.maximum(count - 1, 0)[:, None], axis=1)
    steps = jnp.arange(blocks, dtype=jnp.int32)[None, :]
    table = jnp.where(steps < count[:, None], order, last)
    full = jnp.take_along_axis(whole, table, axis=1).astype(jnp.int32)
    meta = jnp.stack(
        [
            count,
            roles,
            sinks,
            windows,
            jnp.broadcast_to(row_base, count.shape),
            jnp.broadcast_to(key_offset, count.shape),
        ],
        axis=1,
    ).astype(jnp.int32)
    meta = jnp.pad(meta, ((0, 0), (0, 2)))
    return jnp.concatenate([table, full], axis=1), meta


def attend(stacked, both, table, meta):
    local_heads, stack_rows, _ = stacked.shape
    blocks = table.shape[1] // 2
    return pl.pallas_call(
        attention_kernel,
        out_shape=(
            jax.ShapeDtypeStruct(stacked.shape, jnp.float32),
            jax.ShapeDtypeStruct((local_heads, stack_rows, 1), jnp.float32),
            jax.ShapeDtypeStruct((local_heads, stack_rows, 1), jnp.float32),
        ),
        grid_spec=pltpu.PrefetchScalarGridSpec(
            num_scalar_prefetch=2,
            grid=(local_heads, blocks),
            in_specs=[
                pl.BlockSpec((1, stack_rows, HD), lambda g, s, t, m: (g, 0, 0)),
                pl.BlockSpec((KEY_BLOCK, HD), lambda g, s, t, m: (t[g, s], g)),
                pl.BlockSpec((KEY_BLOCK, HD), lambda g, s, t, m: (t[g, s], local_heads + g)),
            ],
            out_specs=(
                pl.BlockSpec((1, stack_rows, HD), lambda g, s, t, m: (g, 0, 0)),
                pl.BlockSpec((1, stack_rows, 1), lambda g, s, t, m: (g, 0, 0)),
                pl.BlockSpec((1, stack_rows, 1), lambda g, s, t, m: (g, 0, 0)),
            ),
        ),
        compiler_params=pltpu.CompilerParams(
            dimension_semantics=("arbitrary", "arbitrary")
        ),
    )(table, meta, stacked, both, both)


def stack_heads(queries, local_heads):
    rows = queries.shape[0]
    return (
        queries.reshape(rows, local_heads, GROUP, HD)
        .transpose(1, 2, 0, 3)
        .reshape(local_heads, GROUP * rows, HD)
    )


def merge(own, other, row_count):
    acc_a, peak_a, total_a = own
    acc_b, peak_b, total_b = other
    peak = jnp.maximum(peak_a, peak_b)
    scale_a = jnp.exp(peak_a - peak)
    scale_b = jnp.exp(peak_b - peak)
    acc = acc_a * scale_a + acc_b * scale_b
    total = total_a * scale_a + total_b * scale_b
    local_heads = acc.shape[0]
    attended = (acc / total).astype(jnp.bfloat16)
    return (
        attended.reshape(local_heads, GROUP, row_count, HD)
        .transpose(2, 0, 1, 3)
        .reshape(row_count, local_heads * GROUP * HD)
    )


def place(result, piece, origin):
    return lax.dynamic_update_slice(result, piece, (origin * piece.shape[0], 0))


def gather_ring(block, axis):
    size = lax.axis_size(axis)
    here = lax.axis_index(axis)
    result = jnp.zeros((size * block.shape[0], block.shape[1]), block.dtype)
    result = place(result, block, here)
    for shift in range(1, size):
        piece = lax.ppermute(block, axis, [(i, (i + shift) % size) for i in range(size)])
        result = place(result, piece, (here - shift) % size)
    return result


def gather_both_ways(block, axis):
    size = lax.axis_size(axis)
    here = lax.axis_index(axis)
    right = [(i, (i + 1) % size) for i in range(size)]
    left = [(i, (i - 1) % size) for i in range(size)]
    result = jnp.zeros((size * block.shape[0], block.shape[1]), block.dtype)
    result = place(result, block, here)
    forward = block
    backward = block
    for step in range(1, size // 2 + 1):
        forward = lax.ppermute(forward, axis, right)
        result = place(result, forward, (here - step) % size)
        if step < size - size // 2:
            backward = lax.ppermute(backward, axis, left)
            result = place(result, backward, (here + step) % size)
    return result


def scatter_sum(partial):
    rows, width = partial.shape
    quarter = rows // 4
    parts = partial.reshape(2, 2, quarter, width)
    core = lax.axis_index("core")
    keep = jnp.take(parts, core, axis=1)
    give = jnp.take(parts, 1 - core, axis=1)
    got = lax.ppermute(give.astype(jnp.bfloat16), "core", [(0, 1), (1, 0)])
    summed = keep + got.astype(jnp.float32)
    xl = lax.axis_index("xl")
    keep = jnp.take(summed, xl, axis=0)
    give = jnp.take(summed, 1 - xl, axis=0)
    got = lax.ppermute(give.astype(jnp.bfloat16), "xl", [(0, 1), (1, 0)])
    return (keep + got.astype(jnp.float32)).astype(jnp.bfloat16)


def per_device(queries, key_states, value_states, out_weight, head_role, sink_len, window_len):
    row_count = queries.shape[0]
    local_heads = key_states.shape[1] // HD
    half_size = lax.axis_size("z") * lax.axis_size("y")
    half = lax.axis_index("xh")
    place = lax.axis_index("z") * lax.axis_size("y") + lax.axis_index("y")
    ctx = half * half_size + place
    partner = (1 - half) * half_size + place
    head_index = lax.axis_index("xl") * lax.axis_size("core") + lax.axis_index("core")
    first_head = head_index * local_heads
    roles_here = lax.dynamic_slice_in_dim(head_role, first_head, local_heads)
    sinks_here = lax.dynamic_slice_in_dim(sink_len, first_head, local_heads)
    windows_here = lax.dynamic_slice_in_dim(window_len, first_head, local_heads)
    partner_queries = lax.ppermute(stack_heads(queries, local_heads), "xh", [(1, 0)])
    both = jnp.concatenate([key_states, value_states], axis=1)
    both = gather_ring(both, "y")
    both = gather_both_ways(both, "z")
    key_offset = half * both.shape[0]
    table, meta = block_table(
        partner * row_count, row_count, key_offset, both.shape[0],
        roles_here, sinks_here, windows_here,
    )
    acc_p, peak_p, total_p = attend(partner_queries, both, table, meta)
    stats_p = jnp.concatenate(
        [peak_p.reshape(local_heads, -1), total_p.reshape(local_heads, -1)], axis=0
    )
    acc_p = lax.ppermute(acc_p.astype(jnp.bfloat16), "xh", [(0, 1)])
    stats_p = lax.ppermute(stats_p, "xh", [(0, 1)])
    table, meta = block_table(
        ctx * row_count, row_count, key_offset, both.shape[0],
        roles_here, sinks_here, windows_here,
    )
    own = attend(stack_heads(queries, local_heads), both, table, meta)
    received = half == 1
    peak_b = jnp.where(received, stats_p[:local_heads], NEGATIVE)[:, :, None]
    total_b = jnp.where(received, stats_p[local_heads:], 0.0)[:, :, None]
    acc_b = jnp.where(received, acc_p.astype(jnp.float32), 0.0)
    attended = merge(own, (acc_b, peak_b, total_b), row_count)
    partial = jnp.dot(attended, out_weight, preferred_element_type=jnp.float32)
    return scatter_sum(partial)


def solution(mesh):
    ctx_size = mesh.shape["ctx"]
    y_size = 4
    devices = mesh.devices.reshape(2, ctx_size // (2 * y_size), y_size, 2, mesh.shape["head"] // 2)
    split = jax.sharding.Mesh(devices, ("xh", "z", "y", "xl", "core"))
    tokens = ("xh", "z", "y")
    heads = ("xl", "core")
    in_specs = (
        P(tokens, heads),
        P(tokens, heads),
        P(tokens, heads),
        P(heads, None),
        P(),
        P(),
        P(),
    )
    out_specs = P(("xh", "z", "y", "xl", "core"), None)
    return jax.shard_map(
        per_device, mesh=split, in_specs=in_specs, out_specs=out_specs, check_vma=False
    )
```

```python
import functools

import jax
import jax.numpy as jnp
from jax import lax
from jax.experimental import pallas as pl
from jax.experimental.pallas import tpu as pltpu
from jax.sharding import PartitionSpec as P

HD = 128
GROUP = 4
KEY_BLOCK = 2048

NEGATIVE = -1e30


def attention_kernel(table_ref, meta_ref, q_ref, k_ref, v_ref, acc_ref, peak_ref, total_ref):
    g = pl.program_id(0)
    step = pl.program_id(1)
    blocks = pl.num_programs(1)
    count = meta_ref[g, 0]
    is_retrieval = meta_ref[g, 1]
    sink = meta_ref[g, 2]
    window = meta_ref[g, 3]
    row_base = meta_ref[g, 4]
    key_offset = meta_ref[g, 5]
    rows = q_ref.shape[1] // GROUP
    width = k_ref.shape[0]

    @pl.when(step == 0)
    def _():
        peak_ref[...] = jnp.full_like(peak_ref, NEGATIVE)
        total_ref[...] = jnp.zeros_like(total_ref)
        acc_ref[...] = jnp.zeros_like(acc_ref)

    def update(allowed):
        scores = lax.dot_general(
            q_ref[0], k_ref[...], (((1,), (1,)), ((), ())), preferred_element_type=jnp.float32
        ) * HD ** (-0.5)
        old_peak = peak_ref[0]
        if allowed is None:
            block_peak = jnp.max(scores, axis=-1, keepdims=True)
            new_peak = jnp.maximum(old_peak, block_peak)
            weights = jnp.exp(scores - new_peak)
        else:
            scores = scores.reshape(GROUP, rows, width)
            block_peak = jnp.max(
                jnp.where(allowed, scores, NEGATIVE), axis=-1, keepdims=True
            ).reshape(GROUP * rows, 1)
            new_peak = jnp.maximum(old_peak, block_peak)
            weights = jnp.where(
                allowed, jnp.exp(scores - new_peak.reshape(GROUP, rows, 1)), 0.0
            ).reshape(GROUP * rows, width)
        rescale = jnp.exp(old_peak - new_peak)
        total_ref[0] = rescale * total_ref[0] + jnp.sum(weights, axis=-1, keepdims=True)
        acc_ref[0] = rescale * acc_ref[0] + jnp.dot(
            weights.astype(jnp.bfloat16), v_ref[...], preferred_element_type=jnp.float32
        )
        peak_ref[0] = new_peak

    full = table_ref[g, blocks + step]

    @pl.when((step < count) & (full == 1))
    def _():
        update(None)

    @pl.when((step < count) & (full == 0))
    def _():
        block = table_ref[g, step]
        key_base = key_offset + block * width
        row = lax.broadcasted_iota(jnp.int32, (rows, width), 0)
        col = lax.broadcasted_iota(jnp.int32, (rows, width), 1)
        later_minus_earlier = (row - col) + (row_base - key_base)
        reach = jnp.where(is_retrieval == 1, jnp.int32(2**30), window)
        allowed = (later_minus_earlier >= 0) & (
            (later_minus_earlier < reach) | (col + key_base < sink)
        )
        update(allowed[None])


def piece_kernel(meta_ref, q_ref, k_ref, v_ref, acc_in, peak_in, total_in,
                 acc_ref, peak_ref, total_ref):
    i = pl.program_id(0)
    needed = meta_ref[i, 0]
    full = meta_ref[i, 1]
    is_retrieval = meta_ref[i, 2]
    sink = meta_ref[i, 3]
    window = meta_ref[i, 4]
    row_base = meta_ref[i, 5]
    key_base = meta_ref[i, 6]
    rows = q_ref.shape[1] // GROUP
    width = k_ref.shape[0]
    acc_ref[...] = acc_in[...]
    peak_ref[...] = peak_in[...]
    total_ref[...] = total_in[...]

    def update(allowed):
        scores = lax.dot_general(
            q_ref[0], k_ref[...], (((1,), (1,)), ((), ())), preferred_element_type=jnp.float32
        ) * HD ** (-0.5)
        old_peak = peak_ref[0]
        if allowed is None:
            new_peak = jnp.maximum(old_peak, jnp.max(scores, axis=-1, keepdims=True))
            weights = jnp.exp(scores - new_peak)
        else:
            scores = scores.reshape(GROUP, rows, width)
            block_peak = jnp.max(
                jnp.where(allowed, scores, NEGATIVE), axis=-1, keepdims=True
            ).reshape(GROUP * rows, 1)
            new_peak = jnp.maximum(old_peak, block_peak)
            weights = jnp.where(
                allowed, jnp.exp(scores - new_peak.reshape(GROUP, rows, 1)), 0.0
            ).reshape(GROUP * rows, width)
        rescale = jnp.exp(old_peak - new_peak)
        total_ref[0] = rescale * total_ref[0] + jnp.sum(weights, axis=-1, keepdims=True)
        acc_ref[0] = rescale * acc_ref[0] + jnp.dot(
            weights.astype(jnp.bfloat16), v_ref[...], preferred_element_type=jnp.float32
        )
        peak_ref[0] = new_peak

    @pl.when((needed == 1) & (full == 1))
    def _():
        update(None)

    @pl.when((needed == 1) & (full == 0))
    def _():
        row = lax.broadcasted_iota(jnp.int32, (rows, width), 0)
        col = lax.broadcasted_iota(jnp.int32, (rows, width), 1)
        later_minus_earlier = (row - col) + (row_base - key_base)
        reach = jnp.where(is_retrieval == 1, jnp.int32(2**30), window)
        allowed = (later_minus_earlier >= 0) & (
            (later_minus_earlier < reach) | (col + key_base < sink)
        )
        update(allowed[None])


def piece_meta(row_bases, key_base, width, rows, roles, sinks, windows):
    last_key = key_base + width - 1
    last_rows = row_bases + rows - 1
    retrieval = roles == 1
    needed = (key_base <= last_rows) & (
        retrieval | (last_key >= row_bases - windows + 1) | (key_base < sinks)
    )
    full = (last_key <= row_bases) & (
        retrieval | (last_key < sinks) | (last_rows - key_base < windows)
    )
    zeros = jnp.zeros_like(row_bases)
    return jnp.stack(
        [needed.astype(jnp.int32), full.astype(jnp.int32), roles, sinks, windows,
         row_bases, zeros + key_base, zeros],
        axis=1,
    ).astype(jnp.int32)


def attend_piece(meta, stacked, piece, state):
    count, stack_rows, _ = stacked.shape
    local_heads = piece.shape[1] // (2 * HD)
    width = piece.shape[0]
    acc, peak, total = state
    return pl.pallas_call(
        piece_kernel,
        out_shape=(
            jax.ShapeDtypeStruct(acc.shape, jnp.float32),
            jax.ShapeDtypeStruct(peak.shape, jnp.float32),
            jax.ShapeDtypeStruct(total.shape, jnp.float32),
        ),
        grid_spec=pltpu.PrefetchScalarGridSpec(
            num_scalar_prefetch=1,
            grid=(count,),
            in_specs=[
                pl.BlockSpec((1, stack_rows, HD), lambda i, m: (i, 0, 0)),
                pl.BlockSpec((width, HD), lambda i, m: (0, i % local_heads)),
                pl.BlockSpec((width, HD), lambda i, m: (0, local_heads + i % local_heads)),
                pl.BlockSpec((1, stack_rows, HD), lambda i, m: (i, 0, 0)),
                pl.BlockSpec((1, stack_rows, 1), lambda i, m: (i, 0, 0)),
                pl.BlockSpec((1, stack_rows, 1), lambda i, m: (i, 0, 0)),
            ],
            out_specs=(
                pl.BlockSpec((1, stack_rows, HD), lambda i, m: (i, 0, 0)),
                pl.BlockSpec((1, stack_rows, 1), lambda i, m: (i, 0, 0)),
                pl.BlockSpec((1, stack_rows, 1), lambda i, m: (i, 0, 0)),
            ),
        ),
        compiler_params=pltpu.CompilerParams(dimension_semantics=("arbitrary",)),
        cost_estimate=pl.CostEstimate(
            flops=4 * count * stack_rows * width * HD,
            transcendentals=count * stack_rows * width,
            bytes_accessed=2 * piece.size + 2 * stacked.size + 8 * acc.size,
        ),
    )(meta, stacked, piece, piece, acc, peak, total)


def block_table(row_base, row_count, key_offset, key_count, roles, sinks, windows):
    blocks = key_count // KEY_BLOCK
    first = key_offset + jnp.arange(blocks, dtype=jnp.int32) * KEY_BLOCK
    last_key = first + KEY_BLOCK - 1
    last_row = row_base + row_count - 1
    causal = first <= last_row
    reach = last_key[None, :] >= row_base - windows[:, None] + 1
    sunk = first[None, :] < sinks[:, None]
    retrieval = roles[:, None] == 1
    needed = causal[None, :] & (retrieval | reach | sunk)
    whole = (last_key <= row_base)[None, :] & (
        retrieval
        | (last_key[None, :] < sinks[:, None])
        | (last_row - first[None, :] < windows[:, None])
    )
    order = jnp.argsort(jnp.logical_not(needed), axis=1, stable=True).astype(jnp.int32)
    count = jnp.sum(needed, axis=1).astype(jnp.int32)
    last = jnp.take_along_axis(order, jnp.maximum(count - 1, 0)[:, None], axis=1)
    steps = jnp.arange(blocks, dtype=jnp.int32)[None, :]
    table = jnp.where(steps < count[:, None], order, last)
    full = jnp.take_along_axis(whole, table, axis=1).astype(jnp.int32)
    meta = jnp.stack(
        [
            count,
            roles,
            sinks,
            windows,
            jnp.broadcast_to(row_base, count.shape),
            jnp.broadcast_to(key_offset, count.shape),
        ],
        axis=1,
    ).astype(jnp.int32)
    meta = jnp.pad(meta, ((0, 0), (0, 2)))
    return jnp.concatenate([table, full], axis=1), meta


def attend(stacked, both, table, meta):
    local_heads, stack_rows, _ = stacked.shape
    blocks = table.shape[1] // 2
    return pl.pallas_call(
        attention_kernel,
        out_shape=(
            jax.ShapeDtypeStruct(stacked.shape, jnp.float32),
            jax.ShapeDtypeStruct((local_heads, stack_rows, 1), jnp.float32),
            jax.ShapeDtypeStruct((local_heads, stack_rows, 1), jnp.float32),
        ),
        grid_spec=pltpu.PrefetchScalarGridSpec(
            num_scalar_prefetch=2,
            grid=(local_heads, blocks),
            in_specs=[
                pl.BlockSpec((1, stack_rows, HD), lambda g, s, t, m: (g, 0, 0)),
                pl.BlockSpec((KEY_BLOCK, HD), lambda g, s, t, m: (t[g, s], g)),
                pl.BlockSpec((KEY_BLOCK, HD), lambda g, s, t, m: (t[g, s], local_heads + g)),
            ],
            out_specs=(
                pl.BlockSpec((1, stack_rows, HD), lambda g, s, t, m: (g, 0, 0)),
                pl.BlockSpec((1, stack_rows, 1), lambda g, s, t, m: (g, 0, 0)),
                pl.BlockSpec((1, stack_rows, 1), lambda g, s, t, m: (g, 0, 0)),
            ),
        ),
        compiler_params=pltpu.CompilerParams(
            dimension_semantics=("arbitrary", "arbitrary")
        ),
    )(table, meta, stacked, both, both)


def stack_heads(queries, local_heads):
    rows = queries.shape[0]
    return (
        queries.reshape(rows, local_heads, GROUP, HD)
        .transpose(1, 2, 0, 3)
        .reshape(local_heads, GROUP * rows, HD)
    )


def merge(own, other, row_count):
    acc_a, peak_a, total_a = own
    acc_b, peak_b, total_b = other
    peak = jnp.maximum(peak_a, peak_b)
    scale_a = jnp.exp(peak_a - peak)
    scale_b = jnp.exp(peak_b - peak)
    acc = acc_a * scale_a + acc_b * scale_b
    total = total_a * scale_a + total_b * scale_b
    local_heads = acc.shape[0]
    attended = (acc / total).astype(jnp.bfloat16)
    return (
        attended.reshape(local_heads, GROUP, row_count, HD)
        .transpose(2, 0, 1, 3)
        .reshape(row_count, local_heads * GROUP * HD)
    )


def place(result, piece, origin):
    return lax.dynamic_update_slice(result, piece, (origin * piece.shape[0], 0))


def gather_ring(block, axis):
    size = lax.axis_size(axis)
    here = lax.axis_index(axis)
    result = jnp.zeros((size * block.shape[0], block.shape[1]), block.dtype)
    result = place(result, block, here)
    for shift in range(1, size):
        piece = lax.ppermute(block, axis, [(i, (i + shift) % size) for i in range(size)])
        result = place(result, piece, (here - shift) % size)
    return result


def gather_both_ways(block, axis):
    size = lax.axis_size(axis)
    here = lax.axis_index(axis)
    right = [(i, (i + 1) % size) for i in range(size)]
    left = [(i, (i - 1) % size) for i in range(size)]
    result = jnp.zeros((size * block.shape[0], block.shape[1]), block.dtype)
    result = place(result, block, here)
    forward = block
    backward = block
    for step in range(1, size // 2 + 1):
        forward = lax.ppermute(forward, axis, right)
        result = place(result, forward, (here - step) % size)
        if step < size - size // 2:
            backward = lax.ppermute(backward, axis, left)
            result = place(result, backward, (here + step) % size)
    return result


def scatter_sum(partial):
    rows, width = partial.shape
    quarter = rows // 4
    parts = partial.reshape(2, 2, quarter, width)
    core = lax.axis_index("core")
    keep = jnp.take(parts, core, axis=1)
    give = jnp.take(parts, 1 - core, axis=1)
    got = lax.ppermute(give.astype(jnp.bfloat16), "core", [(0, 1), (1, 0)])
    summed = keep + got.astype(jnp.float32)
    xl = lax.axis_index("xl")
    keep = jnp.take(summed, xl, axis=0)
    give = jnp.take(summed, 1 - xl, axis=0)
    got = lax.ppermute(give.astype(jnp.bfloat16), "xl", [(0, 1), (1, 0)])
    return (keep + got.astype(jnp.float32)).astype(jnp.bfloat16)


def per_device(queries, key_states, value_states, out_weight, head_role, sink_len, window_len):
    row_count = queries.shape[0]
    local_heads = key_states.shape[1] // HD
    half_size = lax.axis_size("z") * lax.axis_size("y")
    half = lax.axis_index("xh")
    place = lax.axis_index("z") * lax.axis_size("y") + lax.axis_index("y")
    ctx = half * half_size + place
    partner = (1 - half) * half_size + place
    head_index = lax.axis_index("xl") * lax.axis_size("core") + lax.axis_index("core")
    first_head = head_index * local_heads
    roles_here = lax.dynamic_slice_in_dim(head_role, first_head, local_heads)
    sinks_here = lax.dynamic_slice_in_dim(sink_len, first_head, local_heads)
    windows_here = lax.dynamic_slice_in_dim(window_len, first_head, local_heads)
    partner_queries = lax.ppermute(stack_heads(queries, local_heads), "xh", [(1, 0)])
    both = jnp.concatenate([key_states, value_states], axis=1)
    both = gather_ring(both, "y")
    stacked = jnp.concatenate([partner_queries, stack_heads(queries, local_heads)], axis=0)
    row_bases = jnp.concatenate(
        [jnp.broadcast_to(partner * row_count, (local_heads,)),
         jnp.broadcast_to(ctx * row_count, (local_heads,))]
    ).astype(jnp.int32)
    roles2 = jnp.concatenate([roles_here, roles_here])
    sinks2 = jnp.concatenate([sinks_here, sinks_here])
    windows2 = jnp.concatenate([windows_here, windows_here])
    width = both.shape[0]
    key_start = half * width * lax.axis_size("z")
    heads2 = 2 * local_heads
    state = (
        jnp.zeros((heads2, GROUP * row_count, HD), jnp.float32),
        jnp.full((heads2, GROUP * row_count, 1), NEGATIVE, jnp.float32),
        jnp.zeros((heads2, GROUP * row_count, 1), jnp.float32),
    )

    def take(state, piece, origin):
        meta = piece_meta(
            row_bases, key_start + origin * width, width, row_count, roles2, sinks2, windows2
        )
        return attend_piece(meta, stacked, piece, state)

    size = lax.axis_size("z")
    here = lax.axis_index("z")
    right = [(i, (i + 1) % size) for i in range(size)]
    left = [(i, (i - 1) % size) for i in range(size)]
    steps = size // 2
    forward = lax.ppermute(both, "z", right)
    backward = lax.ppermute(both, "z", left)
    state = take(state, both, here)
    state, forward, backward = lax.optimization_barrier((state, forward, backward))
    for step in range(1, steps + 1):
        sends_back = step + 1 < size - steps
        if step < steps:
            next_forward = lax.ppermute(forward, "z", right)
        if sends_back:
            next_backward = lax.ppermute(backward, "z", left)
        state = take(state, forward, (here - step) % size)
        if step < size - steps:
            state = take(state, backward, (here + step) % size)
        if step < steps:
            forward = next_forward
            if sends_back:
                backward = next_backward
                state, forward, backward = lax.optimization_barrier((state, forward, backward))
            else:
                state, forward = lax.optimization_barrier((state, forward))
    acc_all, peak_all, total_all = state
    acc_p, peak_p, total_p = acc_all[:local_heads], peak_all[:local_heads], total_all[:local_heads]
    own = (acc_all[local_heads:], peak_all[local_heads:], total_all[local_heads:])
    stats_p = jnp.concatenate(
        [peak_p.reshape(local_heads, -1), total_p.reshape(local_heads, -1)], axis=0
    )
    acc_p = lax.ppermute(acc_p.astype(jnp.bfloat16), "xh", [(0, 1)])
    stats_p = lax.ppermute(stats_p, "xh", [(0, 1)])
    received = half == 1
    peak_b = jnp.where(received, stats_p[:local_heads], NEGATIVE)[:, :, None]
    total_b = jnp.where(received, stats_p[local_heads:], 0.0)[:, :, None]
    acc_b = jnp.where(received, acc_p.astype(jnp.float32), 0.0)
    attended = merge(own, (acc_b, peak_b, total_b), row_count)
    partial = jnp.dot(attended, out_weight, preferred_element_type=jnp.float32)
    return scatter_sum(partial)


def solution(mesh):
    ctx_size = mesh.shape["ctx"]
    y_size = 4
    devices = mesh.devices.reshape(2, ctx_size // (2 * y_size), y_size, 2, mesh.shape["head"] // 2)
    split = jax.sharding.Mesh(devices, ("xh", "z", "y", "xl", "core"))
    tokens = ("xh", "z", "y")
    heads = ("xl", "core")
    in_specs = (
        P(tokens, heads),
        P(tokens, heads),
        P(tokens, heads),
        P(heads, None),
        P(),
        P(),
        P(),
    )
    out_specs = P(("xh", "z", "y", "xl", "core"), None)
    return jax.shard_map(
        per_device, mesh=split, in_specs=in_specs, out_specs=out_specs, check_vma=False
    )
```

```python
import functools

import jax
import jax.numpy as jnp
from jax import lax
from jax.experimental import pallas as pl
from jax.experimental.pallas import tpu as pltpu
from jax.sharding import PartitionSpec as P

HD = 128
GROUP = 4
KEY_BLOCK = 2048

NEGATIVE = -1e30


def attention_kernel(table_ref, meta_ref, q_ref, k_ref, v_ref, acc_ref, peak_ref, total_ref):
    g = pl.program_id(0)
    step = pl.program_id(1)
    blocks = pl.num_programs(1)
    count = meta_ref[g, 0]
    is_retrieval = meta_ref[g, 1]
    sink = meta_ref[g, 2]
    window = meta_ref[g, 3]
    row_base = meta_ref[g, 4]
    key_offset = meta_ref[g, 5]
    rows = q_ref.shape[1] // GROUP
    width = k_ref.shape[0]

    @pl.when(step == 0)
    def _():
        peak_ref[...] = jnp.full_like(peak_ref, NEGATIVE)
        total_ref[...] = jnp.zeros_like(total_ref)
        acc_ref[...] = jnp.zeros_like(acc_ref)

    def update(allowed):
        scores = lax.dot_general(
            q_ref[0], k_ref[...], (((1,), (1,)), ((), ())), preferred_element_type=jnp.float32
        ) * HD ** (-0.5)
        old_peak = peak_ref[0]
        if allowed is None:
            block_peak = jnp.max(scores, axis=-1, keepdims=True)
            new_peak = jnp.maximum(old_peak, block_peak)
            weights = jnp.exp(scores - new_peak)
        else:
            scores = scores.reshape(GROUP, rows, width)
            block_peak = jnp.max(
                jnp.where(allowed, scores, NEGATIVE), axis=-1, keepdims=True
            ).reshape(GROUP * rows, 1)
            new_peak = jnp.maximum(old_peak, block_peak)
            weights = jnp.where(
                allowed, jnp.exp(scores - new_peak.reshape(GROUP, rows, 1)), 0.0
            ).reshape(GROUP * rows, width)
        rescale = jnp.exp(old_peak - new_peak)
        total_ref[0] = rescale * total_ref[0] + jnp.sum(weights, axis=-1, keepdims=True)
        acc_ref[0] = rescale * acc_ref[0] + jnp.dot(
            weights.astype(jnp.bfloat16), v_ref[...], preferred_element_type=jnp.float32
        )
        peak_ref[0] = new_peak

    full = table_ref[g, blocks + step]

    @pl.when((step < count) & (full == 1))
    def _():
        update(None)

    @pl.when((step < count) & (full == 0))
    def _():
        block = table_ref[g, step]
        key_base = key_offset + block * width
        row = lax.broadcasted_iota(jnp.int32, (rows, width), 0)
        col = lax.broadcasted_iota(jnp.int32, (rows, width), 1)
        later_minus_earlier = (row - col) + (row_base - key_base)
        reach = jnp.where(is_retrieval == 1, jnp.int32(2**30), window)
        allowed = (later_minus_earlier >= 0) & (
            (later_minus_earlier < reach) | (col + key_base < sink)
        )
        update(allowed[None])


def block_table(row_base, row_count, key_offset, key_count, roles, sinks, windows):
    blocks = key_count // KEY_BLOCK
    first = key_offset + jnp.arange(blocks, dtype=jnp.int32) * KEY_BLOCK
    last_key = first + KEY_BLOCK - 1
    last_row = row_base + row_count - 1
    causal = first <= last_row
    reach = last_key[None, :] >= row_base - windows[:, None] + 1
    sunk = first[None, :] < sinks[:, None]
    retrieval = roles[:, None] == 1
    needed = causal[None, :] & (retrieval | reach | sunk)
    whole = (last_key <= row_base)[None, :] & (
        retrieval
        | (last_key[None, :] < sinks[:, None])
        | (last_row - first[None, :] < windows[:, None])
    )
    order = jnp.argsort(jnp.logical_not(needed), axis=1, stable=True).astype(jnp.int32)
    count = jnp.sum(needed, axis=1).astype(jnp.int32)
    last = jnp.take_along_axis(order, jnp.maximum(count - 1, 0)[:, None], axis=1)
    steps = jnp.arange(blocks, dtype=jnp.int32)[None, :]
    table = jnp.where(steps < count[:, None], order, last)
    full = jnp.take_along_axis(whole, table, axis=1).astype(jnp.int32)
    meta = jnp.stack(
        [
            count,
            roles,
            sinks,
            windows,
            jnp.broadcast_to(row_base, count.shape),
            jnp.broadcast_to(key_offset, count.shape),
        ],
        axis=1,
    ).astype(jnp.int32)
    meta = jnp.pad(meta, ((0, 0), (0, 2)))
    return jnp.concatenate([table, full], axis=1), meta


def attend(stacked, both, table, meta):
    local_heads, stack_rows, _ = stacked.shape
    blocks = table.shape[1] // 2
    return pl.pallas_call(
        attention_kernel,
        out_shape=(
            jax.ShapeDtypeStruct(stacked.shape, jnp.float32),
            jax.ShapeDtypeStruct((local_heads, stack_rows, 1), jnp.float32),
            jax.ShapeDtypeStruct((local_heads, stack_rows, 1), jnp.float32),
        ),
        grid_spec=pltpu.PrefetchScalarGridSpec(
            num_scalar_prefetch=2,
            grid=(local_heads, blocks),
            in_specs=[
                pl.BlockSpec((1, stack_rows, HD), lambda g, s, t, m: (g, 0, 0)),
                pl.BlockSpec((KEY_BLOCK, HD), lambda g, s, t, m: (t[g, s], g)),
                pl.BlockSpec((KEY_BLOCK, HD), lambda g, s, t, m: (t[g, s], local_heads + g)),
            ],
            out_specs=(
                pl.BlockSpec((1, stack_rows, HD), lambda g, s, t, m: (g, 0, 0)),
                pl.BlockSpec((1, stack_rows, 1), lambda g, s, t, m: (g, 0, 0)),
                pl.BlockSpec((1, stack_rows, 1), lambda g, s, t, m: (g, 0, 0)),
            ),
        ),
        compiler_params=pltpu.CompilerParams(
            dimension_semantics=("arbitrary", "arbitrary")
        ),
    )(table, meta, stacked, both, both)


def stack_heads(queries, local_heads):
    rows = queries.shape[0]
    return (
        queries.reshape(rows, local_heads, GROUP, HD)
        .transpose(1, 2, 0, 3)
        .reshape(local_heads, GROUP * rows, HD)
    )


def merge(own, other, row_count):
    acc_a, peak_a, total_a = own
    acc_b, peak_b, total_b = other
    peak = jnp.maximum(peak_a, peak_b)
    scale_a = jnp.exp(peak_a - peak)
    scale_b = jnp.exp(peak_b - peak)
    acc = acc_a * scale_a + acc_b * scale_b
    total = total_a * scale_a + total_b * scale_b
    local_heads = acc.shape[0]
    attended = (acc / total).astype(jnp.bfloat16)
    return (
        attended.reshape(local_heads, GROUP, row_count, HD)
        .transpose(2, 0, 1, 3)
        .reshape(row_count, local_heads * GROUP * HD)
    )


def place(result, piece, origin):
    return lax.dynamic_update_slice(result, piece, (origin * piece.shape[0], 0))


def gather_ring(block, axis):
    size = lax.axis_size(axis)
    here = lax.axis_index(axis)
    result = jnp.zeros((size * block.shape[0], block.shape[1]), block.dtype)
    result = place(result, block, here)
    for shift in range(1, size):
        piece = lax.ppermute(block, axis, [(i, (i + shift) % size) for i in range(size)])
        result = place(result, piece, (here - shift) % size)
    return result


def gather_both_ways(block, axis):
    size = lax.axis_size(axis)
    here = lax.axis_index(axis)
    right = [(i, (i + 1) % size) for i in range(size)]
    left = [(i, (i - 1) % size) for i in range(size)]
    result = jnp.zeros((size * block.shape[0], block.shape[1]), block.dtype)
    result = place(result, block, here)
    forward = block
    backward = block
    for step in range(1, size // 2 + 1):
        forward = lax.ppermute(forward, axis, right)
        result = place(result, forward, (here - step) % size)
        if step < size - size // 2:
            backward = lax.ppermute(backward, axis, left)
            result = place(result, backward, (here + step) % size)
    return result


def scatter_sum(attended, out_weight):
    rows = attended.shape[0]
    quarter = rows // 4
    parts = attended.reshape(2, 2, quarter, attended.shape[1])
    core = lax.axis_index("core")

    def project(x):
        return jnp.einsum("aqf,fd->aqd", x, out_weight, preferred_element_type=jnp.float32)

    give = project(jnp.take(parts, 1 - core, axis=1))
    got = lax.ppermute(give.astype(jnp.bfloat16), "core", [(0, 1), (1, 0)])
    keep = lax.optimization_barrier(project(jnp.take(parts, core, axis=1)))
    summed = keep + got.astype(jnp.float32)
    xl = lax.axis_index("xl")
    keep = jnp.take(summed, xl, axis=0)
    give = jnp.take(summed, 1 - xl, axis=0)
    got = lax.ppermute(give.astype(jnp.bfloat16), "xl", [(0, 1), (1, 0)])
    return (keep + got.astype(jnp.float32)).astype(jnp.bfloat16)


def per_device(queries, key_states, value_states, out_weight, head_role, sink_len, window_len):
    row_count = queries.shape[0]
    local_heads = key_states.shape[1] // HD
    half_size = lax.axis_size("z") * lax.axis_size("y")
    half = lax.axis_index("xh")
    place = lax.axis_index("z") * lax.axis_size("y") + lax.axis_index("y")
    ctx = half * half_size + place
    partner = (1 - half) * half_size + place
    head_index = lax.axis_index("xl") * lax.axis_size("core") + lax.axis_index("core")
    first_head = head_index * local_heads
    roles_here = lax.dynamic_slice_in_dim(head_role, first_head, local_heads)
    sinks_here = lax.dynamic_slice_in_dim(sink_len, first_head, local_heads)
    windows_here = lax.dynamic_slice_in_dim(window_len, first_head, local_heads)
    partner_queries = lax.ppermute(stack_heads(queries, local_heads), "xh", [(1, 0)])
    both = jnp.concatenate([key_states, value_states], axis=1)
    both = gather_ring(both, "y")
    both = gather_both_ways(both, "z")
    key_offset = half * both.shape[0]
    table, meta = block_table(
        partner * row_count, row_count, key_offset, both.shape[0],
        roles_here, sinks_here, windows_here,
    )
    acc_p, peak_p, total_p = attend(partner_queries, both, table, meta)
    stats_p = jnp.concatenate(
        [peak_p.reshape(local_heads, -1), total_p.reshape(local_heads, -1)], axis=0
    )
    acc_p = lax.ppermute(acc_p.astype(jnp.bfloat16), "xh", [(0, 1)])
    stats_p = lax.ppermute(stats_p, "xh", [(0, 1)])
    table, meta = block_table(
        ctx * row_count, row_count, key_offset, both.shape[0],
        roles_here, sinks_here, windows_here,
    )
    own = attend(stack_heads(queries, local_heads), both, table, meta)
    received = half == 1
    peak_b = jnp.where(received, stats_p[:local_heads], NEGATIVE)[:, :, None]
    total_b = jnp.where(received, stats_p[local_heads:], 0.0)[:, :, None]
    acc_b = jnp.where(received, acc_p.astype(jnp.float32), 0.0)
    attended = merge(own, (acc_b, peak_b, total_b), row_count)
    return scatter_sum(attended, out_weight)


def solution(mesh):
    ctx_size = mesh.shape["ctx"]
    y_size = 4
    devices = mesh.devices.reshape(2, ctx_size // (2 * y_size), y_size, 2, mesh.shape["head"] // 2)
    split = jax.sharding.Mesh(devices, ("xh", "z", "y", "xl", "core"))
    tokens = ("xh", "z", "y")
    heads = ("xl", "core")
    in_specs = (
        P(tokens, heads),
        P(tokens, heads),
        P(tokens, heads),
        P(heads, None),
        P(),
        P(),
        P(),
    )
    out_specs = P(("xh", "z", "y", "xl", "core"), None)
    return jax.shard_map(
        per_device, mesh=split, in_specs=in_specs, out_specs=out_specs, check_vma=False
    )
```

```python
import functools

import jax
import jax.numpy as jnp
from jax import lax
from jax.experimental import pallas as pl
from jax.experimental.pallas import tpu as pltpu
from jax.sharding import PartitionSpec as P

HD = 128
GROUP = 4
KEY_BLOCK = 2048

NEGATIVE = -1e30


def attention_kernel(table_ref, meta_ref, q_ref, k_ref, v_ref, acc_ref, peak_ref, total_ref):
    g = pl.program_id(0)
    step = pl.program_id(1)
    blocks = pl.num_programs(1)
    count = meta_ref[g, 0]
    is_retrieval = meta_ref[g, 1]
    sink = meta_ref[g, 2]
    window = meta_ref[g, 3]
    row_base = meta_ref[g, 4]
    key_offset = meta_ref[g, 5]
    rows = q_ref.shape[1] // GROUP
    width = k_ref.shape[0]

    @pl.when(step == 0)
    def _():
        peak_ref[...] = jnp.full_like(peak_ref, NEGATIVE)
        total_ref[...] = jnp.zeros_like(total_ref)
        acc_ref[...] = jnp.zeros_like(acc_ref)

    def update(allowed):
        scores = lax.dot_general(
            q_ref[0], k_ref[...], (((1,), (1,)), ((), ())), preferred_element_type=jnp.float32
        ) * HD ** (-0.5)
        old_peak = peak_ref[0]
        if allowed is None:
            block_peak = jnp.max(scores, axis=-1, keepdims=True)
            new_peak = jnp.maximum(old_peak, block_peak)
            weights = jnp.exp(scores - new_peak)
        else:
            scores = scores.reshape(GROUP, rows, width)
            block_peak = jnp.max(
                jnp.where(allowed, scores, NEGATIVE), axis=-1, keepdims=True
            ).reshape(GROUP * rows, 1)
            new_peak = jnp.maximum(old_peak, block_peak)
            weights = jnp.where(
                allowed, jnp.exp(scores - new_peak.reshape(GROUP, rows, 1)), 0.0
            ).reshape(GROUP * rows, width)
        rescale = jnp.exp(old_peak - new_peak)
        total_ref[0] = rescale * total_ref[0] + jnp.sum(weights, axis=-1, keepdims=True)
        acc_ref[0] = rescale * acc_ref[0] + jnp.dot(
            weights.astype(jnp.bfloat16), v_ref[...], preferred_element_type=jnp.float32
        )
        peak_ref[0] = new_peak

    full = table_ref[g, blocks + step]

    @pl.when((step < count) & (full == 1))
    def _():
        update(None)

    @pl.when((step < count) & (full == 0))
    def _():
        block = table_ref[g, step]
        key_base = key_offset + block * width
        row = lax.broadcasted_iota(jnp.int32, (rows, width), 0)
        col = lax.broadcasted_iota(jnp.int32, (rows, width), 1)
        later_minus_earlier = (row - col) + (row_base - key_base)
        reach = jnp.where(is_retrieval == 1, jnp.int32(2**30), window)
        allowed = (later_minus_earlier >= 0) & (
            (later_minus_earlier < reach) | (col + key_base < sink)
        )
        update(allowed[None])


def block_table(row_base, row_count, key_offset, key_count, roles, sinks, windows):
    blocks = key_count // KEY_BLOCK
    first = key_offset + jnp.arange(blocks, dtype=jnp.int32) * KEY_BLOCK
    last_key = first + KEY_BLOCK - 1
    last_row = row_base + row_count - 1
    causal = first <= last_row
    reach = last_key[None, :] >= row_base - windows[:, None] + 1
    sunk = first[None, :] < sinks[:, None]
    retrieval = roles[:, None] == 1
    needed = causal[None, :] & (retrieval | reach | sunk)
    whole = (last_key <= row_base)[None, :] & (
        retrieval
        | (last_key[None, :] < sinks[:, None])
        | (last_row - first[None, :] < windows[:, None])
    )
    order = jnp.argsort(jnp.logical_not(needed), axis=1, stable=True).astype(jnp.int32)
    count = jnp.sum(needed, axis=1).astype(jnp.int32)
    last = jnp.take_along_axis(order, jnp.maximum(count - 1, 0)[:, None], axis=1)
    steps = jnp.arange(blocks, dtype=jnp.int32)[None, :]
    table = jnp.where(steps < count[:, None], order, last)
    full = jnp.take_along_axis(whole, table, axis=1).astype(jnp.int32)
    meta = jnp.stack(
        [
            count,
            roles,
            sinks,
            windows,
            jnp.broadcast_to(row_base, count.shape),
            jnp.broadcast_to(key_offset, count.shape),
        ],
        axis=1,
    ).astype(jnp.int32)
    meta = jnp.pad(meta, ((0, 0), (0, 2)))
    return jnp.concatenate([table, full], axis=1), meta


def attend(stacked, keys, values, table, meta):
    local_heads, stack_rows, _ = stacked.shape
    blocks = table.shape[1] // 2
    return pl.pallas_call(
        attention_kernel,
        out_shape=(
            jax.ShapeDtypeStruct(stacked.shape, jnp.float32),
            jax.ShapeDtypeStruct((local_heads, stack_rows, 1), jnp.float32),
            jax.ShapeDtypeStruct((local_heads, stack_rows, 1), jnp.float32),
        ),
        grid_spec=pltpu.PrefetchScalarGridSpec(
            num_scalar_prefetch=2,
            grid=(local_heads, blocks),
            in_specs=[
                pl.BlockSpec((1, stack_rows, HD), lambda g, s, t, m: (g, 0, 0)),
                pl.BlockSpec((KEY_BLOCK, HD), lambda g, s, t, m: (t[g, s], g)),
                pl.BlockSpec((KEY_BLOCK, HD), lambda g, s, t, m: (t[g, s], g)),
            ],
            out_specs=(
                pl.BlockSpec((1, stack_rows, HD), lambda g, s, t, m: (g, 0, 0)),
                pl.BlockSpec((1, stack_rows, 1), lambda g, s, t, m: (g, 0, 0)),
                pl.BlockSpec((1, stack_rows, 1), lambda g, s, t, m: (g, 0, 0)),
            ),
        ),
        compiler_params=pltpu.CompilerParams(
            dimension_semantics=("arbitrary", "arbitrary")
        ),
    )(table, meta, stacked, keys, values)


def stack_heads(queries, local_heads):
    rows = queries.shape[0]
    return (
        queries.reshape(rows, local_heads, GROUP, HD)
        .transpose(1, 2, 0, 3)
        .reshape(local_heads, GROUP * rows, HD)
    )


def merge(own, other, row_count):
    acc_a, peak_a, total_a = own
    acc_b, peak_b, total_b = other
    peak = jnp.maximum(peak_a, peak_b)
    scale_a = jnp.exp(peak_a - peak)
    scale_b = jnp.exp(peak_b - peak)
    acc = acc_a * scale_a + acc_b * scale_b
    total = total_a * scale_a + total_b * scale_b
    local_heads = acc.shape[0]
    attended = (acc / total).astype(jnp.bfloat16)
    return (
        attended.reshape(local_heads, GROUP, row_count, HD)
        .transpose(2, 0, 1, 3)
        .reshape(row_count, local_heads * GROUP * HD)
    )


def place(result, piece, origin):
    return lax.dynamic_update_slice(result, piece, (origin * piece.shape[0], 0))


def gather_ring(block, axis):
    size = lax.axis_size(axis)
    here = lax.axis_index(axis)
    result = jnp.zeros((size * block.shape[0], block.shape[1]), block.dtype)
    result = place(result, block, here)
    for shift in range(1, size):
        piece = lax.ppermute(block, axis, [(i, (i + shift) % size) for i in range(size)])
        result = place(result, piece, (here - shift) % size)
    return result


def gather_both_ways(block, axis, result=None, put=place):
    size = lax.axis_size(axis)
    here = lax.axis_index(axis)
    right = [(i, (i + 1) % size) for i in range(size)]
    left = [(i, (i - 1) % size) for i in range(size)]
    if result is None:
        result = jnp.zeros((size * block.shape[0], block.shape[1]), block.dtype)
    result = put(result, block, here)
    forward = block
    backward = block
    for step in range(1, size // 2 + 1):
        forward = lax.ppermute(forward, axis, right)
        result = put(result, forward, (here - step) % size)
        if step < size - size // 2:
            backward = lax.ppermute(backward, axis, left)
            result = put(result, backward, (here + step) % size)
    return result


def place_strided(result, piece, origin):
    outer = result.shape[0]
    return lax.dynamic_update_slice(
        result, piece.reshape(outer, 1, -1, piece.shape[1]), (0, origin, 0, 0)
    )


def gather_values(block, outer_axis, inner_axis):
    column = gather_both_ways(block, outer_axis)
    outer = lax.axis_size(outer_axis)
    inner = lax.axis_size(inner_axis)
    result = jnp.zeros((outer, inner, block.shape[0], block.shape[1]), block.dtype)
    result = gather_both_ways(column, inner_axis, result, place_strided)
    return result.reshape(outer * inner * block.shape[0], block.shape[1])


def scatter_sum(partial):
    rows, width = partial.shape
    quarter = rows // 4
    parts = partial.reshape(2, 2, quarter, width)
    core = lax.axis_index("core")
    keep = jnp.take(parts, core, axis=1)
    give = jnp.take(parts, 1 - core, axis=1)
    got = lax.ppermute(give.astype(jnp.bfloat16), "core", [(0, 1), (1, 0)])
    summed = keep + got.astype(jnp.float32)
    xl = lax.axis_index("xl")
    keep = jnp.take(summed, xl, axis=0)
    give = jnp.take(summed, 1 - xl, axis=0)
    got = lax.ppermute(give.astype(jnp.bfloat16), "xl", [(0, 1), (1, 0)])
    return (keep + got.astype(jnp.float32)).astype(jnp.bfloat16)


def per_device(queries, key_states, value_states, out_weight, head_role, sink_len, window_len):
    row_count = queries.shape[0]
    local_heads = key_states.shape[1] // HD
    half_size = lax.axis_size("z") * lax.axis_size("y")
    half = lax.axis_index("xh")
    place = lax.axis_index("z") * lax.axis_size("y") + lax.axis_index("y")
    ctx = half * half_size + place
    partner = (1 - half) * half_size + place
    head_index = lax.axis_index("xl") * lax.axis_size("core") + lax.axis_index("core")
    first_head = head_index * local_heads
    roles_here = lax.dynamic_slice_in_dim(head_role, first_head, local_heads)
    sinks_here = lax.dynamic_slice_in_dim(sink_len, first_head, local_heads)
    windows_here = lax.dynamic_slice_in_dim(window_len, first_head, local_heads)
    partner_queries = lax.ppermute(stack_heads(queries, local_heads), "xh", [(1, 0)])
    keys = gather_both_ways(gather_ring(key_states, "y"), "z")
    values = gather_values(value_states, "z", "y")
    key_offset = half * keys.shape[0]
    table, meta = block_table(
        partner * row_count, row_count, key_offset, keys.shape[0],
        roles_here, sinks_here, windows_here,
    )
    acc_p, peak_p, total_p = attend(partner_queries, keys, values, table, meta)
    stats_p = jnp.concatenate(
        [peak_p.reshape(local_heads, -1), total_p.reshape(local_heads, -1)], axis=0
    )
    acc_p = lax.ppermute(acc_p.astype(jnp.bfloat16), "xh", [(0, 1)])
    stats_p = lax.ppermute(stats_p, "xh", [(0, 1)])
    table, meta = block_table(
        ctx * row_count, row_count, key_offset, keys.shape[0],
        roles_here, sinks_here, windows_here,
    )
    own = attend(stack_heads(queries, local_heads), keys, values, table, meta)
    received = half == 1
    peak_b = jnp.where(received, stats_p[:local_heads], NEGATIVE)[:, :, None]
    total_b = jnp.where(received, stats_p[local_heads:], 0.0)[:, :, None]
    acc_b = jnp.where(received, acc_p.astype(jnp.float32), 0.0)
    attended = merge(own, (acc_b, peak_b, total_b), row_count)
    partial = jnp.dot(attended, out_weight, preferred_element_type=jnp.float32)
    return scatter_sum(partial)


def solution(mesh):
    ctx_size = mesh.shape["ctx"]
    y_size = 4
    devices = mesh.devices.reshape(2, ctx_size // (2 * y_size), y_size, 2, mesh.shape["head"] // 2)
    split = jax.sharding.Mesh(devices, ("xh", "z", "y", "xl", "core"))
    tokens = ("xh", "z", "y")
    heads = ("xl", "core")
    in_specs = (
        P(tokens, heads),
        P(tokens, heads),
        P(tokens, heads),
        P(heads, None),
        P(),
        P(),
        P(),
    )
    out_specs = P(("xh", "z", "y", "xl", "core"), None)
    return jax.shard_map(
        per_device, mesh=split, in_specs=in_specs, out_specs=out_specs, check_vma=False
    )
```

```python
import functools

import jax
import jax.numpy as jnp
from jax import lax
from jax.experimental import pallas as pl
from jax.experimental.pallas import tpu as pltpu
from jax.sharding import PartitionSpec as P

HD = 128
GROUP = 4
KEY_BLOCK = 2048

NEGATIVE = -1e30


def attention_kernel(table_ref, meta_ref, q_ref, k_ref, v_ref, acc_ref, peak_ref, total_ref,
                     send_ref, stats_ref):
    g = pl.program_id(0)
    step = pl.program_id(1)
    blocks = pl.num_programs(1)
    count = meta_ref[g, 0]
    is_retrieval = meta_ref[g, 1]
    sink = meta_ref[g, 2]
    window = meta_ref[g, 3]
    row_base = meta_ref[g, 4]
    key_offset = meta_ref[g, 5]
    rows = q_ref.shape[1] // GROUP
    width = k_ref.shape[0]

    @pl.when(step == 0)
    def _():
        peak_ref[...] = jnp.full_like(peak_ref, NEGATIVE)
        total_ref[...] = jnp.zeros_like(total_ref)
        acc_ref[...] = jnp.zeros_like(acc_ref)

    def update(allowed):
        scores = lax.dot_general(
            q_ref[0], k_ref[...], (((1,), (1,)), ((), ())), preferred_element_type=jnp.float32
        ) * HD ** (-0.5)
        old_peak = peak_ref[0]
        if allowed is None:
            block_peak = jnp.max(scores, axis=-1, keepdims=True)
            new_peak = jnp.maximum(old_peak, block_peak)
            weights = jnp.exp(scores - new_peak)
        else:
            scores = scores.reshape(GROUP, rows, width)
            block_peak = jnp.max(
                jnp.where(allowed, scores, NEGATIVE), axis=-1, keepdims=True
            ).reshape(GROUP * rows, 1)
            new_peak = jnp.maximum(old_peak, block_peak)
            weights = jnp.where(
                allowed, jnp.exp(scores - new_peak.reshape(GROUP, rows, 1)), 0.0
            ).reshape(GROUP * rows, width)
        rescale = jnp.exp(old_peak - new_peak)
        total_ref[0] = rescale * total_ref[0] + jnp.sum(weights, axis=-1, keepdims=True)
        acc_ref[0] = rescale * acc_ref[0] + jnp.dot(
            weights.astype(jnp.bfloat16), v_ref[...], preferred_element_type=jnp.float32
        )
        peak_ref[0] = new_peak

    full = table_ref[g, blocks + step]

    @pl.when((step < count) & (full == 1))
    def _():
        update(None)

    @pl.when((step < count) & (full == 0))
    def _():
        block = table_ref[g, step]
        key_base = key_offset + block * width
        row = lax.broadcasted_iota(jnp.int32, (rows, width), 0)
        col = lax.broadcasted_iota(jnp.int32, (rows, width), 1)
        later_minus_earlier = (row - col) + (row_base - key_base)
        reach = jnp.where(is_retrieval == 1, jnp.int32(2**30), window)
        allowed = (later_minus_earlier >= 0) & (
            (later_minus_earlier < reach) | (col + key_base < sink)
        )
        update(allowed[None])

    @pl.when(step == blocks - 1)
    def _():
        send_ref[...] = acc_ref[...].astype(send_ref.dtype)
        stats_ref[0, 0:1, :] = jnp.transpose(peak_ref[0])
        stats_ref[0, 1:2, :] = jnp.transpose(total_ref[0])


def block_table(row_base, row_count, key_offset, key_count, roles, sinks, windows):
    blocks = key_count // KEY_BLOCK
    first = key_offset + jnp.arange(blocks, dtype=jnp.int32) * KEY_BLOCK
    last_key = first + KEY_BLOCK - 1
    last_row = row_base + row_count - 1
    causal = first <= last_row
    reach = last_key[None, :] >= row_base - windows[:, None] + 1
    sunk = first[None, :] < sinks[:, None]
    retrieval = roles[:, None] == 1
    needed = causal[None, :] & (retrieval | reach | sunk)
    whole = (last_key <= row_base)[None, :] & (
        retrieval
        | (last_key[None, :] < sinks[:, None])
        | (last_row - first[None, :] < windows[:, None])
    )
    order = jnp.argsort(jnp.logical_not(needed), axis=1, stable=True).astype(jnp.int32)
    count = jnp.sum(needed, axis=1).astype(jnp.int32)
    last = jnp.take_along_axis(order, jnp.maximum(count - 1, 0)[:, None], axis=1)
    steps = jnp.arange(blocks, dtype=jnp.int32)[None, :]
    table = jnp.where(steps < count[:, None], order, last)
    full = jnp.take_along_axis(whole, table, axis=1).astype(jnp.int32)
    meta = jnp.stack(
        [
            count,
            roles,
            sinks,
            windows,
            jnp.broadcast_to(row_base, count.shape),
            jnp.broadcast_to(key_offset, count.shape),
        ],
        axis=1,
    ).astype(jnp.int32)
    meta = jnp.pad(meta, ((0, 0), (0, 2)))
    return jnp.concatenate([table, full], axis=1), meta


def attend(stacked, both, table, meta):
    local_heads, stack_rows, _ = stacked.shape
    blocks = table.shape[1] // 2
    return pl.pallas_call(
        attention_kernel,
        out_shape=(
            jax.ShapeDtypeStruct(stacked.shape, jnp.float32),
            jax.ShapeDtypeStruct((local_heads, stack_rows, 1), jnp.float32),
            jax.ShapeDtypeStruct((local_heads, stack_rows, 1), jnp.float32),
            jax.ShapeDtypeStruct(stacked.shape, jnp.bfloat16),
            jax.ShapeDtypeStruct((local_heads, 2, stack_rows), jnp.float32),
        ),
        grid_spec=pltpu.PrefetchScalarGridSpec(
            num_scalar_prefetch=2,
            grid=(local_heads, blocks),
            in_specs=[
                pl.BlockSpec((1, stack_rows, HD), lambda g, s, t, m: (g, 0, 0)),
                pl.BlockSpec((KEY_BLOCK, HD), lambda g, s, t, m: (t[g, s], g)),
                pl.BlockSpec((KEY_BLOCK, HD), lambda g, s, t, m: (t[g, s], local_heads + g)),
            ],
            out_specs=(
                pl.BlockSpec((1, stack_rows, HD), lambda g, s, t, m: (g, 0, 0)),
                pl.BlockSpec((1, stack_rows, 1), lambda g, s, t, m: (g, 0, 0)),
                pl.BlockSpec((1, stack_rows, 1), lambda g, s, t, m: (g, 0, 0)),
                pl.BlockSpec((1, stack_rows, HD), lambda g, s, t, m: (g, 0, 0)),
                pl.BlockSpec((1, 2, stack_rows), lambda g, s, t, m: (g, 0, 0)),
            ),
        ),
        compiler_params=pltpu.CompilerParams(
            dimension_semantics=("arbitrary", "arbitrary")
        ),
    )(table, meta, stacked, both, both)


def stack_heads(queries, local_heads):
    rows = queries.shape[0]
    return (
        queries.reshape(rows, local_heads, GROUP, HD)
        .transpose(1, 2, 0, 3)
        .reshape(local_heads, GROUP * rows, HD)
    )


def merge(own, other, row_count):
    acc_a, peak_a, total_a = own
    acc_b, peak_b, total_b = other
    peak = jnp.maximum(peak_a, peak_b)
    scale_a = jnp.exp(peak_a - peak)
    scale_b = jnp.exp(peak_b - peak)
    acc = acc_a * scale_a + acc_b * scale_b
    total = total_a * scale_a + total_b * scale_b
    local_heads = acc.shape[0]
    attended = (acc / total).astype(jnp.bfloat16)
    return (
        attended.reshape(local_heads, GROUP, row_count, HD)
        .transpose(2, 0, 1, 3)
        .reshape(row_count, local_heads * GROUP * HD)
    )


def place(result, piece, origin):
    return lax.dynamic_update_slice(result, piece, (origin * piece.shape[0], 0))


def gather_ring(block, axis):
    size = lax.axis_size(axis)
    here = lax.axis_index(axis)
    result = jnp.zeros((size * block.shape[0], block.shape[1]), block.dtype)
    result = place(result, block, here)
    for shift in range(1, size):
        piece = lax.ppermute(block, axis, [(i, (i + shift) % size) for i in range(size)])
        result = place(result, piece, (here - shift) % size)
    return result


def gather_both_ways(block, axis):
    size = lax.axis_size(axis)
    here = lax.axis_index(axis)
    right = [(i, (i + 1) % size) for i in range(size)]
    left = [(i, (i - 1) % size) for i in range(size)]
    result = jnp.zeros((size * block.shape[0], block.shape[1]), block.dtype)
    result = place(result, block, here)
    forward = block
    backward = block
    for step in range(1, size // 2 + 1):
        forward = lax.ppermute(forward, axis, right)
        result = place(result, forward, (here - step) % size)
        if step < size - size // 2:
            backward = lax.ppermute(backward, axis, left)
            result = place(result, backward, (here + step) % size)
    return result


def scatter_sum(partial):
    rows, width = partial.shape
    quarter = rows // 4
    parts = partial.reshape(2, 2, quarter, width)
    core = lax.axis_index("core")
    keep = jnp.take(parts, core, axis=1)
    give = jnp.take(parts, 1 - core, axis=1)
    got = lax.ppermute(give.astype(jnp.bfloat16), "core", [(0, 1), (1, 0)])
    summed = keep + got.astype(jnp.float32)
    xl = lax.axis_index("xl")
    keep = jnp.take(summed, xl, axis=0)
    give = jnp.take(summed, 1 - xl, axis=0)
    got = lax.ppermute(give.astype(jnp.bfloat16), "xl", [(0, 1), (1, 0)])
    return (keep + got.astype(jnp.float32)).astype(jnp.bfloat16)


def per_device(queries, key_states, value_states, out_weight, head_role, sink_len, window_len):
    row_count = queries.shape[0]
    local_heads = key_states.shape[1] // HD
    half_size = lax.axis_size("z") * lax.axis_size("y")
    half = lax.axis_index("xh")
    place = lax.axis_index("z") * lax.axis_size("y") + lax.axis_index("y")
    ctx = half * half_size + place
    partner = (1 - half) * half_size + place
    head_index = lax.axis_index("xl") * lax.axis_size("core") + lax.axis_index("core")
    first_head = head_index * local_heads
    roles_here = lax.dynamic_slice_in_dim(head_role, first_head, local_heads)
    sinks_here = lax.dynamic_slice_in_dim(sink_len, first_head, local_heads)
    windows_here = lax.dynamic_slice_in_dim(window_len, first_head, local_heads)
    partner_queries = lax.ppermute(stack_heads(queries, local_heads), "xh", [(1, 0)])
    both = jnp.concatenate([key_states, value_states], axis=1)
    both = gather_ring(both, "y")
    both = gather_both_ways(both, "z")
    key_offset = half * both.shape[0]
    table, meta = block_table(
        partner * row_count, row_count, key_offset, both.shape[0],
        roles_here, sinks_here, windows_here,
    )
    _, _, _, acc_p, stats_p = attend(partner_queries, both, table, meta)
    acc_p = lax.ppermute(acc_p, "xh", [(0, 1)])
    stats_p = lax.ppermute(stats_p, "xh", [(0, 1)])
    table, meta = block_table(
        ctx * row_count, row_count, key_offset, both.shape[0],
        roles_here, sinks_here, windows_here,
    )
    own = attend(stack_heads(queries, local_heads), both, table, meta)[:3]
    received = half == 1
    peak_b = jnp.where(received, stats_p[:, 0], NEGATIVE)[:, :, None]
    total_b = jnp.where(received, stats_p[:, 1], 0.0)[:, :, None]
    acc_b = jnp.where(received, acc_p.astype(jnp.float32), 0.0)
    attended = merge(own, (acc_b, peak_b, total_b), row_count)
    partial = jnp.dot(attended, out_weight, preferred_element_type=jnp.float32)
    return scatter_sum(partial)


def solution(mesh):
    ctx_size = mesh.shape["ctx"]
    y_size = 4
    devices = mesh.devices.reshape(2, ctx_size // (2 * y_size), y_size, 2, mesh.shape["head"] // 2)
    split = jax.sharding.Mesh(devices, ("xh", "z", "y", "xl", "core"))
    tokens = ("xh", "z", "y")
    heads = ("xl", "core")
    in_specs = (
        P(tokens, heads),
        P(tokens, heads),
        P(tokens, heads),
        P(heads, None),
        P(),
        P(),
        P(),
    )
    out_specs = P(("xh", "z", "y", "xl", "core"), None)
    return jax.shard_map(
        per_device, mesh=split, in_specs=in_specs, out_specs=out_specs, check_vma=False
    )
```

```python
import functools

import jax
import jax.numpy as jnp
from jax import lax
from jax.experimental import pallas as pl
from jax.experimental.pallas import tpu as pltpu
from jax.sharding import PartitionSpec as P

HD = 128
GROUP = 4
KEY_BLOCK = 2048

NEGATIVE = -1e30


def attention_kernel(table_ref, meta_ref, q_ref, k_ref, v_ref, acc_ref, peak_ref, total_ref,
                     send_ref, stats_ref):
    g = pl.program_id(0)
    step = pl.program_id(1)
    blocks = pl.num_programs(1)
    count = meta_ref[g, 0]
    is_retrieval = meta_ref[g, 1]
    sink = meta_ref[g, 2]
    window = meta_ref[g, 3]
    row_base = meta_ref[g, 4]
    key_offset = meta_ref[g, 5]
    rows = q_ref.shape[1] // GROUP
    width = k_ref.shape[0]

    @pl.when(step == 0)
    def _():
        peak_ref[...] = jnp.full_like(peak_ref, NEGATIVE)
        total_ref[...] = jnp.zeros_like(total_ref)
        acc_ref[...] = jnp.zeros_like(acc_ref)

    def update(allowed):
        scores = lax.dot_general(
            q_ref[0], k_ref[...], (((1,), (1,)), ((), ())), preferred_element_type=jnp.float32
        ) * HD ** (-0.5)
        old_peak = peak_ref[0]
        if allowed is None:
            block_peak = jnp.max(scores, axis=-1, keepdims=True)
            new_peak = jnp.maximum(old_peak, block_peak)
            weights = jnp.exp(scores - new_peak)
        else:
            scores = scores.reshape(GROUP, rows, width)
            block_peak = jnp.max(
                jnp.where(allowed, scores, NEGATIVE), axis=-1, keepdims=True
            ).reshape(GROUP * rows, 1)
            new_peak = jnp.maximum(old_peak, block_peak)
            weights = jnp.where(
                allowed, jnp.exp(scores - new_peak.reshape(GROUP, rows, 1)), 0.0
            ).reshape(GROUP * rows, width)
        rescale = jnp.exp(old_peak - new_peak)
        total_ref[0] = rescale * total_ref[0] + jnp.sum(weights, axis=-1, keepdims=True)
        acc_ref[0] = rescale * acc_ref[0] + jnp.dot(
            weights.astype(jnp.bfloat16), v_ref[...], preferred_element_type=jnp.float32
        )
        peak_ref[0] = new_peak

    full = table_ref[g, blocks + step]

    @pl.when((step < count) & (full == 1))
    def _():
        update(None)

    @pl.when((step < count) & (full == 0))
    def _():
        block = table_ref[g, step]
        key_base = key_offset + block * width
        row = lax.broadcasted_iota(jnp.int32, (rows, width), 0)
        col = lax.broadcasted_iota(jnp.int32, (rows, width), 1)
        later_minus_earlier = (row - col) + (row_base - key_base)
        reach = jnp.where(is_retrieval == 1, jnp.int32(2**30), window)
        allowed = (later_minus_earlier >= 0) & (
            (later_minus_earlier < reach) | (col + key_base < sink)
        )
        update(allowed[None])

    @pl.when(step == blocks - 1)
    def _():
        send_ref[...] = acc_ref[...].astype(send_ref.dtype)
        stats_ref[0, 0:1, :] = jnp.transpose(peak_ref[0])
        stats_ref[0, 1:2, :] = jnp.transpose(total_ref[0])


def block_table(row_bases, row_count, key_offset, key_count, roles, sinks, windows):
    blocks = key_count // KEY_BLOCK
    first = key_offset + jnp.arange(blocks, dtype=jnp.int32) * KEY_BLOCK
    last_key = first + KEY_BLOCK - 1
    row_base = row_bases[:, None]
    last_row = row_base + row_count - 1
    causal = first[None, :] <= last_row
    reach = last_key[None, :] >= row_base - windows[:, None] + 1
    sunk = first[None, :] < sinks[:, None]
    retrieval = roles[:, None] == 1
    needed = causal & (retrieval | reach | sunk)
    whole = (last_key[None, :] <= row_base) & (
        retrieval
        | (last_key[None, :] < sinks[:, None])
        | (last_row - first[None, :] < windows[:, None])
    )
    order = jnp.argsort(jnp.logical_not(needed), axis=1, stable=True).astype(jnp.int32)
    count = jnp.sum(needed, axis=1).astype(jnp.int32)
    last = jnp.take_along_axis(order, jnp.maximum(count - 1, 0)[:, None], axis=1)
    steps = jnp.arange(blocks, dtype=jnp.int32)[None, :]
    table = jnp.where(steps < count[:, None], order, last)
    full = jnp.take_along_axis(whole, table, axis=1).astype(jnp.int32)
    meta = jnp.stack(
        [
            count,
            roles,
            sinks,
            windows,
            row_bases,
            jnp.broadcast_to(key_offset, count.shape),
        ],
        axis=1,
    ).astype(jnp.int32)
    meta = jnp.pad(meta, ((0, 0), (0, 2)))
    return jnp.concatenate([table, full], axis=1), meta


def attend(stacked, both, table, meta):
    local_heads, stack_rows, _ = stacked.shape
    blocks = table.shape[1] // 2
    return pl.pallas_call(
        attention_kernel,
        out_shape=(
            jax.ShapeDtypeStruct(stacked.shape, jnp.float32),
            jax.ShapeDtypeStruct((local_heads, stack_rows, 1), jnp.float32),
            jax.ShapeDtypeStruct((local_heads, stack_rows, 1), jnp.float32),
            jax.ShapeDtypeStruct(stacked.shape, jnp.bfloat16),
            jax.ShapeDtypeStruct((local_heads, 2, stack_rows), jnp.float32),
        ),
        grid_spec=pltpu.PrefetchScalarGridSpec(
            num_scalar_prefetch=2,
            grid=(local_heads, blocks),
            in_specs=[
                pl.BlockSpec((1, stack_rows, HD), lambda g, s, t, m: (g, 0, 0)),
                pl.BlockSpec((KEY_BLOCK, HD), lambda g, s, t, m: (t[g, s], g)),
                pl.BlockSpec((KEY_BLOCK, HD), lambda g, s, t, m: (t[g, s], local_heads + g)),
            ],
            out_specs=(
                pl.BlockSpec((1, stack_rows, HD), lambda g, s, t, m: (g, 0, 0)),
                pl.BlockSpec((1, stack_rows, 1), lambda g, s, t, m: (g, 0, 0)),
                pl.BlockSpec((1, stack_rows, 1), lambda g, s, t, m: (g, 0, 0)),
                pl.BlockSpec((1, stack_rows, HD), lambda g, s, t, m: (g, 0, 0)),
                pl.BlockSpec((1, 2, stack_rows), lambda g, s, t, m: (g, 0, 0)),
            ),
        ),
        compiler_params=pltpu.CompilerParams(
            dimension_semantics=("arbitrary", "arbitrary")
        ),
    )(table, meta, stacked, both, both)


def stack_heads(queries, local_heads):
    rows = queries.shape[0]
    return (
        queries.reshape(rows, local_heads, GROUP, HD)
        .transpose(1, 2, 0, 3)
        .reshape(local_heads, GROUP * rows, HD)
    )


def merge(own, other, row_count):
    acc_a, peak_a, total_a = own
    acc_b, peak_b, total_b = other
    peak = jnp.maximum(peak_a, peak_b)
    scale_a = jnp.exp(peak_a - peak)
    scale_b = jnp.exp(peak_b - peak)
    acc = acc_a * scale_a + acc_b * scale_b
    total = total_a * scale_a + total_b * scale_b
    local_heads = acc.shape[0]
    attended = (acc / total).astype(jnp.bfloat16)
    return (
        attended.reshape(local_heads, GROUP, row_count, HD)
        .transpose(2, 0, 1, 3)
        .reshape(row_count, local_heads * GROUP * HD)
    )


def place(result, piece, origin):
    return lax.dynamic_update_slice(result, piece, (origin * piece.shape[0], 0))


def gather_ring(block, axis):
    size = lax.axis_size(axis)
    here = lax.axis_index(axis)
    result = jnp.zeros((size * block.shape[0], block.shape[1]), block.dtype)
    result = place(result, block, here)
    for shift in range(1, size):
        piece = lax.ppermute(block, axis, [(i, (i + shift) % size) for i in range(size)])
        result = place(result, piece, (here - shift) % size)
    return result


def gather_both_ways(block, axis):
    size = lax.axis_size(axis)
    here = lax.axis_index(axis)
    right = [(i, (i + 1) % size) for i in range(size)]
    left = [(i, (i - 1) % size) for i in range(size)]
    result = jnp.zeros((size * block.shape[0], block.shape[1]), block.dtype)
    result = place(result, block, here)
    forward = block
    backward = block
    for step in range(1, size // 2 + 1):
        forward = lax.ppermute(forward, axis, right)
        result = place(result, forward, (here - step) % size)
        if step < size - size // 2:
            backward = lax.ppermute(backward, axis, left)
            result = place(result, backward, (here + step) % size)
    return result


def scatter_sum(partial):
    rows, width = partial.shape
    quarter = rows // 4
    parts = partial.reshape(2, 2, quarter, width)
    core = lax.axis_index("core")
    keep = jnp.take(parts, core, axis=1)
    give = jnp.take(parts, 1 - core, axis=1)
    got = lax.ppermute(give.astype(jnp.bfloat16), "core", [(0, 1), (1, 0)])
    summed = keep + got.astype(jnp.float32)
    xl = lax.axis_index("xl")
    keep = jnp.take(summed, xl, axis=0)
    give = jnp.take(summed, 1 - xl, axis=0)
    got = lax.ppermute(give.astype(jnp.bfloat16), "xl", [(0, 1), (1, 0)])
    return (keep + got.astype(jnp.float32)).astype(jnp.bfloat16)


def per_device(queries, key_states, value_states, out_weight, head_role, sink_len, window_len):
    row_count = queries.shape[0]
    local_heads = key_states.shape[1] // HD
    half_size = lax.axis_size("z") * lax.axis_size("y")
    half = lax.axis_index("xh")
    place = lax.axis_index("z") * lax.axis_size("y") + lax.axis_index("y")
    ctx = half * half_size + place
    partner = (1 - half) * half_size + place
    head_index = lax.axis_index("xl") * lax.axis_size("core") + lax.axis_index("core")
    first_head = head_index * local_heads
    roles_here = lax.dynamic_slice_in_dim(head_role, first_head, local_heads)
    sinks_here = lax.dynamic_slice_in_dim(sink_len, first_head, local_heads)
    windows_here = lax.dynamic_slice_in_dim(window_len, first_head, local_heads)
    partner_queries = lax.ppermute(stack_heads(queries, local_heads), "xh", [(1, 0)])
    both = jnp.concatenate([key_states, value_states], axis=1)
    both = gather_ring(both, "y")
    both = gather_both_ways(both, "z")
    key_offset = half * both.shape[0]
    row_bases = jnp.concatenate(
        [jnp.broadcast_to(partner * row_count, (local_heads,)),
         jnp.broadcast_to(ctx * row_count, (local_heads,))]
    ).astype(jnp.int32)
    tables, metas = block_table(
        row_bases, row_count, key_offset, both.shape[0],
        jnp.concatenate([roles_here, roles_here]),
        jnp.concatenate([sinks_here, sinks_here]),
        jnp.concatenate([windows_here, windows_here]),
    )
    table, meta = tables[:local_heads], metas[:local_heads]
    _, _, _, acc_p, stats_p = attend(partner_queries, both, table, meta)
    acc_p = lax.ppermute(acc_p, "xh", [(0, 1)])
    stats_p = lax.ppermute(stats_p, "xh", [(0, 1)])
    table, meta = tables[local_heads:], metas[local_heads:]
    own = attend(stack_heads(queries, local_heads), both, table, meta)[:3]
    received = half == 1
    peak_b = jnp.where(received, stats_p[:, 0], NEGATIVE)[:, :, None]
    total_b = jnp.where(received, stats_p[:, 1], 0.0)[:, :, None]
    acc_b = jnp.where(received, acc_p.astype(jnp.float32), 0.0)
    attended = merge(own, (acc_b, peak_b, total_b), row_count)
    partial = jnp.dot(attended, out_weight, preferred_element_type=jnp.float32)
    return scatter_sum(partial)


def solution(mesh):
    ctx_size = mesh.shape["ctx"]
    y_size = 4
    devices = mesh.devices.reshape(2, ctx_size // (2 * y_size), y_size, 2, mesh.shape["head"] // 2)
    split = jax.sharding.Mesh(devices, ("xh", "z", "y", "xl", "core"))
    tokens = ("xh", "z", "y")
    heads = ("xl", "core")
    in_specs = (
        P(tokens, heads),
        P(tokens, heads),
        P(tokens, heads),
        P(heads, None),
        P(),
        P(),
        P(),
    )
    out_specs = P(("xh", "z", "y", "xl", "core"), None)
    return jax.shard_map(
        per_device, mesh=split, in_specs=in_specs, out_specs=out_specs, check_vma=False
    )
```

```python
import functools

import jax
import jax.numpy as jnp
from jax import lax
from jax.experimental import pallas as pl
from jax.experimental.pallas import tpu as pltpu
from jax.sharding import PartitionSpec as P

HD = 128
GROUP = 4
KEY_BLOCK = 2048

NEGATIVE = -1e30


def attention_kernel(table_ref, meta_ref, q_ref, k_ref, v_ref, acc_ref, peak_ref, total_ref,
                     send_ref, stats_ref):
    g = pl.program_id(0)
    step = pl.program_id(1)
    blocks = pl.num_programs(1)
    count = meta_ref[g, 0]
    is_retrieval = meta_ref[g, 1]
    sink = meta_ref[g, 2]
    window = meta_ref[g, 3]
    row_base = meta_ref[g, 4]
    key_offset = meta_ref[g, 5]
    rows = q_ref.shape[1] // GROUP
    width = k_ref.shape[0]

    @pl.when(step == 0)
    def _():
        peak_ref[...] = jnp.full_like(peak_ref, NEGATIVE)
        total_ref[...] = jnp.zeros_like(total_ref)
        acc_ref[...] = jnp.zeros_like(acc_ref)

    def update(allowed):
        scores = lax.dot_general(
            q_ref[0], k_ref[...], (((1,), (1,)), ((), ())), preferred_element_type=jnp.float32
        ) * HD ** (-0.5)
        old_peak = peak_ref[0]
        if allowed is None:
            block_peak = jnp.max(scores, axis=-1, keepdims=True)
            new_peak = jnp.maximum(old_peak, block_peak)
            weights = jnp.exp(scores - new_peak)
        else:
            scores = scores.reshape(GROUP, rows, width)
            block_peak = jnp.max(
                jnp.where(allowed, scores, NEGATIVE), axis=-1, keepdims=True
            ).reshape(GROUP * rows, 1)
            new_peak = jnp.maximum(old_peak, block_peak)
            weights = jnp.where(
                allowed, jnp.exp(scores - new_peak.reshape(GROUP, rows, 1)), 0.0
            ).reshape(GROUP * rows, width)
        rescale = jnp.exp(old_peak - new_peak)
        total_ref[0] = rescale * total_ref[0] + jnp.sum(weights, axis=-1, keepdims=True)
        acc_ref[0] = rescale * acc_ref[0] + jnp.dot(
            weights.astype(jnp.bfloat16), v_ref[...], preferred_element_type=jnp.float32
        )
        peak_ref[0] = new_peak

    full = table_ref[g, blocks + step]

    @pl.when((step < count) & (full == 1))
    def _():
        update(None)

    @pl.when((step < count) & (full == 0))
    def _():
        block = table_ref[g, step]
        key_base = key_offset + block * width
        row = lax.broadcasted_iota(jnp.int32, (rows, width), 0)
        col = lax.broadcasted_iota(jnp.int32, (rows, width), 1)
        later_minus_earlier = (row - col) + (row_base - key_base)
        reach = jnp.where(is_retrieval == 1, jnp.int32(2**30), window)
        allowed = (later_minus_earlier >= 0) & (
            (later_minus_earlier < reach) | (col + key_base < sink)
        )
        update(allowed[None])

    @pl.when(step == blocks - 1)
    def _():
        send_ref[...] = acc_ref[...].astype(send_ref.dtype)
        stats_ref[0, 0:1, :] = jnp.transpose(peak_ref[0])
        stats_ref[0, 1:2, :] = jnp.transpose(total_ref[0])


def block_table(row_bases, row_count, key_offset, key_count, roles, sinks, windows):
    blocks = key_count // KEY_BLOCK
    first = key_offset + jnp.arange(blocks, dtype=jnp.int32) * KEY_BLOCK
    last_key = first + KEY_BLOCK - 1
    row_base = row_bases[:, None]
    last_row = row_base + row_count - 1
    causal = first[None, :] <= last_row
    reach = last_key[None, :] >= row_base - windows[:, None] + 1
    sunk = first[None, :] < sinks[:, None]
    retrieval = roles[:, None] == 1
    needed = causal & (retrieval | reach | sunk)
    whole = (last_key[None, :] <= row_base) & (
        retrieval
        | (last_key[None, :] < sinks[:, None])
        | (last_row - first[None, :] < windows[:, None])
    )
    order = jnp.argsort(jnp.logical_not(needed), axis=1, stable=True).astype(jnp.int32)
    count = jnp.sum(needed, axis=1).astype(jnp.int32)
    last = jnp.take_along_axis(order, jnp.maximum(count - 1, 0)[:, None], axis=1)
    steps = jnp.arange(blocks, dtype=jnp.int32)[None, :]
    table = jnp.where(steps < count[:, None], order, last)
    full = jnp.take_along_axis(whole, table, axis=1).astype(jnp.int32)
    meta = jnp.stack(
        [
            count,
            roles,
            sinks,
            windows,
            row_bases,
            jnp.broadcast_to(key_offset, count.shape),
        ],
        axis=1,
    ).astype(jnp.int32)
    meta = jnp.pad(meta, ((0, 0), (0, 2)))
    return jnp.concatenate([table, full], axis=1), meta


def attend(stacked, both, table, meta):
    local_heads, stack_rows, _ = stacked.shape
    blocks = table.shape[1] // 2
    return pl.pallas_call(
        attention_kernel,
        out_shape=(
            jax.ShapeDtypeStruct(stacked.shape, jnp.float32),
            jax.ShapeDtypeStruct((local_heads, stack_rows, 1), jnp.float32),
            jax.ShapeDtypeStruct((local_heads, stack_rows, 1), jnp.float32),
            jax.ShapeDtypeStruct(stacked.shape, jnp.bfloat16),
            jax.ShapeDtypeStruct((local_heads, 2, stack_rows), jnp.float32),
        ),
        grid_spec=pltpu.PrefetchScalarGridSpec(
            num_scalar_prefetch=2,
            grid=(local_heads, blocks),
            in_specs=[
                pl.BlockSpec((1, stack_rows, HD), lambda g, s, t, m: (g, 0, 0)),
                pl.BlockSpec((KEY_BLOCK, HD), lambda g, s, t, m: (t[g, s], g)),
                pl.BlockSpec((KEY_BLOCK, HD), lambda g, s, t, m: (t[g, s], local_heads + g)),
            ],
            out_specs=(
                pl.BlockSpec((1, stack_rows, HD), lambda g, s, t, m: (g, 0, 0)),
                pl.BlockSpec((1, stack_rows, 1), lambda g, s, t, m: (g, 0, 0)),
                pl.BlockSpec((1, stack_rows, 1), lambda g, s, t, m: (g, 0, 0)),
                pl.BlockSpec((1, stack_rows, HD), lambda g, s, t, m: (g, 0, 0)),
                pl.BlockSpec((1, 2, stack_rows), lambda g, s, t, m: (g, 0, 0)),
            ),
        ),
        compiler_params=pltpu.CompilerParams(
            dimension_semantics=("arbitrary", "arbitrary")
        ),
    )(table, meta, stacked, both, both)


def stack_heads(queries, local_heads):
    rows = queries.shape[0]
    return (
        queries.reshape(rows, local_heads, GROUP, HD)
        .transpose(1, 2, 0, 3)
        .reshape(local_heads, GROUP * rows, HD)
    )


def merge(own, other, row_count):
    acc_a, peak_a, total_a = own
    acc_b, peak_b, total_b = other
    peak = jnp.maximum(peak_a, peak_b)
    scale_a = jnp.exp(peak_a - peak)
    scale_b = jnp.exp(peak_b - peak)
    acc = acc_a * scale_a + acc_b * scale_b
    total = total_a * scale_a + total_b * scale_b
    local_heads = acc.shape[0]
    attended = (acc / total).astype(jnp.bfloat16)
    return (
        attended.reshape(local_heads, GROUP, row_count, HD)
        .transpose(2, 0, 1, 3)
        .reshape(row_count, local_heads * GROUP * HD)
    )


def place(result, piece, origin):
    return lax.dynamic_update_slice(result, piece, (origin * piece.shape[0], 0))


def gather_ring(block, axis):
    size = lax.axis_size(axis)
    here = lax.axis_index(axis)
    result = jnp.zeros((size * block.shape[0], block.shape[1]), block.dtype)
    result = place(result, block, here)
    for shift in range(1, size):
        piece = lax.ppermute(block, axis, [(i, (i + shift) % size) for i in range(size)])
        result = place(result, piece, (here - shift) % size)
    return result


def gather_both_ways(block, axis, result):
    size = lax.axis_size(axis)
    here = lax.axis_index(axis)
    right = [(i, (i + 1) % size) for i in range(size)]
    left = [(i, (i - 1) % size) for i in range(size)]
    result = place(result, block, here)
    forward = block
    backward = block
    for step in range(1, size // 2 + 1):
        forward = lax.ppermute(forward, axis, right)
        result = place(result, forward, (here - step) % size)
        if step < size - size // 2:
            backward = lax.ppermute(backward, axis, left)
            result = place(result, backward, (here + step) % size)
    return result


def scatter_sum(partial):
    rows, width = partial.shape
    quarter = rows // 4
    parts = partial.reshape(2, 2, quarter, width)
    core = lax.axis_index("core")
    keep = jnp.take(parts, core, axis=1)
    give = jnp.take(parts, 1 - core, axis=1)
    got = lax.ppermute(give.astype(jnp.bfloat16), "core", [(0, 1), (1, 0)])
    summed = keep + got.astype(jnp.float32)
    xl = lax.axis_index("xl")
    keep = jnp.take(summed, xl, axis=0)
    give = jnp.take(summed, 1 - xl, axis=0)
    got = lax.ppermute(give.astype(jnp.bfloat16), "xl", [(0, 1), (1, 0)])
    return (keep + got.astype(jnp.float32)).astype(jnp.bfloat16)


def per_device(queries, key_states, value_states, out_weight, head_role, sink_len, window_len):
    row_count = queries.shape[0]
    local_heads = key_states.shape[1] // HD
    half_size = lax.axis_size("z") * lax.axis_size("y")
    half = lax.axis_index("xh")
    place = lax.axis_index("z") * lax.axis_size("y") + lax.axis_index("y")
    ctx = half * half_size + place
    partner = (1 - half) * half_size + place
    head_index = lax.axis_index("xl") * lax.axis_size("core") + lax.axis_index("core")
    first_head = head_index * local_heads
    roles_here = lax.dynamic_slice_in_dim(head_role, first_head, local_heads)
    sinks_here = lax.dynamic_slice_in_dim(sink_len, first_head, local_heads)
    windows_here = lax.dynamic_slice_in_dim(window_len, first_head, local_heads)
    blank = jnp.broadcast_to(
        key_states[0, 0] * 0,
        (lax.axis_size("z") * lax.axis_size("y") * key_states.shape[0], 2 * key_states.shape[1]),
    )
    blank, own_queries = lax.optimization_barrier((blank, stack_heads(queries, local_heads)))
    partner_queries = lax.ppermute(own_queries, "xh", [(1, 0)])
    both = jnp.concatenate([key_states, value_states], axis=1)
    both = gather_ring(both, "y")
    both = gather_both_ways(both, "z", blank)
    key_offset = half * both.shape[0]
    row_bases = jnp.concatenate(
        [jnp.broadcast_to(partner * row_count, (local_heads,)),
         jnp.broadcast_to(ctx * row_count, (local_heads,))]
    ).astype(jnp.int32)
    tables, metas = block_table(
        row_bases, row_count, key_offset, both.shape[0],
        jnp.concatenate([roles_here, roles_here]),
        jnp.concatenate([sinks_here, sinks_here]),
        jnp.concatenate([windows_here, windows_here]),
    )
    table, meta = tables[:local_heads], metas[:local_heads]
    _, _, _, acc_p, stats_p = attend(partner_queries, both, table, meta)
    acc_p = lax.ppermute(acc_p, "xh", [(0, 1)])
    stats_p = lax.ppermute(stats_p, "xh", [(0, 1)])
    table, meta = tables[local_heads:], metas[local_heads:]
    own = attend(stack_heads(queries, local_heads), both, table, meta)[:3]
    received = half == 1
    peak_b = jnp.where(received, stats_p[:, 0], NEGATIVE)[:, :, None]
    total_b = jnp.where(received, stats_p[:, 1], 0.0)[:, :, None]
    acc_b = jnp.where(received, acc_p.astype(jnp.float32), 0.0)
    attended = merge(own, (acc_b, peak_b, total_b), row_count)
    partial = jnp.dot(attended, out_weight, preferred_element_type=jnp.float32)
    return scatter_sum(partial)


def solution(mesh):
    ctx_size = mesh.shape["ctx"]
    y_size = 4
    devices = mesh.devices.reshape(2, ctx_size // (2 * y_size), y_size, 2, mesh.shape["head"] // 2)
    split = jax.sharding.Mesh(devices, ("xh", "z", "y", "xl", "core"))
    tokens = ("xh", "z", "y")
    heads = ("xl", "core")
    in_specs = (
        P(tokens, heads),
        P(tokens, heads),
        P(tokens, heads),
        P(heads, None),
        P(),
        P(),
        P(),
    )
    out_specs = P(("xh", "z", "y", "xl", "core"), None)
    return jax.shard_map(
        per_device, mesh=split, in_specs=in_specs, out_specs=out_specs, check_vma=False
    )
```

```python
import functools

import jax
import jax.numpy as jnp
from jax import lax
from jax.experimental import pallas as pl
from jax.experimental.pallas import tpu as pltpu
from jax.sharding import PartitionSpec as P

HD = 128
GROUP = 4
KEY_BLOCK = 2048

NEGATIVE = -1e30


def attention_kernel(table_ref, meta_ref, q_ref, k_ref, v_ref, acc_ref, peak_ref, total_ref,
                     send_ref, stats_ref):
    g = pl.program_id(0)
    step = pl.program_id(1)
    blocks = pl.num_programs(1)
    count = meta_ref[g, 0]
    is_retrieval = meta_ref[g, 1]
    sink = meta_ref[g, 2]
    window = meta_ref[g, 3]
    row_base = meta_ref[g, 4]
    key_offset = meta_ref[g, 5]
    rows = q_ref.shape[1] // GROUP
    width = k_ref.shape[0]

    @pl.when(step == 0)
    def _():
        peak_ref[...] = jnp.full_like(peak_ref, NEGATIVE)
        total_ref[...] = jnp.zeros_like(total_ref)
        acc_ref[...] = jnp.zeros_like(acc_ref)

    def update(allowed):
        scores = lax.dot_general(
            q_ref[0], k_ref[...], (((1,), (1,)), ((), ())), preferred_element_type=jnp.float32
        ) * HD ** (-0.5)
        old_peak = peak_ref[0]
        if allowed is None:
            block_peak = jnp.max(scores, axis=-1, keepdims=True)
            new_peak = jnp.maximum(old_peak, block_peak)
            weights = jnp.exp(scores - new_peak)
        else:
            scores = scores.reshape(GROUP, rows, width)
            block_peak = jnp.max(
                jnp.where(allowed, scores, NEGATIVE), axis=-1, keepdims=True
            ).reshape(GROUP * rows, 1)
            new_peak = jnp.maximum(old_peak, block_peak)
            weights = jnp.where(
                allowed, jnp.exp(scores - new_peak.reshape(GROUP, rows, 1)), 0.0
            ).reshape(GROUP * rows, width)
        rescale = jnp.exp(old_peak - new_peak)
        total_ref[0] = rescale * total_ref[0] + jnp.sum(weights, axis=-1, keepdims=True)
        acc_ref[0] = rescale * acc_ref[0] + jnp.dot(
            weights.astype(jnp.bfloat16), v_ref[...], preferred_element_type=jnp.float32
        )
        peak_ref[0] = new_peak

    full = table_ref[g, blocks + step]

    @pl.when((step < count) & (full == 1))
    def _():
        update(None)

    @pl.when((step < count) & (full == 0))
    def _():
        block = table_ref[g, step]
        key_base = key_offset + block * width
        row = lax.broadcasted_iota(jnp.int32, (rows, width), 0)
        col = lax.broadcasted_iota(jnp.int32, (rows, width), 1)
        later_minus_earlier = (row - col) + (row_base - key_base)
        reach = jnp.where(is_retrieval == 1, jnp.int32(2**30), window)
        allowed = (later_minus_earlier >= 0) & (
            (later_minus_earlier < reach) | (col + key_base < sink)
        )
        update(allowed[None])

    @pl.when(step == blocks - 1)
    def _():
        send_ref[...] = acc_ref[...].astype(send_ref.dtype)
        stats_ref[0, 0:1, :] = jnp.transpose(peak_ref[0])
        stats_ref[0, 1:2, :] = jnp.transpose(total_ref[0])


def block_table(row_bases, row_count, key_offset, key_count, roles, sinks, windows):
    blocks = key_count // KEY_BLOCK
    first = key_offset + jnp.arange(blocks, dtype=jnp.int32) * KEY_BLOCK
    last_key = first + KEY_BLOCK - 1
    row_base = row_bases[:, None]
    last_row = row_base + row_count - 1
    causal = first[None, :] <= last_row
    reach = last_key[None, :] >= row_base - windows[:, None] + 1
    sunk = first[None, :] < sinks[:, None]
    retrieval = roles[:, None] == 1
    needed = causal & (retrieval | reach | sunk)
    whole = (last_key[None, :] <= row_base) & (
        retrieval
        | (last_key[None, :] < sinks[:, None])
        | (last_row - first[None, :] < windows[:, None])
    )
    order = jnp.argsort(jnp.logical_not(needed), axis=1, stable=True).astype(jnp.int32)
    count = jnp.sum(needed, axis=1).astype(jnp.int32)
    last = jnp.take_along_axis(order, jnp.maximum(count - 1, 0)[:, None], axis=1)
    steps = jnp.arange(blocks, dtype=jnp.int32)[None, :]
    table = jnp.where(steps < count[:, None], order, last)
    full = jnp.take_along_axis(whole, table, axis=1).astype(jnp.int32)
    meta = jnp.stack(
        [
            count,
            roles,
            sinks,
            windows,
            row_bases,
            jnp.broadcast_to(key_offset, count.shape),
        ],
        axis=1,
    ).astype(jnp.int32)
    meta = jnp.pad(meta, ((0, 0), (0, 2)))
    return jnp.concatenate([table, full], axis=1), meta


def attend(stacked, both, table, meta):
    local_heads, stack_rows, _ = stacked.shape
    blocks = table.shape[1] // 2
    return pl.pallas_call(
        attention_kernel,
        out_shape=(
            jax.ShapeDtypeStruct(stacked.shape, jnp.float32),
            jax.ShapeDtypeStruct((local_heads, stack_rows, 1), jnp.float32),
            jax.ShapeDtypeStruct((local_heads, stack_rows, 1), jnp.float32),
            jax.ShapeDtypeStruct(stacked.shape, jnp.bfloat16),
            jax.ShapeDtypeStruct((local_heads, 2, stack_rows), jnp.float32),
        ),
        grid_spec=pltpu.PrefetchScalarGridSpec(
            num_scalar_prefetch=2,
            grid=(local_heads, blocks),
            in_specs=[
                pl.BlockSpec((1, stack_rows, HD), lambda g, s, t, m: (g, 0, 0)),
                pl.BlockSpec((KEY_BLOCK, HD), lambda g, s, t, m: (t[g, s], g)),
                pl.BlockSpec((KEY_BLOCK, HD), lambda g, s, t, m: (t[g, s], local_heads + g)),
            ],
            out_specs=(
                pl.BlockSpec((1, stack_rows, HD), lambda g, s, t, m: (g, 0, 0)),
                pl.BlockSpec((1, stack_rows, 1), lambda g, s, t, m: (g, 0, 0)),
                pl.BlockSpec((1, stack_rows, 1), lambda g, s, t, m: (g, 0, 0)),
                pl.BlockSpec((1, stack_rows, HD), lambda g, s, t, m: (g, 0, 0)),
                pl.BlockSpec((1, 2, stack_rows), lambda g, s, t, m: (g, 0, 0)),
            ),
        ),
        compiler_params=pltpu.CompilerParams(
            dimension_semantics=("arbitrary", "arbitrary")
        ),
    )(table, meta, stacked, both, both)


def stack_heads(queries, local_heads):
    rows = queries.shape[0]
    return (
        queries.reshape(rows, local_heads, GROUP, HD)
        .transpose(1, 2, 0, 3)
        .reshape(local_heads, GROUP * rows, HD)
    )


def merge(own, other, row_count):
    acc_a, peak_a, total_a = own
    acc_b, peak_b, total_b = other
    peak = jnp.maximum(peak_a, peak_b)
    scale_a = jnp.exp(peak_a - peak)
    scale_b = jnp.exp(peak_b - peak)
    acc = acc_a * scale_a + acc_b * scale_b
    total = total_a * scale_a + total_b * scale_b
    local_heads = acc.shape[0]
    attended = (acc / total).astype(jnp.bfloat16)
    return (
        attended.reshape(local_heads, GROUP, row_count, HD)
        .transpose(2, 0, 1, 3)
        .reshape(row_count, local_heads * GROUP * HD)
    )


def place(result, piece, origin):
    return lax.dynamic_update_slice(result, piece, (origin * piece.shape[0], 0))


def gather_ring(block, axis):
    size = lax.axis_size(axis)
    here = lax.axis_index(axis)
    result = jnp.zeros((size * block.shape[0], block.shape[1]), block.dtype)
    result = place(result, block, here)
    for shift in range(1, size):
        piece = lax.ppermute(block, axis, [(i, (i + shift) % size) for i in range(size)])
        result = place(result, piece, (here - shift) % size)
    return result


def gather_both_ways(block, axis):
    size = lax.axis_size(axis)
    here = lax.axis_index(axis)
    right = [(i, (i + 1) % size) for i in range(size)]
    left = [(i, (i - 1) % size) for i in range(size)]
    result = jnp.zeros((size * block.shape[0], block.shape[1]), block.dtype)
    result = place(result, block, here)
    forward = block
    backward = block
    for step in range(1, size // 2 + 1):
        forward = lax.ppermute(forward, axis, right)
        result = place(result, forward, (here - step) % size)
        if step < size - size // 2:
            backward = lax.ppermute(backward, axis, left)
            result = place(result, backward, (here + step) % size)
    return result


def scatter_sum(partial):
    rows, width = partial.shape
    quarter = rows // 4
    parts = partial.reshape(2, 2, quarter, width)
    core = lax.axis_index("core")
    keep = jnp.take(parts, core, axis=1)
    give = jnp.take(parts, 1 - core, axis=1)
    got = lax.ppermute(give.astype(jnp.bfloat16), "core", [(0, 1), (1, 0)])
    xl = lax.axis_index("xl")
    give = jnp.take(keep, 1 - xl, axis=0) + jnp.take(got, 1 - xl, axis=0).astype(jnp.float32)
    sent = lax.ppermute(give.astype(jnp.bfloat16), "xl", [(0, 1), (1, 0)])
    keep = jnp.take(keep, xl, axis=0) + jnp.take(got, xl, axis=0).astype(jnp.float32)
    got = sent
    return (keep + got.astype(jnp.float32)).astype(jnp.bfloat16)


def per_device(queries, key_states, value_states, out_weight, head_role, sink_len, window_len):
    row_count = queries.shape[0]
    local_heads = key_states.shape[1] // HD
    half_size = lax.axis_size("z") * lax.axis_size("y")
    half = lax.axis_index("xh")
    place = lax.axis_index("z") * lax.axis_size("y") + lax.axis_index("y")
    ctx = half * half_size + place
    partner = (1 - half) * half_size + place
    head_index = lax.axis_index("xl") * lax.axis_size("core") + lax.axis_index("core")
    first_head = head_index * local_heads
    roles_here = lax.dynamic_slice_in_dim(head_role, first_head, local_heads)
    sinks_here = lax.dynamic_slice_in_dim(sink_len, first_head, local_heads)
    windows_here = lax.dynamic_slice_in_dim(window_len, first_head, local_heads)
    partner_queries = lax.ppermute(stack_heads(queries, local_heads), "xh", [(1, 0)])
    both = jnp.concatenate([key_states, value_states], axis=1)
    both = gather_ring(both, "y")
    both = gather_both_ways(both, "z")
    key_offset = half * both.shape[0]
    row_bases = jnp.concatenate(
        [jnp.broadcast_to(partner * row_count, (local_heads,)),
         jnp.broadcast_to(ctx * row_count, (local_heads,))]
    ).astype(jnp.int32)
    tables, metas = block_table(
        row_bases, row_count, key_offset, both.shape[0],
        jnp.concatenate([roles_here, roles_here]),
        jnp.concatenate([sinks_here, sinks_here]),
        jnp.concatenate([windows_here, windows_here]),
    )
    table, meta = tables[:local_heads], metas[:local_heads]
    _, _, _, acc_p, stats_p = attend(partner_queries, both, table, meta)
    acc_p = lax.ppermute(acc_p, "xh", [(0, 1)])
    stats_p = lax.ppermute(stats_p, "xh", [(0, 1)])
    table, meta = tables[local_heads:], metas[local_heads:]
    own = attend(stack_heads(queries, local_heads), both, table, meta)[:3]
    received = half == 1
    peak_b = jnp.where(received, stats_p[:, 0], NEGATIVE)[:, :, None]
    total_b = jnp.where(received, stats_p[:, 1], 0.0)[:, :, None]
    acc_b = jnp.where(received, acc_p.astype(jnp.float32), 0.0)
    attended = merge(own, (acc_b, peak_b, total_b), row_count)
    partial = jnp.dot(attended, out_weight, preferred_element_type=jnp.float32)
    return scatter_sum(partial)


def solution(mesh):
    ctx_size = mesh.shape["ctx"]
    y_size = 4
    devices = mesh.devices.reshape(2, ctx_size // (2 * y_size), y_size, 2, mesh.shape["head"] // 2)
    split = jax.sharding.Mesh(devices, ("xh", "z", "y", "xl", "core"))
    tokens = ("xh", "z", "y")
    heads = ("xl", "core")
    in_specs = (
        P(tokens, heads),
        P(tokens, heads),
        P(tokens, heads),
        P(heads, None),
        P(),
        P(),
        P(),
    )
    out_specs = P(("xh", "z", "y", "xl", "core"), None)
    return jax.shard_map(
        per_device, mesh=split, in_specs=in_specs, out_specs=out_specs, check_vma=False
    )
```
